32 devices in a mesh: shard: 4 (over y, x), ctx: 2 (over core), tp: 4 (over z).
Axes of the slice: x: 2, y: 2, z: 4, core: 2. Of those that a mesh axis runs over, the one named last changes fastest.
Arguments:
- activations: bfloat16 [4, 2048, 1024], P('shard', 'ctx'), may hold values from -6 to 6
- timestep: int32 [4], P('shard'), may hold values from 0 to 999
- positions: int32 [4, 2048], P('shard', 'ctx'), may hold values from 0 to 16383
- qkv_weight: bfloat16 [3, 1024, 1024], P(None, 'shard', 'tp'), may hold values from -0.1875 to 0.1875
- out_weight: bfloat16 [1024, 1024], P('tp', 'shard'), may hold values from -4 to 4
- up_weight: bfloat16 [1024, 4096], P('shard', 'tp'), may hold values from -0.1875 to 0.1875
- down_weight: bfloat16 [4096, 1024], P('tp', 'shard'), may hold values from -0.125 to 0.125
- time_weight: bfloat16 [256, 4, 1024], P(None, None, 'shard'), may hold values from -0.1875 to 0.1875
- norm_gains: bfloat16 [2, 1024], P(None, 'shard'), may hold values from 0.5 to 1.5
- cotangent: bfloat16 [4, 2048, 1024], P('shard', 'ctx'), may hold values from -6 to 6
Outputs:
- output: bfloat16 [4, 2048, 1024], P('shard', 'ctx')
- input_grad: bfloat16 [4, 2048, 1024], P('shard', 'ctx')
- grad_qkv: float32 [3, 1024, 1024], P(None, 'shard', 'tp')
- grad_out: float32 [1024, 1024], P('tp', 'shard')
- grad_up: float32 [1024, 4096], P('shard', 'tp')
- grad_down: float32 [4096, 1024], P('tp', 'shard')
- grad_time: float32 [256, 4, 1024], P(None, None, 'shard')
- grad_gains: float32 [2, 1024], P(None, 'shard')
The draws below stay inside these ranges and needn't reach their ends.
All inputs are finite; a program needn't handle non-finite values.
Results may differ from the reference program's by a relative error of at most 0.015.
Values may be sent and summed in bfloat16 or wider, within the bound.
No kernel may reach another device: no remote copies, remote signals or barrier semaphores. Data moves between devices by JAX's collectives and lax.ppermute only.
A program may use at most 320 MiB of HBM per device.

```python
import math
import jax
import jax.numpy as jnp
from jax import lax

D = 1024
HEADS = 16
HEAD_DIM = 64
FF = 4096
TEMB = 256
MAXLEN = 4096
LENGTH = 2048
SEQS = 4


def with_ends(values, key, least, top_value):
    dims = values.shape
    spot = [jax.random.randint(jax.random.fold_in(key, axis), (), 0, dims[axis]) for axis in range(len(dims))]
    values = values.at[tuple(spot)].set(least)
    longest = dims.index(max(dims))
    spot[longest] = (spot[longest] + 1) % dims[longest]
    return values.at[tuple(spot)].set(top_value)


def block_scale(stream_key, shape, cuts, least, largest):
    gain = 1.0
    for axis_at, blocks in cuts:
        heights = jax.random.uniform(jax.random.fold_in(jax.random.fold_in(stream_key, 6), axis_at), (blocks,), jnp.float32, least / len(cuts), largest / len(cuts))
        gain = gain * jnp.repeat(jnp.exp(heights), shape[axis_at] // blocks).reshape((-1,) + (1,) * (len(shape) - 1 - axis_at))
    return gain


def scatter_about(key, dims, width, most, pieces=(), kind=jnp.bfloat16):
    gain = block_scale(key, dims, pieces, -0.22, 0.18) if pieces else 1.0
    array = jax.random.normal(key, dims, jnp.float32) * width * gain
    return jnp.minimum(jnp.maximum(array, -most), most).astype(kind)


def setup_inputs(seed: int = 0) -> dict:
    splits = jax.random.split(jax.random.key(seed), 11)
    activations = scatter_about(splits[0], (SEQS, LENGTH, D), 1.0, 6.0, ((0, 4), (1, 2)))
    timestep = with_ends(jax.random.randint(splits[1], (SEQS,), 0, 1000), jax.random.fold_in(splits[1], 1), 0, 999).astype(jnp.int32)
    positions = with_ends(jax.random.randint(splits[2], (SEQS, LENGTH), 0, 4 * MAXLEN), jax.random.fold_in(splits[2], 1), 0, (4 * MAXLEN) - 1).astype(jnp.int32)
    qkv_weight = scatter_about(splits[3], (3, D, D), D ** -0.5, 0.1875, ((1, 4), (2, 4)))
    out_weight = scatter_about(splits[4], (D, D), (max(1, D * 4 // LENGTH)) ** -0.5, 4.0, ((0, 4), (1, 4)))
    up_weight = scatter_about(splits[5], (D, FF), D ** -0.5, 0.1875, ((0, 4), (1, 4)))
    down_weight = scatter_about(splits[6], (FF, D), (FF // 2) ** -0.5, 0.125, ((0, 4), (1, 4)))
    time_weight = scatter_about(splits[7], (TEMB, 4, D), (4 * TEMB) ** -0.5, 0.1875, ((2, 4),))
    norm_gains = jnp.clip(1.0 + 0.1 * jax.random.normal(splits[8], (2, D), jnp.float32), 0.5, 1.5).astype(jnp.bfloat16)
    cotangent = scatter_about(splits[9], (SEQS, LENGTH, D), 1.0, 6.0, ((0, 4), (1, 2)))
    return dict(activations=activations, timestep=timestep, positions=positions, qkv_weight=qkv_weight, out_weight=out_weight, up_weight=up_weight, down_weight=down_weight, time_weight=time_weight, norm_gains=norm_gains, cotangent=cotangent)


@jax.custom_vjp
def low(v):
    return lax.optimization_barrier(v.astype(jnp.bfloat16)).astype(jnp.float32)

@jax.custom_vjp
def low_back(v):
    return v

def low_keep(v):
    return (low(v), None)

def low_pass(kept, grad):
    return (grad,)

def back_keep(v):
    return (v, None)

def back_low(kept, grad):
    return (low(grad),)
low.defvjp(low_keep, low_pass)
low_back.defvjp(back_keep, back_low)
highest = lax.Precision.HIGHEST
norm_epsilon = 1e-05

def embed_time(timestep):
    half_width = TEMB // 2
    frequency = jnp.exp(-math.log(10000.0) * jnp.arange(half_width, dtype=jnp.float32) / half_width)
    angles = timestep.astype(jnp.float32)[:, None] * frequency[None, :]
    return jnp.concatenate([jnp.sin(angles), jnp.cos(angles)], axis=-1)

def rotary_tables(positions):
    half_width = HEAD_DIM // 2
    frequency = jnp.exp(-math.log(10000.0) * jnp.arange(half_width, dtype=jnp.float32) / half_width)
    angles = positions.astype(jnp.float32)[..., None] * frequency
    return (jnp.cos(angles), jnp.sin(angles))

def rotate(heads_in, cosines, sines):
    half_width = HEAD_DIM // 2
    first = heads_in[..., :half_width]
    second = heads_in[..., half_width:]
    cos_wide = cosines[..., None, :]
    sin_wide = sines[..., None, :]
    return jnp.concatenate([first * cos_wide - second * sin_wide, second * cos_wide + first * sin_wide], axis=-1)

def scaled_norm(values, gain_vec, scaling, offset):
    centered = values - lax.optimization_barrier(jnp.mean(values, axis=-1, keepdims=True))
    variance = lax.optimization_barrier(jnp.mean(centered * centered, axis=-1, keepdims=True))
    return centered * lax.rsqrt(variance + norm_epsilon) * gain_vec * (1.0 + scaling) + offset

def head_attention(triple):
    queries, keys, values = triple
    scores = low_back(jnp.dot(queries, keys.T, precision=highest) * HEAD_DIM ** (-0.5))
    weights = jax.nn.softmax(scores, axis=-1)
    return jnp.dot(low(weights), values, precision=highest)

def layer(tokens_in, w_qkv, w_out, w_up, w_down, w_time, gains_all, embedding, cosines, sines):
    length_here = tokens_in.shape[0]
    modulation = jnp.dot(embedding, w_time.reshape(TEMB, 4 * D), precision=highest).reshape(4, D)
    normed = low(scaled_norm(tokens_in, gains_all[0], modulation[0], modulation[1]))
    projected = low_back(jnp.einsum('td,cde->cte', normed, w_qkv, precision=highest))
    queries = low(rotate(projected[0].reshape(length_here, HEADS, HEAD_DIM), cosines, sines))
    keys = low(rotate(projected[1].reshape(length_here, HEADS, HEAD_DIM), cosines, sines))
    values = low(projected[2].reshape(length_here, HEADS, HEAD_DIM))
    by_head = tuple((jnp.transpose(member, (1, 0, 2)) for member in (queries, keys, values)))
    attended = lax.map(jax.checkpoint(head_attention), by_head)
    attended = low(low_back(jnp.transpose(attended, (1, 0, 2)).reshape(length_here, D)))
    branch = low_back(jnp.dot(attended, w_out, precision=highest))
    middle = tokens_in + branch
    normed_two = low(scaled_norm(middle, gains_all[1], modulation[2], modulation[3]))
    hidden = low_back(jnp.dot(normed_two, w_up, precision=highest))
    activated = low(jax.nn.gelu(hidden, approximate=False))
    return middle + jnp.dot(activated, w_down, precision=highest)

def reference(activations, timestep, positions, qkv_weight, out_weight, up_weight, down_weight, time_weight, norm_gains, cotangent):
    weights = (qkv_weight.astype(jnp.float32), out_weight.astype(jnp.float32), up_weight.astype(jnp.float32), down_weight.astype(jnp.float32), time_weight.astype(jnp.float32), norm_gains.astype(jnp.float32))
    embedding = embed_time(timestep)
    cosines, sines = rotary_tables(positions)

    def one_sequence(totals, inputs_seq):
        tokens_in, cos_seq, sin_seq, embed_seq, cot_seq = inputs_seq

        def forward(tokens_f, *weight_list):
            return layer(tokens_f, *weight_list, embed_seq, cos_seq, sin_seq)
        result, pullback = jax.vjp(forward, tokens_in.astype(jnp.float32), *weights)
        gradients = pullback(cot_seq.astype(jnp.float32))
        totals = tuple((total + grad_one for total, grad_one in zip(totals, gradients[1:])))
        return (totals, (result.astype(jnp.bfloat16), gradients[0].astype(jnp.bfloat16)))
    initial = tuple((jnp.zeros(weight_one.shape, jnp.float32) for weight_one in weights))
    totals, (outputs, input_grads) = lax.scan(one_sequence, initial, (activations, cosines, sines, embedding, cotangent))
    return (outputs, input_grads, totals[0], totals[1], totals[2], totals[3], totals[4], totals[5])
```

```python
from functools import partial
import math

import jax
import jax.numpy as jnp
from jax import lax
from jax.experimental import pallas as pl
from jax.experimental.pallas import tpu as pltpu
from jax.sharding import PartitionSpec as P

HEAD_DIM = 64
TEMB = 256


highest = lax.Precision.HIGHEST
norm_epsilon = 1e-05


def embed_time(timestep):
    half_width = TEMB // 2
    frequency = jnp.exp(-math.log(10000.0) * jnp.arange(half_width, dtype=jnp.float32) / half_width)
    angles = timestep.astype(jnp.float32)[:, None] * frequency[None, :]
    return jnp.concatenate([jnp.sin(angles), jnp.cos(angles)], axis=-1)


def rotary_tables(positions):
    half_width = HEAD_DIM // 2
    frequency = jnp.exp(-math.log(10000.0) * jnp.arange(half_width, dtype=jnp.float32) / half_width)
    angles = positions.astype(jnp.float32)[..., None] * frequency
    return (jnp.cos(angles), jnp.sin(angles))


def rotate(heads_in, cosines, sines):
    half_width = HEAD_DIM // 2
    first = heads_in[..., :half_width]
    second = heads_in[..., half_width:]
    cos_wide = cosines[..., None, :]
    sin_wide = sines[..., None, :]
    return jnp.concatenate(
        [first * cos_wide - second * sin_wide, second * cos_wide + first * sin_wide], axis=-1
    )


def unrotate(heads_in, cosines, sines):
    half_width = HEAD_DIM // 2
    first = heads_in[..., :half_width]
    second = heads_in[..., half_width:]
    cos_wide = cosines[..., None, :]
    sin_wide = sines[..., None, :]
    return jnp.concatenate(
        [first * cos_wide + second * sin_wide, second * cos_wide - first * sin_wide], axis=-1
    )


def scaled_norm(values, gain_vec, scaling, offset):
    centered = values - jnp.mean(values, axis=-1, keepdims=True)
    variance = jnp.mean(centered * centered, axis=-1, keepdims=True)
    inverse_std = lax.rsqrt(variance + norm_epsilon)
    normed = centered * inverse_std
    return (
        normed * gain_vec * (1.0 + scaling[:, None, :]) + offset[:, None, :],
        normed,
        inverse_std,
    )


def norm_back(grad_in, normed, inverse_std, gain_vec, scaling):
    factor = gain_vec * (1.0 + scaling[:, None, :])
    grad_normed = grad_in * factor
    grad_values = inverse_std * (
        grad_normed
        - jnp.mean(grad_normed, axis=-1, keepdims=True)
        - normed * jnp.mean(grad_normed * normed, axis=-1, keepdims=True)
    )
    grad_gain = jnp.sum(grad_in * normed * (1.0 + scaling[:, None, :]), axis=(0, 1))
    grad_scaling = jnp.sum(grad_in * normed * gain_vec, axis=1)
    grad_offset = jnp.sum(grad_in, axis=1)
    return (grad_values, grad_gain, grad_scaling, grad_offset)


def group_heads(field, per_group):
    seq_count, rows_count, _ = field.shape
    split = field.reshape(seq_count, rows_count, -1, HEAD_DIM).transpose(0, 2, 1, 3)
    return split.reshape(-1, per_group, rows_count, HEAD_DIM)


def ungroup_heads(field, seq_count):
    rows_count = field.shape[2]
    joined = field.reshape(seq_count, -1, rows_count, HEAD_DIM).transpose(0, 2, 1, 3)
    return joined.reshape(seq_count, rows_count, -1)


def attend_block(triple, scaling):
    queries, keys, values = triple
    scores = jnp.einsum("gqd,gkd->gqk", queries, keys, preferred_element_type=jnp.float32) * scaling
    top_score = jnp.max(scores, axis=-1, keepdims=True)
    raised = jnp.exp(scores - top_score)
    total = jnp.sum(raised, axis=-1, keepdims=True)
    weights = (raised / total).astype(jnp.bfloat16)
    attended = jnp.einsum("gqk,gkd->gqd", weights, values, preferred_element_type=jnp.float32)
    return (attended, (top_score + jnp.log(total))[..., 0])


def attend_back(bundle, scaling):
    queries, keys, values, grad_out, log_total = bundle
    scores = jnp.einsum("gqd,gkd->gqk", queries, keys, preferred_element_type=jnp.float32) * scaling
    weights = jnp.exp(scores - log_total[..., None])
    grad_values = jnp.einsum(
        "gqk,gqd->gkd", weights.astype(jnp.bfloat16), grad_out, preferred_element_type=jnp.float32
    )
    grad_weights = jnp.einsum("gqd,gkd->gqk", grad_out, values, preferred_element_type=jnp.float32)
    row_term = jnp.sum(weights * grad_weights, axis=-1, keepdims=True)
    grad_scores = (weights * (grad_weights - row_term)).astype(jnp.bfloat16)
    grad_queries = (
        jnp.einsum("gqk,gkd->gqd", grad_scores, keys, preferred_element_type=jnp.float32) * scaling
    )
    grad_keys = (
        jnp.einsum("gqk,gqd->gkd", grad_scores, queries, preferred_element_type=jnp.float32)
        * scaling
    )
    return (grad_queries, grad_keys, grad_values)


def gelu_slope(hidden):
    return (
        0.5 * (1.0 + lax.erf(hidden * 0.7071067811865476))
        + hidden * jnp.exp(-0.5 * hidden * hidden) * 0.3989422804014327
    )


def body(
    activations,
    timestep,
    positions,
    qkv_weight,
    out_weight,
    up_weight,
    down_weight,
    time_weight,
    norm_gains,
    cotangent,
):
    seq_count, tokens, width = activations.shape
    local_width = qkv_weight.shape[2]
    heads_local = local_width // HEAD_DIM
    per_group = min(heads_local, max(1, 512 // tokens))
    while heads_local % per_group:
        per_group -= 1
    scaling = HEAD_DIM ** (-0.5)
    full_qkv, full_out, full_up, full_down, full_time, full_gains = (
        lax.all_gather(qkv_weight, "shard", axis=1, tiled=True),
        lax.all_gather(out_weight, "shard", axis=1, tiled=True),
        lax.all_gather(up_weight, "shard", axis=0, tiled=True),
        lax.all_gather(down_weight, "shard", axis=1, tiled=True),
        lax.all_gather(time_weight, "shard", axis=2, tiled=True),
        lax.all_gather(norm_gains, "shard", axis=1, tiled=True),
    )
    gains_f = full_gains.astype(jnp.float32)
    embedding = embed_time(timestep)
    modulation = jnp.einsum(
        "sk,kcd->scd", embedding, full_time.astype(jnp.float32), precision=highest
    )
    cosines, sines = rotary_tables(positions)
    inputs_f = activations.astype(jnp.float32)
    first_out, normed_one, inverse_one = scaled_norm(
        inputs_f, gains_f[0], modulation[:, 0], modulation[:, 1]
    )
    first_low = first_out.astype(jnp.bfloat16)
    projected = jnp.einsum("std,cde->cste", first_low, full_qkv, preferred_element_type=jnp.float32)
    head_shape = (seq_count, tokens, heads_local, HEAD_DIM)
    query_rot = (
        rotate(projected[0].reshape(head_shape), cosines, sines)
        .reshape(seq_count, tokens, local_width)
        .astype(jnp.bfloat16)
    )
    key_rot = (
        rotate(projected[1].reshape(head_shape), cosines, sines)
        .reshape(seq_count, tokens, local_width)
        .astype(jnp.bfloat16)
    )
    value_low = projected[2].astype(jnp.bfloat16)
    keys_all, values_all = (
        lax.all_gather(key_rot, "ctx", axis=1, tiled=True),
        lax.all_gather(value_low, "ctx", axis=1, tiled=True),
    )
    query_groups = group_heads(query_rot, per_group)
    attended, log_total = lax.map(
        partial(attend_block, scaling=scaling),
        (query_groups, group_heads(keys_all, per_group), group_heads(values_all, per_group)),
    )
    attended_low = ungroup_heads(attended, seq_count).astype(jnp.bfloat16)
    branch_part = jnp.einsum(
        "ste,ed->std", attended_low, full_out, preferred_element_type=jnp.float32
    )
    middle = inputs_f + lax.psum(branch_part, "tp")
    second_out, normed_two, inverse_two = scaled_norm(
        middle, gains_f[1], modulation[:, 2], modulation[:, 3]
    )
    second_low = second_out.astype(jnp.bfloat16)
    hidden = jnp.einsum("std,df->stf", second_low, full_up, preferred_element_type=jnp.float32)
    activated = jax.nn.gelu(hidden, approximate=False).astype(jnp.bfloat16)
    mlp_part = jnp.einsum("stf,fd->std", activated, full_down, preferred_element_type=jnp.float32)
    output = (middle + lax.psum(mlp_part, "tp")).astype(jnp.bfloat16)
    back_qkv, back_out, back_up, back_down = (
        lax.all_gather(qkv_weight, "shard", axis=1, tiled=True),
        lax.all_gather(out_weight, "shard", axis=1, tiled=True),
        lax.all_gather(up_weight, "shard", axis=0, tiled=True),
        lax.all_gather(down_weight, "shard", axis=1, tiled=True),
    )
    keys_back, values_back = (
        lax.all_gather(key_rot, "ctx", axis=1, tiled=True),
        lax.all_gather(value_low, "ctx", axis=1, tiled=True),
    )
    grad_down = jnp.einsum("stf,std->fd", activated, cotangent, preferred_element_type=jnp.float32)
    grad_act = jnp.einsum("std,fd->stf", cotangent, back_down, preferred_element_type=jnp.float32)
    grad_hidden = (grad_act * gelu_slope(hidden)).astype(jnp.bfloat16)
    grad_up = jnp.einsum("std,stf->df", second_low, grad_hidden, preferred_element_type=jnp.float32)
    grad_second = lax.psum(
        jnp.einsum("stf,df->std", grad_hidden, back_up, preferred_element_type=jnp.float32), "tp"
    )
    grad_mid_norm, gain_two, scaling_two, offset_two = norm_back(
        grad_second, normed_two, inverse_two, gains_f[1], modulation[:, 2]
    )
    grad_middle = cotangent.astype(jnp.float32) + grad_mid_norm
    grad_branch = grad_middle.astype(jnp.bfloat16)
    grad_out = jnp.einsum(
        "ste,std->ed", attended_low, grad_branch, preferred_element_type=jnp.float32
    )
    grad_attended = jnp.einsum(
        "std,ed->ste", grad_branch, back_out, preferred_element_type=jnp.float32
    ).astype(jnp.bfloat16)
    grad_query_g, grad_key_g, grad_value_g = lax.map(
        partial(attend_back, scaling=scaling),
        (
            query_groups,
            group_heads(keys_back, per_group),
            group_heads(values_back, per_group),
            group_heads(grad_attended, per_group),
            log_total,
        ),
    )
    grad_key_all = ungroup_heads(grad_key_g, seq_count)
    grad_value_all = ungroup_heads(grad_value_g, seq_count)
    grad_key, grad_value = (
        lax.psum_scatter(grad_key_all, "ctx", scatter_dimension=1, tiled=True),
        lax.psum_scatter(grad_value_all, "ctx", scatter_dimension=1, tiled=True),
    )
    grad_query = ungroup_heads(grad_query_g, seq_count)
    query_back = unrotate(grad_query.reshape(head_shape), cosines, sines).reshape(
        seq_count, tokens, local_width
    )
    key_back = unrotate(grad_key.reshape(head_shape), cosines, sines).reshape(
        seq_count, tokens, local_width
    )
    grad_projected = jnp.stack([query_back, key_back, grad_value], axis=0).astype(jnp.bfloat16)
    grad_qkv = jnp.einsum(
        "std,cste->cde", first_low, grad_projected, preferred_element_type=jnp.float32
    )
    grad_first = lax.psum(
        jnp.einsum("cste,cde->std", grad_projected, back_qkv, preferred_element_type=jnp.float32),
        "tp",
    )
    grad_in_norm, gain_one, scaling_one, offset_one = norm_back(
        grad_first, normed_one, inverse_one, gains_f[0], modulation[:, 0]
    )
    input_grad = (grad_middle + grad_in_norm).astype(jnp.bfloat16)
    grad_modulation = jnp.stack([scaling_one, offset_one, scaling_two, offset_two], axis=1)
    grad_time = jnp.einsum("sk,scd->kcd", embedding, grad_modulation, precision=highest)
    grad_gains = jnp.stack([gain_one, gain_two], axis=0)
    shares = (
        lax.psum_scatter(grad_qkv, "shard", scatter_dimension=1, tiled=True),
        lax.psum_scatter(grad_out, "shard", scatter_dimension=1, tiled=True),
        lax.psum_scatter(grad_up, "shard", scatter_dimension=0, tiled=True),
        lax.psum_scatter(grad_down, "shard", scatter_dimension=1, tiled=True),
        lax.psum_scatter(grad_time, "shard", scatter_dimension=2, tiled=True),
        lax.psum_scatter(grad_gains, "shard", scatter_dimension=1, tiled=True),
    )
    shares = lax.psum((shares[0], shares[1], shares[2], shares[3], shares[4], shares[5]), "ctx")
    return (output, input_grad, shares[0], shares[1], shares[2], shares[3], shares[4], shares[5])


BF = jnp.bfloat16
F32 = jnp.float32
NN = (((1,), (0,)), ((), ()))
NT = (((1,), (1,)), ((), ()))
TN = (((0,), (0,)), ((), ()))
VMEM_BIG = 56 << 20


def mm(a, b, dims=NN):
    return lax.dot_general(a, b, dims, preferred_element_type=F32)


def cost(flops, nbytes, trans=0):
    return pl.CostEstimate(flops=int(flops), bytes_accessed=int(nbytes), transcendentals=int(trans))


def whole(array):
    zeros = (0,) * array.ndim
    return pl.BlockSpec(array.shape, lambda *_: zeros)


def call(kernel, name, grid, scalars, ins, in_specs, outs, out_specs, est, scratch=()):
    return pl.pallas_call(
        kernel,
        out_shape=outs,
        grid_spec=pltpu.PrefetchScalarGridSpec(
            num_scalar_prefetch=len(scalars),
            grid=grid,
            in_specs=in_specs,
            out_specs=out_specs,
            scratch_shapes=list(scratch),
        ),
        compiler_params=pltpu.CompilerParams(vmem_limit_bytes=VMEM_BIG),
        cost_estimate=est,
        name=name,
    )(*scalars, *ins)


def shape(dims, dtype):
    return jax.ShapeDtypeStruct(dims, dtype)


def cols(index, width):
    return pl.ds(pl.multiple_of(index * width, width), width)


def half_turn(values):
    lane = lax.broadcasted_iota(jnp.int32, values.shape, 1) % HEAD_DIM
    width = values.shape[1]
    up = pltpu.roll(values, HEAD_DIM // 2, 1)
    down = pltpu.roll(values, width - HEAD_DIM // 2, 1)
    return jnp.where(lane < HEAD_DIM // 2, down, up)


def pick(step, first_ref, second_ref, per_half):
    return jnp.where(step < per_half, first_ref[...], second_ref[...])


def own_map(per_half):
    return lambda i, *_: (jnp.minimum(i, per_half - 1), 0)


def other_map(per_half):
    return lambda i, *_: (jnp.maximum(i - per_half, 0), 0)


def project_kernel(per_half, blk, xa, xb, w0, w1, w2, w3, mods, cosb, sinb, h_ref, q_ref, k_ref, kt_ref, v_ref, vt_ref):
    x = pick(pl.program_id(0), xa, xb, per_half).astype(F32)
    x = x - jnp.mean(x, axis=1, keepdims=True)
    var = jnp.mean(x * x, axis=1, keepdims=True)
    n = x * lax.rsqrt(var + norm_epsilon)
    h_ref[...] = (n * mods[0:1, :] + mods[1:2, :]).astype(BF)
    rows = w0.shape[0]
    acc = None
    for j, w in enumerate((w0, w1, w2, w3)):
        part = mm(h_ref[:, cols(blk[j], rows)], w[...])
        acc = part if acc is None else acc + part
    wide = acc.shape[1] // 3
    cosines, sines = cosb[...], sinb[...]
    q = acc[:, :wide]
    k = acc[:, wide : 2 * wide]
    v = acc[:, 2 * wide :]
    q = q * cosines + half_turn(q) * sines
    k = k * cosines + half_turn(k) * sines
    q_ref[...] = q.astype(BF)
    k_ref[...] = k.astype(BF)
    kt_ref[...] = k.T.astype(BF)
    v_ref[...] = v.astype(BF)
    vt_ref[...] = v.T.astype(BF)


def project(blk, xa, xb, ws, mods, cosb, sinb, tile=256):
    half, width = xa.shape
    total = 2 * half
    wide = ws[0].shape[1] // 3
    per_half = half // tile
    row = lambda w: pl.BlockSpec((tile, w), lambda i, *_: (i, 0))
    turned = pl.BlockSpec((wide, tile), lambda i, *_: (0, i))
    return call(
        partial(project_kernel, per_half), "project", (total // tile,), (blk,),
        (xa, xb, *ws, mods, cosb, sinb),
        [pl.BlockSpec((tile, width), own_map(per_half)), pl.BlockSpec((tile, width), other_map(per_half)),
         *[whole(w) for w in ws], whole(mods), row(wide), row(wide)],
        [shape((total, width), BF), shape((total, wide), BF), shape((total, wide), BF), shape((wide, total), BF),
         shape((total, wide), BF), shape((wide, total), BF)],
        [row(width), row(wide), row(wide), turned, row(wide), turned],
        cost(2 * total * width * 3 * wide, 4 * total * width + 10 * total * wide),
    )


def attend_kernel(scale, q_ref, k_ref, vt_ref, o_ref, ot_ref, lse_ref):
    rows, wide = q_ref.shape
    q = q_ref[...]
    lane = lax.broadcasted_iota(jnp.int32, (rows, wide), 1) // HEAD_DIM
    for h in range(wide // HEAD_DIM):
        at = slice(h * HEAD_DIM, (h + 1) * HEAD_DIM)
        qh = jnp.where(lane == h, q, jnp.zeros_like(q))
        s = mm(k_ref[...], qh, NT) * scale
        top = jnp.max(s, axis=0, keepdims=True)
        p = jnp.exp(s - top)
        total = jnp.sum(p, axis=0, keepdims=True)
        ot_ref[at, :] = mm(vt_ref[at, :], p.astype(BF)) / total
        lse_ref[h : h + 1, :] = top + jnp.log(total)
    o_ref[...] = ot_ref[...].T.astype(BF)


def attend(q, k, vt, tile=512):
    total, wide = q.shape
    heads = wide // HEAD_DIM
    return call(
        partial(attend_kernel, HEAD_DIM**-0.5), "attend", (total // tile,), (), (q, k, vt),
        [pl.BlockSpec((tile, wide), lambda i: (i, 0)), whole(k), whole(vt)],
        [shape((total, wide), BF), shape((wide, total), F32), shape((heads, total), F32)],
        [pl.BlockSpec((tile, wide), lambda i: (i, 0)), pl.BlockSpec((wide, tile), lambda i: (0, i)),
         pl.BlockSpec((heads, tile), lambda i: (0, i))],
        cost(16 * total * total * wide, 8 * total * wide, total * total * heads),
    )


def join_kernel(blk, blo, x_ref, o0, o1, o2, o3, a0, a1, a2, a3, b0, b1, b2, b3, mods, x1_ref, h_ref):
    wide = o0.shape[1] // 2
    slots = (o0, o1, o2, o3)
    own = jnp.concatenate([o[:, :wide] for o in slots], axis=1)
    oth = jnp.concatenate([o[:, wide:] for o in slots], axis=1)
    span = a0.shape[1]
    for j, w in enumerate((a0, a1, a2, a3)):
        at = cols(blk[j], span)
        x1_ref[:, at] = x_ref[:, at].astype(F32) + mm(own, w[...])
    for j, w in enumerate((b0, b1, b2, b3)):
        at = cols(blo[j], span)
        x1_ref[:, at] += mm(oth, w[...])
    x = x1_ref[...]
    x = x - jnp.mean(x, axis=1, keepdims=True)
    var = jnp.mean(x * x, axis=1, keepdims=True)
    n = x * lax.rsqrt(var + norm_epsilon)
    h_ref[...] = (n * mods[2:3, :] + mods[3:4, :]).astype(BF)


def join(blk, blo, x, os, wa, wb, mods, tile=256):
    half, width = x.shape
    row = lambda w: pl.BlockSpec((tile, w), lambda i, *_: (i, 0))
    return call(
        join_kernel, "join", (half // tile,), (blk, blo), (x, *os, *wa, *wb, mods),
        [row(width), *[row(o.shape[1]) for o in os], *[whole(w) for w in (*wa, *wb)], whole(mods)],
        [shape((half, width), F32), shape((half, width), BF)],
        [row(width), row(width)],
        cost(2 * half * width * width, 10 * half * width),
    )


def gelu_parts(u):
    half = 0.5 * (1.0 + lax.erf(u * 0.7071067811865476))
    slope = half + u * jnp.exp(-0.5 * u * u) * 0.3989422804014327
    return u * half, slope


def mlp_kernel(per_half, n_slots, has_base, keep_du, blk, *refs):
    ha, hb, ca, cb = refs[:4]
    ws = [refs[4 + 4 * i : 8 + 4 * i] for i in range(n_slots)]
    at = 4 + 4 * n_slots
    base = refs[at] if has_base else None
    at += has_base
    dh_ref = refs[at]
    g_ref = refs[at + 1]
    du_ref = refs[at + 2] if keep_du else None
    h_buf, c_buf = refs[at + 2 + keep_du :]
    step = pl.program_id(0)
    h_buf[...] = pick(step, ha, hb, per_half)
    c_buf[...] = pick(step, ca, cb, per_half)
    span = ws[0][0].shape[1]
    for i, slot in enumerate(ws):
        for b in range(2):
            up = slice(b * span, (b + 1) * span)
            down = slice((2 + b) * span, (3 + b) * span)
            u = dg = None
            for j, w in enumerate(slot):
                here = cols(blk[j], span)
                part = mm(h_buf[:, here], w[up, :])
                u = part if u is None else u + part
                part = mm(c_buf[:, here], w[down, :], NT)
                dg = part if dg is None else dg + part
            g, slope = gelu_parts(u)
            du = (dg * slope).astype(BF)
            g_ref[:, (2 * i + b) * span : (2 * i + b + 1) * span] = g.astype(BF)
            if keep_du and i == 0:
                du_ref[:, up] = du
            for j, w in enumerate(slot):
                here = cols(blk[j], span)
                part = mm(du, w[up, :], NT)
                if i == 0 and b == 0:
                    dh_ref[:, here] = base[:, here] + part if has_base else part
                else:
                    dh_ref[:, here] += part


def mlp(blk, ha, hb, ca, cb, slots, base, keep_du, tile=256):
    half, width = ha.shape
    total = 2 * half
    per_half = half // tile
    n_slots = len(slots)
    hidden = 2 * slots[0][0].shape[1]
    row = lambda w: pl.BlockSpec((tile, w), lambda i, *_: (i, 0))
    mine = pl.BlockSpec((tile, width), own_map(per_half))
    theirs = pl.BlockSpec((tile, width), other_map(per_half))
    flat = [w for slot in slots for w in slot]
    ins = [ha, hb, ca, cb, *flat]
    specs = [mine, theirs, mine, theirs, *[whole(w) for w in flat]]
    if base is not None:
        ins.append(base)
        specs.append(row(width))
    outs = [shape((total, width), F32), shape((total, n_slots * hidden), BF)]
    out_specs = [row(width), row(n_slots * hidden)]
    if keep_du:
        outs.append(shape((total, hidden), BF))
        out_specs.append(row(hidden))
    return call(
        partial(mlp_kernel, per_half, n_slots, int(base is not None), int(keep_du)),
        "mlp", (total // tile,), (blk,), ins, specs, outs, out_specs,
        cost(6 * total * width * hidden * n_slots, total * width * 12, total * hidden * n_slots * 4),
        [pltpu.VMEM((tile, width), BF), pltpu.VMEM((tile, width), BF)],
    )


def lift_kernel(groups, per_half, blk, *refs):
    n = sum(groups)
    gs = refs[: len(groups)]
    ws = [refs[len(groups) + 4 * i : len(groups) + 4 * i + 4] for i in range(n)]
    own_ref, oth_ref, buf = refs[len(groups) + 4 * n :]
    span = ws[0][0].shape[1]
    for j in range(4):
        here = cols(blk[j], span)
        acc = None
        i = 0
        for g, count in zip(gs, groups):
            for k in range(count):
                for b in range(2):
                    part = mm(g[:, (2 * k + b) * span : (2 * k + b + 1) * span], ws[i][j][(2 + b) * span : (3 + b) * span, :])
                    acc = part if acc is None else acc + part
                i += 1
        buf[:, here] = acc
    step = pl.program_id(0)

    @pl.when(step < per_half)
    def _():
        own_ref[...] = buf[...]

    @pl.when(step >= per_half)
    def _():
        oth_ref[...] = buf[...].astype(BF)


def lift(blk, gs, groups, slots, width, tile=256):
    total = gs[0].shape[0]
    half = total // 2
    per_half = half // tile
    flat = [w for slot in slots for w in slot]
    return call(
        partial(lift_kernel, groups, per_half), "lift", (total // tile,), (blk,), (*gs, *flat),
        [*[pl.BlockSpec((tile, g.shape[1]), lambda i, *_: (i, 0)) for g in gs], *[whole(w) for w in flat]],
        [shape((half, width), F32), shape((half, width), BF)],
        [pl.BlockSpec((tile, width), own_map(per_half)), pl.BlockSpec((tile, width), other_map(per_half))],
        cost(2 * total * width * sum(g.shape[1] for g in gs), total * width * 8),
        [pltpu.VMEM((tile, width), F32)],
    )


def norm_turn(dh, x, factor):
    x = x - jnp.mean(x, axis=1, keepdims=True)
    var = jnp.mean(x * x, axis=1, keepdims=True)
    r = lax.rsqrt(var + norm_epsilon)
    n = x * r
    dn = dh * factor
    dx = r * (dn - jnp.mean(dn, axis=1, keepdims=True) - n * jnp.mean(dn * n, axis=1, keepdims=True))
    return dx, jnp.sum(dh * n, axis=0, keepdims=True), jnp.sum(dh, axis=0, keepdims=True)


def turn_kernel(blk, blo, dh_ref, in_ref, x_ref, c_ref, mods, a0, a1, a2, a3, b0, b1, b2, b3, dx_ref, da_ref, own_ref, oth_ref, sums):
    dh = dh_ref[...] + in_ref[...].astype(F32)
    dx, s1, s0 = norm_turn(dh, x_ref[...], mods[2:3, :])
    dx = dx + c_ref[...].astype(F32)
    dx_ref[...] = dx
    da_ref[...] = dx.astype(BF)
    wide = own_ref.shape[1]
    span = a0.shape[1]
    for order, ws, out in ((blk, (a0, a1, a2, a3), own_ref), (blo, (b0, b1, b2, b3), oth_ref)):
        acc = None
        for j, w in enumerate(ws):
            part = mm(da_ref[:, cols(order[j], span)], w[0:wide, :], NT)
            acc = part if acc is None else acc + part
        out[...] = acc.astype(BF)

    @pl.when(pl.program_id(0) == 0)
    def _():
        sums[...] = jnp.zeros_like(sums)

    sums[0:1, :] += s1
    sums[1:2, :] += s0


def turn(blk, blo, dh, received, x1, cot, mods, wa, wb, wide, tile=256):
    half, width = x1.shape
    row = lambda w: pl.BlockSpec((tile, w), lambda i, *_: (i, 0))
    return call(
        turn_kernel, "turn", (half // tile,), (blk, blo), (dh, received, x1, cot, mods, *wa, *wb),
        [row(width)] * 4 + [whole(mods), *[whole(w) for w in (*wa, *wb)]],
        [shape((half, width), F32), shape((half, width), BF), shape((half, wide), BF), shape((half, wide), BF), shape((8, width), F32)],
        [row(width), row(width), row(wide), row(wide), pl.BlockSpec((8, width), lambda i, *_: (0, 0))],
        cost(4 * half * width * wide, half * width * 18),
    )


def attend_back_kernel(scale, tk, per_half, q_ref, da_ref, db_ref, ot_ref, lse_ref, cos_ref, sin_ref, k_ref, v_ref, kt_ref, cosb, sinb, dq_ref, dk_ref, dv_ref, dqt, dk_acc, dv_acc):
    rows, wide = q_ref.shape
    total = k_ref.shape[0]
    step = pl.program_id(0)
    q = q_ref[...]
    do = pick(step, da_ref, db_ref, per_half)
    lane = lax.broadcasted_iota(jnp.int32, (rows, wide), 1) // HEAD_DIM
    heads = wide // HEAD_DIM
    qs = [jnp.where(lane == h, q, jnp.zeros_like(q)) for h in range(heads)]
    ds = [jnp.where(lane == h, do, jnp.zeros_like(do)) for h in range(heads)]
    od = do.astype(F32).T * ot_ref[...]
    deltas = [jnp.sum(od[h * HEAD_DIM : (h + 1) * HEAD_DIM, :], axis=0, keepdims=True) for h in range(heads)]

    @pl.when(step == 0)
    def _():
        dk_acc[...] = jnp.zeros_like(dk_acc)
        dv_acc[...] = jnp.zeros_like(dv_acc)

    dqt[...] = jnp.zeros_like(dqt)
    for j in range(total // tk):
        at = slice(j * tk, (j + 1) * tk)
        kj, vj = k_ref[at, :], v_ref[at, :]
        for h in range(heads):
            hs = slice(h * HEAD_DIM, (h + 1) * HEAD_DIM)
            s = mm(kj, qs[h], NT) * scale
            p = jnp.exp(s - lse_ref[h : h + 1, :])
            dp = mm(vj, ds[h], NT)
            dsc = (p * (dp - deltas[h])).astype(BF)
            dv_acc[at, :] += mm(p.astype(BF), ds[h])
            dk_acc[at, :] += mm(dsc, qs[h])
            dqt[hs, :] += mm(kt_ref[hs, at], dsc)
    dq = dqt[...].T * scale
    dq_ref[...] = (dq * cos_ref[...] - half_turn(dq) * sin_ref[...]).astype(BF)

    @pl.when(step == pl.num_programs(0) - 1)
    def _():
        dk = dk_acc[...] * scale
        dk_ref[...] = (dk * cosb[...] - half_turn(dk) * sinb[...]).astype(BF)
        dv_ref[...] = dv_acc[...].astype(BF)


def attend_back_call(q, do_a, do_b, ot, lse, k, v, kt, cosb, sinb, tile=512, tk=512):
    total, wide = q.shape
    heads = wide // HEAD_DIM
    per_half = total // 2 // tile
    row = pl.BlockSpec((tile, wide), lambda i: (i, 0))
    lanes = lambda h: pl.BlockSpec((h, tile), lambda i: (0, i))
    full = pl.BlockSpec((total, wide), lambda i: (0, 0))
    return call(
        partial(attend_back_kernel, HEAD_DIM**-0.5, tk, per_half), "attend_back", (total // tile,), (),
        (q, do_a, do_b, ot, lse, cosb, sinb, k, v, kt, cosb, sinb),
        [row, pl.BlockSpec((tile, wide), own_map(per_half)), pl.BlockSpec((tile, wide), other_map(per_half)),
         lanes(wide), lanes(heads), row, row, full, full, whole(kt), full, full],
        [shape((total, wide), BF)] * 3,
        [row, full, full],
        cost(40 * total * total * wide, 20 * total * wide, total * total * heads),
        [pltpu.VMEM((wide, tile), F32), pltpu.VMEM((total, wide), F32), pltpu.VMEM((total, wide), F32)],
    )


def spread_kernel(per_half, blk, q_ref, k_ref, v_ref, w0, w1, w2, w3, own_ref, oth_ref, buf):
    d = jnp.concatenate([q_ref[...], k_ref[...], v_ref[...]], axis=1)
    rows = w0.shape[0]
    for j, w in enumerate((w0, w1, w2, w3)):
        buf[:, cols(blk[j], rows)] = mm(d, w[...], NT)
    step = pl.program_id(0)

    @pl.when(step < per_half)
    def _():
        own_ref[...] = buf[...]

    @pl.when(step >= per_half)
    def _():
        oth_ref[...] = buf[...].astype(BF)


def spread(blk, dq, dk, dv, ws, width, tile=256):
    total, wide = dq.shape
    half = total // 2
    per_half = half // tile
    row = pl.BlockSpec((tile, wide), lambda i, *_: (i, 0))
    return call(
        partial(spread_kernel, per_half), "spread", (total // tile,), (blk,), (dq, dk, dv, *ws),
        [row, row, row, *[whole(w) for w in ws]],
        [shape((half, width), F32), shape((half, width), BF)],
        [pl.BlockSpec((tile, width), own_map(per_half)), pl.BlockSpec((tile, width), other_map(per_half))],
        cost(6 * total * width * wide, total * width * 4),
        [pltpu.VMEM((tile, width), F32)],
    )


def last_kernel(dh_ref, x_ref, dx_ref, mods, out_ref, sums):
    dx, s1, s0 = norm_turn(dh_ref[...], x_ref[...].astype(F32), mods[0:1, :])
    out_ref[...] = (dx + dx_ref[...]).astype(BF)
    sums[...] = jnp.zeros_like(sums)
    sums[0:1, :] = s1
    sums[1:2, :] = s0


def last(dh, x, dx, mods):
    rows, width = dh.shape
    return call(
        last_kernel, "last", (1,), (), (dh, x, dx, mods), [whole(v) for v in (dh, x, dx, mods)],
        [shape((rows, width), BF), shape((8, width), F32)],
        [pl.BlockSpec((rows, width), lambda i: (0, 0)), pl.BlockSpec((8, width), lambda i: (0, 0))],
        cost(20 * rows * width, 12 * rows * width),
    )


def ring_order(n):
    if n == 4:
        return [0, 1, 3, 2]
    return list(range(n))


def fast_body(
    activations, timestep, positions, qkv_weight, out_weight, up_weight, down_weight, time_weight, norm_gains, cotangent
):
    n_s, n_t = lax.axis_size("shard"), lax.axis_size("tp")
    s, c, t = lax.axis_index("shard"), lax.axis_index("ctx"), lax.axis_index("tp")
    x_own = activations[0]
    cot_own = cotangent[0]
    half, width = x_own.shape
    total = 2 * half
    span = width // n_s
    quarter = half // n_t
    order = ring_order(n_s)
    place = {v: i for i, v in enumerate(order)}
    walk = [
        pair
        for v in range(n_s)
        for pair in (
            (v * 2, order[(place[v] + 1) % n_s] * 2),
            (v * 2 + 1, order[(place[v] - 1) % n_s] * 2 + 1),
        )
    ]
    cycle = [(i, (i + 1) % n_t) for i in range(n_t)]
    table = jnp.array(
        [[[order[(place[v] - j) % n_s] for j in range(n_s)], [order[(place[v] + j) % n_s] for j in range(n_s)]] for v in range(n_s)],
        jnp.int32,
    )
    blk = table[s, c]
    blo = table[s, 1 - c]
    swap = lambda v: lax.ppermute(v, "ctx", [(0, 1), (1, 0)])
    along = lambda v: lax.ppermute(v, ("shard", "ctx"), walk)
    upward = lambda v: lax.ppermute(v, "tp", cycle)

    def ring(v, move, n):
        out = [v]
        for _ in range(n - 1):
            out.append(move(out[-1]))
        return out

    def turn_shard(v, d):
        return lax.ppermute(v, "shard", [(i, (i + d) % n_s) for i in range(n_s)])

    def half_of(v, axis):
        size = v.shape[axis] // 2
        return lax.dynamic_slice_in_dim(v, c * size, size, axis)

    def both(v, axis):
        other = swap(v)
        return jnp.where(c == 0, jnp.concatenate([v, other], axis), jnp.concatenate([other, v], axis))

    wide = qkv_weight.shape[2] // 2
    qkv_half = half_of(qkv_weight, 2)
    w_qkv = ring(jnp.concatenate([qkv_half[0], qkv_half[1], qkv_half[2]], axis=1), along, n_s)
    out_half = ring(half_of(out_weight, 0), upward, n_t)
    w_out = ring(jnp.concatenate(out_half, axis=0), along, n_s)
    up_half = half_of(up_weight, 1)
    down_half = half_of(down_weight, 0)
    pack = jnp.concatenate([up_half[:, :span], up_half[:, span:], down_half], axis=0)
    packs = ring(pack, upward, n_t)
    w_mlp = [ring(v, along, n_s) for v in packs]
    w_out_other = [swap(v) for v in w_out]

    gains = norm_gains.astype(F32)
    small = jnp.concatenate([gains, jnp.broadcast_to(timestep.astype(F32)[:, None], (1, span))], axis=0)
    smalls = [small] + [turn_shard(small, d) for d in range(1, n_s)]
    steps = jnp.stack([v[2, 0] for v in smalls])
    embedding = embed_time(steps)
    parts = jnp.einsum("sk,kcd->scd", embedding, time_weight.astype(F32), precision=highest)
    gain_full = jnp.zeros((2, width), F32)
    mod_full = jnp.zeros((4, width), F32)
    for d in range(n_s):
        from_s = (s - d) % n_s
        gain_full = lax.dynamic_update_slice_in_dim(gain_full, smalls[d][:2], from_s * span, 1)
        got = parts[0] if d == 0 else turn_shard(parts[d], n_s - d)
        mod_full = lax.dynamic_update_slice_in_dim(mod_full, got, ((s + d) % n_s) * span, 1)
    factor_one = gain_full[0] * (1.0 + mod_full[0])
    factor_two = gain_full[1] * (1.0 + mod_full[2])
    zero = jnp.zeros_like(factor_one)
    mods = jnp.stack([factor_one, mod_full[1], factor_two, mod_full[3], zero, zero, zero, zero])

    half_width = HEAD_DIM // 2
    frequency = jnp.exp(-math.log(10000.0) * jnp.arange(half_width, dtype=F32) / half_width)
    pos_own = positions.astype(F32)
    pos_all = jnp.concatenate([pos_own, swap(pos_own)], axis=1)
    angles = frequency[:, None] * pos_all
    cosines, sines = jnp.cos(angles).T, jnp.sin(angles).T
    cosb = jnp.tile(cosines, (1, wide // half_width))
    sinb = jnp.tile(jnp.concatenate([-sines, sines], axis=1), (1, wide // HEAD_DIM))

    x_oth = swap(x_own)
    cot_oth = swap(cot_own)
    h1, q, k, kt, v, vt = project(blk, x_own, x_oth, w_qkv, mods, cosb, sinb)
    o, ot, lse = attend(q, k, vt)
    o_mine = jnp.concatenate([o[:half], swap(o[half:])], axis=1)
    o_slots = ring(o_mine, upward, n_t)
    x1, h2 = join(blk, blo, x_own, o_slots, w_out, w_out_other, mods)
    h2_oth = swap(h2)
    groups = (3, 1) if n_t == 4 else (n_t,)
    dh2, gs, first, du0 = None, [], 0, None
    for count in groups:
        res = mlp(blk, h2, h2_oth, cot_own, cot_oth, w_mlp[first : first + count], dh2, first == 0)
        dh2 = res[0]
        gs.append(res[1])
        if first == 0:
            du0 = res[2]
        first += count
    dh2_in = swap(dh2[half:].astype(BF))
    y_own, y_send = lift(blk, gs, groups, w_mlp, width)
    output = (x1 + y_own + swap(y_send).astype(F32)).astype(BF)
    dx1, da, do_own, do_send, sums_two = turn(blk, blo, dh2, dh2_in, x1, cot_own, mods, w_out, w_out_other, wide)
    do_got = swap(do_send)
    dq, dk, dv = attend_back_call(q, do_own, do_got, ot, lse, k, v, kt, cosb, sinb)
    dh1_own, dh1_send = spread(blk, dq, dk, dv, w_qkv, width)
    dh1 = dh1_own + swap(dh1_send).astype(F32)

    def token_block(v, j):
        return lax.dynamic_slice_in_dim(v, ((t - j) % n_t) * quarter, quarter, 0)

    moving = token_block(dh1, 1).astype(BF)
    for j in range(2, n_t):
        moving = (upward(moving).astype(F32) + token_block(dh1, j)).astype(BF)
    dh1_mine = upward(moving).astype(F32) + token_block(dh1, 0)
    grad_mine, sums_one = last(dh1_mine, token_block(x_own, 0), token_block(dx1, 0), mods)
    grad_slots = ring(grad_mine, upward, n_t)
    input_grad = jnp.zeros((half, width), BF)
    for j, piece in enumerate(grad_slots):
        input_grad = lax.dynamic_update_slice_in_dim(input_grad, piece, ((t - j) % n_t) * quarter, 0)

    def reduce_ring(pieces):
        going = pieces(1).astype(BF)
        for j in range(2, n_s):
            going = (along(going).astype(F32) + pieces(j)).astype(BF)
        return along(going).astype(F32) + pieces(0)

    g0 = gs[0][:, : 2 * span]
    h2_all = jnp.concatenate([h2, h2_oth], axis=0)
    cot_all = jnp.concatenate([cot_own, cot_oth], axis=0)
    g_up = mm(h2_all, du0, TN)
    g_down = mm(g0, cot_all, TN)
    o_first = o_slots[0]
    g_out_own = mm(o_first[:, :wide], da, TN)
    g_out = g_out_own + swap(mm(o_first[:, wide:], da, TN))

    def mlp_piece(j):
        ups = lax.dynamic_slice_in_dim(g_up, blk[j] * span, span, 0)
        downs = lax.dynamic_slice_in_dim(g_down, blk[j] * span, span, 1)
        outs = lax.dynamic_slice_in_dim(g_out, blk[j] * span, span, 1)
        return jnp.concatenate([ups[:, :span], ups[:, span:], downs, outs], axis=0)

    done = reduce_ring(mlp_piece)
    grad_up = both(jnp.concatenate([done[:span], done[span : 2 * span]], axis=1), 1)
    grad_down = both(done[2 * span : 4 * span], 0)
    grad_out = both(done[4 * span :], 0)
    g_qkv = mm(h1, jnp.concatenate([dq, dk, dv], axis=1), TN)
    done_qkv = reduce_ring(lambda j: lax.dynamic_slice_in_dim(g_qkv, blk[j] * span, span, 0))
    grad_qkv = both(jnp.stack([done_qkv[:, i * wide : (i + 1) * wide] for i in range(3)]), 2)

    keep = jnp.where(t == 0, 1.0, 0.0)
    tally = jnp.concatenate([sums_one[:2], sums_two[:2] * keep], axis=0)
    tally = tally + swap(tally)
    full = tally
    for d in range(1, n_t):
        full = full + lax.ppermute(tally, "tp", [(i, (i + d) % n_t) for i in range(n_t)])
    dmods = jnp.stack([full[0] * gain_full[0], full[1], full[2] * gain_full[1], full[3],
                       full[0] * (1.0 + mod_full[0]), full[2] * (1.0 + mod_full[2])])
    per_seq = []
    for d in range(n_s):
        block = lax.dynamic_slice_in_dim(dmods, ((s + d) % n_s) * span, span, 1)
        per_seq.append(block if d == 0 else turn_shard(block, d))
    seqs = jnp.stack(per_seq)
    grad_time = jnp.einsum("sk,scd->kcd", embedding, seqs[:, :4], precision=highest)
    grad_gains = jnp.sum(seqs[:, 4:], axis=0)
    return (output[None], input_grad[None], grad_qkv, grad_out, grad_up, grad_down, grad_time, grad_gains)


def solution(mesh):
    sizes = dict(mesh.shape)
    chosen = fast_body if sizes["ctx"] == 2 and sizes["shard"] == 4 else body
    placed = (
        P("shard", "ctx", None),
        P("shard"),
        P("shard", "ctx"),
        P(None, "shard", "tp"),
        P("tp", "shard"),
        P("shard", "tp"),
        P("tp", "shard"),
        P(None, None, "shard"),
        P(None, "shard"),
        P("shard", "ctx", None),
    )
    return jax.shard_map(
        chosen,
        mesh=mesh,
        in_specs=placed,
        out_specs=(
            P("shard", "ctx", None),
            P("shard", "ctx", None),
            P(None, "shard", "tp"),
            P("tp", "shard"),
            P("shard", "tp"),
            P("tp", "shard"),
            P(None, None, "shard"),
            P(None, "shard"),
        ),
        check_vma=False,
    )
```

```python
from functools import partial
import math

import jax
import jax.numpy as jnp
from jax import lax
from jax.experimental import pallas as pl
from jax.experimental.pallas import tpu as pltpu
from jax.sharding import PartitionSpec as P

HEAD_DIM = 64
TEMB = 256


highest = lax.Precision.HIGHEST
norm_epsilon = 1e-05


def embed_time(timestep):
    half_width = TEMB // 2
    frequency = jnp.exp(-math.log(10000.0) * jnp.arange(half_width, dtype=jnp.float32) / half_width)
    angles = timestep.astype(jnp.float32)[:, None] * frequency[None, :]
    return jnp.concatenate([jnp.sin(angles), jnp.cos(angles)], axis=-1)


def rotary_tables(positions):
    half_width = HEAD_DIM // 2
    frequency = jnp.exp(-math.log(10000.0) * jnp.arange(half_width, dtype=jnp.float32) / half_width)
    angles = positions.astype(jnp.float32)[..., None] * frequency
    return (jnp.cos(angles), jnp.sin(angles))


def rotate(heads_in, cosines, sines):
    half_width = HEAD_DIM // 2
    first = heads_in[..., :half_width]
    second = heads_in[..., half_width:]
    cos_wide = cosines[..., None, :]
    sin_wide = sines[..., None, :]
    return jnp.concatenate(
        [first * cos_wide - second * sin_wide, second * cos_wide + first * sin_wide], axis=-1
    )


def unrotate(heads_in, cosines, sines):
    half_width = HEAD_DIM // 2
    first = heads_in[..., :half_width]
    second = heads_in[..., half_width:]
    cos_wide = cosines[..., None, :]
    sin_wide = sines[..., None, :]
    return jnp.concatenate(
        [first * cos_wide + second * sin_wide, second * cos_wide - first * sin_wide], axis=-1
    )


def scaled_norm(values, gain_vec, scaling, offset):
    centered = values - jnp.mean(values, axis=-1, keepdims=True)
    variance = jnp.mean(centered * centered, axis=-1, keepdims=True)
    inverse_std = lax.rsqrt(variance + norm_epsilon)
    normed = centered * inverse_std
    return (
        normed * gain_vec * (1.0 + scaling[:, None, :]) + offset[:, None, :],
        normed,
        inverse_std,
    )


def norm_back(grad_in, normed, inverse_std, gain_vec, scaling):
    factor = gain_vec * (1.0 + scaling[:, None, :])
    grad_normed = grad_in * factor
    grad_values = inverse_std * (
        grad_normed
        - jnp.mean(grad_normed, axis=-1, keepdims=True)
        - normed * jnp.mean(grad_normed * normed, axis=-1, keepdims=True)
    )
    grad_gain = jnp.sum(grad_in * normed * (1.0 + scaling[:, None, :]), axis=(0, 1))
    grad_scaling = jnp.sum(grad_in * normed * gain_vec, axis=1)
    grad_offset = jnp.sum(grad_in, axis=1)
    return (grad_values, grad_gain, grad_scaling, grad_offset)


def group_heads(field, per_group):
    seq_count, rows_count, _ = field.shape
    split = field.reshape(seq_count, rows_count, -1, HEAD_DIM).transpose(0, 2, 1, 3)
    return split.reshape(-1, per_group, rows_count, HEAD_DIM)


def ungroup_heads(field, seq_count):
    rows_count = field.shape[2]
    joined = field.reshape(seq_count, -1, rows_count, HEAD_DIM).transpose(0, 2, 1, 3)
    return joined.reshape(seq_count, rows_count, -1)


def attend_block(triple, scaling):
    queries, keys, values = triple
    scores = jnp.einsum("gqd,gkd->gqk", queries, keys, preferred_element_type=jnp.float32) * scaling
    top_score = jnp.max(scores, axis=-1, keepdims=True)
    raised = jnp.exp(scores - top_score)
    total = jnp.sum(raised, axis=-1, keepdims=True)
    weights = (raised / total).astype(jnp.bfloat16)
    attended = jnp.einsum("gqk,gkd->gqd", weights, values, preferred_element_type=jnp.float32)
    return (attended, (top_score + jnp.log(total))[..., 0])


def attend_back(bundle, scaling):
    queries, keys, values, grad_out, log_total = bundle
    scores = jnp.einsum("gqd,gkd->gqk", queries, keys, preferred_element_type=jnp.float32) * scaling
    weights = jnp.exp(scores - log_total[..., None])
    grad_values = jnp.einsum(
        "gqk,gqd->gkd", weights.astype(jnp.bfloat16), grad_out, preferred_element_type=jnp.float32
    )
    grad_weights = jnp.einsum("gqd,gkd->gqk", grad_out, values, preferred_element_type=jnp.float32)
    row_term = jnp.sum(weights * grad_weights, axis=-1, keepdims=True)
    grad_scores = (weights * (grad_weights - row_term)).astype(jnp.bfloat16)
    grad_queries = (
        jnp.einsum("gqk,gkd->gqd", grad_scores, keys, preferred_element_type=jnp.float32) * scaling
    )
    grad_keys = (
        jnp.einsum("gqk,gqd->gkd", grad_scores, queries, preferred_element_type=jnp.float32)
        * scaling
    )
    return (grad_queries, grad_keys, grad_values)


def gelu_slope(hidden):
    return (
        0.5 * (1.0 + lax.erf(hidden * 0.7071067811865476))
        + hidden * jnp.exp(-0.5 * hidden * hidden) * 0.3989422804014327
    )


def body(
    activations,
    timestep,
    positions,
    qkv_weight,
    out_weight,
    up_weight,
    down_weight,
    time_weight,
    norm_gains,
    cotangent,
):
    seq_count, tokens, width = activations.shape
    local_width = qkv_weight.shape[2]
    heads_local = local_width // HEAD_DIM
    per_group = min(heads_local, max(1, 512 // tokens))
    while heads_local % per_group:
        per_group -= 1
    scaling = HEAD_DIM ** (-0.5)
    full_qkv, full_out, full_up, full_down, full_time, full_gains = (
        lax.all_gather(qkv_weight, "shard", axis=1, tiled=True),
        lax.all_gather(out_weight, "shard", axis=1, tiled=True),
        lax.all_gather(up_weight, "shard", axis=0, tiled=True),
        lax.all_gather(down_weight, "shard", axis=1, tiled=True),
        lax.all_gather(time_weight, "shard", axis=2, tiled=True),
        lax.all_gather(norm_gains, "shard", axis=1, tiled=True),
    )
    gains_f = full_gains.astype(jnp.float32)
    embedding = embed_time(timestep)
    modulation = jnp.einsum(
        "sk,kcd->scd", embedding, full_time.astype(jnp.float32), precision=highest
    )
    cosines, sines = rotary_tables(positions)
    inputs_f = activations.astype(jnp.float32)
    first_out, normed_one, inverse_one = scaled_norm(
        inputs_f, gains_f[0], modulation[:, 0], modulation[:, 1]
    )
    first_low = first_out.astype(jnp.bfloat16)
    projected = jnp.einsum("std,cde->cste", first_low, full_qkv, preferred_element_type=jnp.float32)
    head_shape = (seq_count, tokens, heads_local, HEAD_DIM)
    query_rot = (
        rotate(projected[0].reshape(head_shape), cosines, sines)
        .reshape(seq_count, tokens, local_width)
        .astype(jnp.bfloat16)
    )
    key_rot = (
        rotate(projected[1].reshape(head_shape), cosines, sines)
        .reshape(seq_count, tokens, local_width)
        .astype(jnp.bfloat16)
    )
    value_low = projected[2].astype(jnp.bfloat16)
    keys_all, values_all = (
        lax.all_gather(key_rot, "ctx", axis=1, tiled=True),
        lax.all_gather(value_low, "ctx", axis=1, tiled=True),
    )
    query_groups = group_heads(query_rot, per_group)
    attended, log_total = lax.map(
        partial(attend_block, scaling=scaling),
        (query_groups, group_heads(keys_all, per_group), group_heads(values_all, per_group)),
    )
    attended_low = ungroup_heads(attended, seq_count).astype(jnp.bfloat16)
    branch_part = jnp.einsum(
        "ste,ed->std", attended_low, full_out, preferred_element_type=jnp.float32
    )
    middle = inputs_f + lax.psum(branch_part, "tp")
    second_out, normed_two, inverse_two = scaled_norm(
        middle, gains_f[1], modulation[:, 2], modulation[:, 3]
    )
    second_low = second_out.astype(jnp.bfloat16)
    hidden = jnp.einsum("std,df->stf", second_low, full_up, preferred_element_type=jnp.float32)
    activated = jax.nn.gelu(hidden, approximate=False).astype(jnp.bfloat16)
    mlp_part = jnp.einsum("stf,fd->std", activated, full_down, preferred_element_type=jnp.float32)
    output = (middle + lax.psum(mlp_part, "tp")).astype(jnp.bfloat16)
    back_qkv, back_out, back_up, back_down = (
        lax.all_gather(qkv_weight, "shard", axis=1, tiled=True),
        lax.all_gather(out_weight, "shard", axis=1, tiled=True),
        lax.all_gather(up_weight, "shard", axis=0, tiled=True),
        lax.all_gather(down_weight, "shard", axis=1, tiled=True),
    )
    keys_back, values_back = (
        lax.all_gather(key_rot, "ctx", axis=1, tiled=True),
        lax.all_gather(value_low, "ctx", axis=1, tiled=True),
    )
    grad_down = jnp.einsum("stf,std->fd", activated, cotangent, preferred_element_type=jnp.float32)
    grad_act = jnp.einsum("std,fd->stf", cotangent, back_down, preferred_element_type=jnp.float32)
    grad_hidden = (grad_act * gelu_slope(hidden)).astype(jnp.bfloat16)
    grad_up = jnp.einsum("std,stf->df", second_low, grad_hidden, preferred_element_type=jnp.float32)
    grad_second = lax.psum(
        jnp.einsum("stf,df->std", grad_hidden, back_up, preferred_element_type=jnp.float32), "tp"
    )
    grad_mid_norm, gain_two, scaling_two, offset_two = norm_back(
        grad_second, normed_two, inverse_two, gains_f[1], modulation[:, 2]
    )
    grad_middle = cotangent.astype(jnp.float32) + grad_mid_norm
    grad_branch = grad_middle.astype(jnp.bfloat16)
    grad_out = jnp.einsum(
        "ste,std->ed", attended_low, grad_branch, preferred_element_type=jnp.float32
    )
    grad_attended = jnp.einsum(
        "std,ed->ste", grad_branch, back_out, preferred_element_type=jnp.float32
    ).astype(jnp.bfloat16)
    grad_query_g, grad_key_g, grad_value_g = lax.map(
        partial(attend_back, scaling=scaling),
        (
            query_groups,
            group_heads(keys_back, per_group),
            group_heads(values_back, per_group),
            group_heads(grad_attended, per_group),
            log_total,
        ),
    )
    grad_key_all = ungroup_heads(grad_key_g, seq_count)
    grad_value_all = ungroup_heads(grad_value_g, seq_count)
    grad_key, grad_value = (
        lax.psum_scatter(grad_key_all, "ctx", scatter_dimension=1, tiled=True),
        lax.psum_scatter(grad_value_all, "ctx", scatter_dimension=1, tiled=True),
    )
    grad_query = ungroup_heads(grad_query_g, seq_count)
    query_back = unrotate(grad_query.reshape(head_shape), cosines, sines).reshape(
        seq_count, tokens, local_width
    )
    key_back = unrotate(grad_key.reshape(head_shape), cosines, sines).reshape(
        seq_count, tokens, local_width
    )
    grad_projected = jnp.stack([query_back, key_back, grad_value], axis=0).astype(jnp.bfloat16)
    grad_qkv = jnp.einsum(
        "std,cste->cde", first_low, grad_projected, preferred_element_type=jnp.float32
    )
    grad_first = lax.psum(
        jnp.einsum("cste,cde->std", grad_projected, back_qkv, preferred_element_type=jnp.float32),
        "tp",
    )
    grad_in_norm, gain_one, scaling_one, offset_one = norm_back(
        grad_first, normed_one, inverse_one, gains_f[0], modulation[:, 0]
    )
    input_grad = (grad_middle + grad_in_norm).astype(jnp.bfloat16)
    grad_modulation = jnp.stack([scaling_one, offset_one, scaling_two, offset_two], axis=1)
    grad_time = jnp.einsum("sk,scd->kcd", embedding, grad_modulation, precision=highest)
    grad_gains = jnp.stack([gain_one, gain_two], axis=0)
    shares = (
        lax.psum_scatter(grad_qkv, "shard", scatter_dimension=1, tiled=True),
        lax.psum_scatter(grad_out, "shard", scatter_dimension=1, tiled=True),
        lax.psum_scatter(grad_up, "shard", scatter_dimension=0, tiled=True),
        lax.psum_scatter(grad_down, "shard", scatter_dimension=1, tiled=True),
        lax.psum_scatter(grad_time, "shard", scatter_dimension=2, tiled=True),
        lax.psum_scatter(grad_gains, "shard", scatter_dimension=1, tiled=True),
    )
    shares = lax.psum((shares[0], shares[1], shares[2], shares[3], shares[4], shares[5]), "ctx")
    return (output, input_grad, shares[0], shares[1], shares[2], shares[3], shares[4], shares[5])


BF = jnp.bfloat16
F32 = jnp.float32
NN = (((1,), (0,)), ((), ()))
NT = (((1,), (1,)), ((), ()))
TN = (((0,), (0,)), ((), ()))
VMEM_BIG = 56 << 20
PER_US = 0.8e9


def mm(a, b, dims=NN):
    return lax.dot_general(a, b, dims, preferred_element_type=F32)


def cost(flops, nbytes=0, trans=0):
    return pl.CostEstimate(flops=int(flops), bytes_accessed=int(nbytes), transcendentals=int(trans))


def whole(array):
    zeros = (0,) * array.ndim
    return pl.BlockSpec(array.shape, lambda *_: zeros)


def call(kernel, name, grid, scalars, ins, in_specs, outs, out_specs, est, scratch=()):
    return pl.pallas_call(
        kernel,
        out_shape=outs,
        grid_spec=pltpu.PrefetchScalarGridSpec(
            num_scalar_prefetch=len(scalars),
            grid=grid,
            in_specs=in_specs,
            out_specs=out_specs,
            scratch_shapes=list(scratch),
        ),
        compiler_params=pltpu.CompilerParams(vmem_limit_bytes=VMEM_BIG),
        cost_estimate=est,
        name=name,
    )(*scalars, *ins)


def shape(dims, dtype):
    return jax.ShapeDtypeStruct(dims, dtype)


def cols(index, width):
    return pl.ds(pl.multiple_of(index * width, width), width)


def half_turn(values):
    lane = lax.broadcasted_iota(jnp.int32, values.shape, 1) % HEAD_DIM
    width = values.shape[1]
    up = pltpu.roll(values, HEAD_DIM // 2, 1)
    down = pltpu.roll(values, width - HEAD_DIM // 2, 1)
    return jnp.where(lane < HEAD_DIM // 2, down, up)


def spin(cos_ref, sin_ref, width):
    cosines, sines = cos_ref[...].T, sin_ref[...].T
    heads = width // HEAD_DIM
    return jnp.concatenate([cosines, cosines] * heads, axis=1), jnp.concatenate([-sines, sines] * heads, axis=1)


def pick(step, first_ref, second_ref, per_half):
    return jnp.where(step < per_half, first_ref[...], second_ref[...])


def own_map(per_half):
    return lambda i, *_: (jnp.minimum(i, per_half - 1), 0)


def other_map(per_half):
    return lambda i, *_: (jnp.maximum(i - per_half, 0), 0)


def project_kernel(per_half, blk, xa, xb, w0, w1, w2, w3, mods, cosb, sinb, h_ref, q_ref, k_ref, kt_ref, v_ref, vt_ref):
    x = pick(pl.program_id(0), xa, xb, per_half).astype(F32)
    x = x - jnp.mean(x, axis=1, keepdims=True)
    var = jnp.mean(x * x, axis=1, keepdims=True)
    n = x * lax.rsqrt(var + norm_epsilon)
    h_ref[...] = (n * mods[0:1, :] + mods[1:2, :]).astype(BF)
    rows = w0.shape[0]
    acc = None
    for j, w in enumerate((w0, w1, w2, w3)):
        part = mm(h_ref[:, cols(blk[j], rows)], w[...])
        acc = part if acc is None else acc + part
    wide = acc.shape[1] // 3
    cosines, sines = spin(cosb, sinb, wide)
    q = acc[:, :wide]
    k = acc[:, wide : 2 * wide]
    v = acc[:, 2 * wide :]
    q = q * cosines + half_turn(q) * sines
    k = k * cosines + half_turn(k) * sines
    q_ref[...] = q.astype(BF)
    k_ref[...] = k.astype(BF)
    kt_ref[...] = k.T.astype(BF)
    v_ref[...] = v.astype(BF)
    vt_ref[...] = v.T.astype(BF)


def project(blk, xa, xb, ws, mods, cosb, sinb, tile=256):
    half, width = xa.shape
    total = 2 * half
    wide = ws[0].shape[1] // 3
    per_half = half // tile
    row = lambda w: pl.BlockSpec((tile, w), lambda i, *_: (i, 0))
    turned = pl.BlockSpec((wide, tile), lambda i, *_: (0, i))
    return call(
        partial(project_kernel, per_half), "project", (total // tile,), (blk,),
        (xa, xb, *ws, mods, cosb, sinb),
        [pl.BlockSpec((tile, width), own_map(per_half)), pl.BlockSpec((tile, width), other_map(per_half)),
         *[whole(w) for w in ws], whole(mods), *[pl.BlockSpec((v.shape[0], tile), lambda i, *_: (0, i)) for v in (cosb, sinb)]],
        [shape((total, width), BF), shape((total, wide), BF), shape((total, wide), BF), shape((wide, total), BF),
         shape((total, wide), BF), shape((wide, total), BF)],
        [row(width), row(wide), row(wide), turned, row(wide), turned],
        cost(12.5 * PER_US),
    )


def attend_kernel(scale, q_ref, k_ref, vt_ref, o_ref, ot_ref, lse_ref):
    rows, wide = q_ref.shape
    q = q_ref[...]
    lane = lax.broadcasted_iota(jnp.int32, (rows, wide), 1) // HEAD_DIM
    for h in range(wide // HEAD_DIM):
        at = slice(h * HEAD_DIM, (h + 1) * HEAD_DIM)
        qh = jnp.where(lane == h, q, jnp.zeros_like(q))
        s = mm(k_ref[...], qh, NT) * scale
        top = jnp.max(s, axis=0, keepdims=True)
        p = jnp.exp(s - top)
        total = jnp.sum(p, axis=0, keepdims=True)
        ot_ref[at, :] = mm(vt_ref[at, :], p.astype(BF)) / total
        lse_ref[h : h + 1, :] = top + jnp.log(total)
    o_ref[...] = ot_ref[...].T.astype(BF)


def attend(q, k, vt, first, rows, tile=512):
    total, wide = q.shape
    heads = wide // HEAD_DIM
    skip = first // tile
    return call(
        partial(attend_kernel, HEAD_DIM**-0.5), "attend", (rows // tile,), (), (q, k, vt),
        [pl.BlockSpec((tile, wide), lambda i: (i + skip, 0)), whole(k), whole(vt)],
        [shape((rows, wide), BF), shape((wide, rows), F32), shape((heads, rows), F32)],
        [pl.BlockSpec((tile, wide), lambda i: (i, 0)), pl.BlockSpec((wide, tile), lambda i: (0, i)),
         pl.BlockSpec((heads, tile), lambda i: (0, i))],
        cost(10.0 * PER_US),
    )


def join_kernel(n_t, blk, blo, x_ref, *refs):
    near, far = refs[:n_t], refs[n_t : 2 * n_t]
    mine = refs[2 * n_t : 6 * n_t]
    theirs, mods, x1_ref, h_ref = refs[6 * n_t :]
    own = jnp.concatenate([o[...] for o in near], axis=1)
    oth = jnp.concatenate([o[...] for o in far], axis=1)
    span = theirs.shape[1]
    deep = own.shape[1]
    for k in range(4):
        at = cols(blk[k], span)
        w = jnp.concatenate([mine[4 * j + k][...] for j in range(n_t)], axis=0)
        x1_ref[:, at] = x_ref[:, at].astype(F32) + mm(own, w)
    for k in range(4):
        at = cols(blo[k], span)
        x1_ref[:, at] += mm(oth, theirs[k * deep : (k + 1) * deep, :])
    x = x1_ref[...]
    x = x - jnp.mean(x, axis=1, keepdims=True)
    var = jnp.mean(x * x, axis=1, keepdims=True)
    n = x * lax.rsqrt(var + norm_epsilon)
    h_ref[...] = (n * mods[2:3, :] + mods[3:4, :]).astype(BF)


def part_of(array, index, rows):
    return pl.BlockSpec((rows, array.shape[1]), lambda *_: (index, 0))


def stack_kernel(*refs):
    rows = refs[0].shape[0]
    for i, ref in enumerate(refs[:-1]):
        refs[-1][i * rows : (i + 1) * rows, :] = ref[...]


def stack_parts(arrays, rows):
    width = arrays[0].shape[1]
    return call(
        stack_kernel, "stack_parts", (1,), (), arrays,
        [part_of(v, v.shape[0] // rows - 1, rows) for v in arrays],
        shape((len(arrays) * rows, width), BF), pl.BlockSpec((len(arrays) * rows, width), lambda i: (0, 0)),
        cost(2.3 * PER_US),
    )


def join(blk, blo, x, near, far, slots, theirs, mods, tile=256):
    half, width = x.shape
    n_t = len(slots)
    wide = near[0].shape[1]
    row = lambda w: pl.BlockSpec((tile, w), lambda i, *_: (i, 0))
    flat = [w for slot in slots for w in slot]
    last_part = flat[0].shape[0] // wide - 1
    return call(
        partial(join_kernel, n_t), "join", (half // tile,), (blk, blo), (x, *near, *far, *flat, theirs, mods),
        [row(width), *[row(wide)] * (2 * n_t), *[part_of(w, last_part, wide) for w in flat], whole(theirs), whole(mods)],
        [shape((half, width), F32), shape((half, width), BF)],
        [row(width), row(width)],
        cost(8.5 * PER_US),
    )


def gelu_parts(u):
    half = 0.5 * (1.0 + lax.erf(u * 0.7071067811865476))
    slope = half + u * jnp.exp(-0.5 * u * u) * 0.3989422804014327
    return u * half, slope


def mlp_kernel(per_half, n_slots, has_base, keep_du, blk, *refs):
    ha, hb, ca, cb = refs[:4]
    ws = [refs[4 + 4 * i : 8 + 4 * i] for i in range(n_slots)]
    at = 4 + 4 * n_slots
    base = refs[at] if has_base else None
    at += has_base
    dh_ref = refs[at]
    g_ref = refs[at + 1]
    du_ref = refs[at + 2] if keep_du else None
    h_buf, c_buf = refs[at + 2 + keep_du :]
    step = pl.program_id(0)
    h_buf[...] = pick(step, ha, hb, per_half)
    c_buf[...] = pick(step, ca, cb, per_half)
    span = ws[0][0].shape[1]
    for i, slot in enumerate(ws):
        for b in range(2):
            up = slice(b * span, (b + 1) * span)
            down = slice((2 + b) * span, (3 + b) * span)
            u = dg = None
            for j, w in enumerate(slot):
                here = cols(blk[j], span)
                part = mm(h_buf[:, here], w[up, :])
                u = part if u is None else u + part
                part = mm(c_buf[:, here], w[down, :], NT)
                dg = part if dg is None else dg + part
            g, slope = gelu_parts(u)
            du = (dg * slope).astype(BF)
            g_ref[:, (2 * i + b) * span : (2 * i + b + 1) * span] = g.astype(BF)
            if keep_du and i == 0:
                du_ref[:, up] = du
            for j, w in enumerate(slot):
                here = cols(blk[j], span)
                part = mm(du, w[up, :], NT)
                if i == 0 and b == 0:
                    dh_ref[:, here] = base[:, here] + part if has_base else part
                else:
                    dh_ref[:, here] += part


def mlp(blk, ha, hb, ca, cb, slots, base, keep_du, tile=256):
    half, width = ha.shape
    total = 2 * half
    per_half = half // tile
    n_slots = len(slots)
    hidden = 2 * slots[0][0].shape[1]
    row = lambda w: pl.BlockSpec((tile, w), lambda i, *_: (i, 0))
    mine = pl.BlockSpec((tile, width), own_map(per_half))
    theirs = pl.BlockSpec((tile, width), other_map(per_half))
    flat = [w for slot in slots for w in slot]
    ins = [ha, hb, ca, cb, *flat]
    specs = [mine, theirs, mine, theirs, *[part_of(w, 0, 4 * w.shape[1]) for w in flat]]
    if base is not None:
        ins.append(base)
        specs.append(row(width))
    outs = [shape((total, width), F32), shape((total, n_slots * hidden), BF)]
    out_specs = [row(width), row(n_slots * hidden)]
    if keep_du:
        outs.append(shape((total, hidden), BF))
        out_specs.append(row(hidden))
    return call(
        partial(mlp_kernel, per_half, n_slots, int(base is not None), int(keep_du)),
        "mlp", (total // tile,), (blk,), ins, specs, outs, out_specs,
        cost(48.0 * PER_US),
        [pltpu.VMEM((tile, width), BF), pltpu.VMEM((tile, width), BF)],
    )


def lift_kernel(groups, per_half, blk, *refs):
    n = sum(groups)
    gs = refs[: len(groups)]
    ws = [refs[len(groups) + 4 * i : len(groups) + 4 * i + 4] for i in range(n)]
    own_ref, oth_ref, buf = refs[len(groups) + 4 * n :]
    span = ws[0][0].shape[1]
    for j in range(4):
        here = cols(blk[j], span)
        acc = None
        i = 0
        for g, count in zip(gs, groups):
            for k in range(count):
                for b in range(2):
                    part = mm(g[:, (2 * k + b) * span : (2 * k + b + 1) * span], ws[i][j][b * span : (b + 1) * span, :])
                    acc = part if acc is None else acc + part
                i += 1
        buf[:, here] = acc
    step = pl.program_id(0)

    @pl.when(step < per_half)
    def _():
        own_ref[...] = buf[...]

    @pl.when(step >= per_half)
    def _():
        oth_ref[...] = buf[...].astype(BF)


def lift(blk, gs, groups, slots, width, tile=256):
    total = gs[0].shape[0]
    half = total // 2
    per_half = half // tile
    flat = [w for slot in slots for w in slot]
    return call(
        partial(lift_kernel, groups, per_half), "lift", (total // tile,), (blk,), (*gs, *flat),
        [*[pl.BlockSpec((tile, g.shape[1]), lambda i, *_: (i, 0)) for g in gs], *[part_of(w, 1, 2 * w.shape[1]) for w in flat]],
        [shape((half, width), F32), shape((half, width), BF)],
        [pl.BlockSpec((tile, width), own_map(per_half)), pl.BlockSpec((tile, width), other_map(per_half))],
        cost(16.0 * PER_US),
        [pltpu.VMEM((tile, width), F32)],
    )


def norm_turn(dh, x, factor):
    x = x - jnp.mean(x, axis=1, keepdims=True)
    var = jnp.mean(x * x, axis=1, keepdims=True)
    r = lax.rsqrt(var + norm_epsilon)
    n = x * r
    dn = dh * factor
    dx = r * (dn - jnp.mean(dn, axis=1, keepdims=True) - n * jnp.mean(dn * n, axis=1, keepdims=True))
    return dx, jnp.sum(dh * n, axis=0, keepdims=True), jnp.sum(dh, axis=0, keepdims=True)


def turn_kernel(blk, blo, dh_ref, in_ref, x_ref, c_ref, mods, a0, a1, a2, a3, b_ref, dx_ref, da_ref, own_ref, oth_ref, sums):
    dh = dh_ref[...] + in_ref[...].astype(F32)
    dx, s1, s0 = norm_turn(dh, x_ref[...], mods[2:3, :])
    dx = dx + c_ref[...].astype(F32)
    dx_ref[...] = dx
    da_ref[...] = dx.astype(BF)
    wide = own_ref.shape[1]
    span = a0.shape[1]
    step = b_ref.shape[0] // 4
    theirs = [b_ref[k * step : k * step + wide, :] for k in range(4)]
    for order, ws, out in ((blk, [a[...] for a in (a0, a1, a2, a3)], own_ref), (blo, theirs, oth_ref)):
        acc = None
        for j, w in enumerate(ws):
            part = mm(da_ref[:, cols(order[j], span)], w, NT)
            acc = part if acc is None else acc + part
        out[...] = acc.astype(BF)

    @pl.when(pl.program_id(0) == 0)
    def _():
        sums[...] = jnp.zeros_like(sums)

    sums[0:1, :] += s1
    sums[1:2, :] += s0


def turn(blk, blo, dh, received, x1, cot, mods, wa, wb, wide, tile=256):
    half, width = x1.shape
    row = lambda w: pl.BlockSpec((tile, w), lambda i, *_: (i, 0))
    return call(
        turn_kernel, "turn", (half // tile,), (blk, blo), (dh, received, x1, cot, mods, *wa, wb),
        [row(width)] * 4 + [whole(mods), *[part_of(w, w.shape[0] // wide - 1, wide) for w in wa], whole(wb)],
        [shape((half, width), F32), shape((half, width), BF), shape((half, wide), BF), shape((half, wide), BF), shape((8, width), F32)],
        [row(width), row(width), row(wide), row(wide), pl.BlockSpec((8, width), lambda i, *_: (0, 0))],
        cost(11.3 * PER_US),
    )


def attend_back_kernel(scale, tk, per_half, q_ref, da_ref, db_ref, ota_ref, otb_ref, la_ref, lb_ref, cos_ref, sin_ref, k_ref, v_ref, kt_ref, cosb, sinb, dq_ref, dk_ref, dv_ref, dqt, dk_acc, dv_acc):
    rows, wide = q_ref.shape
    total = k_ref.shape[0]
    step = pl.program_id(0)
    q = q_ref[...]
    do = pick(step, da_ref, db_ref, per_half)
    lse = pick(step, la_ref, lb_ref, per_half)
    lane = lax.broadcasted_iota(jnp.int32, (rows, wide), 1) // HEAD_DIM
    heads = wide // HEAD_DIM
    qs = [jnp.where(lane == h, q, jnp.zeros_like(q)) for h in range(heads)]
    ds = [jnp.where(lane == h, do, jnp.zeros_like(do)) for h in range(heads)]
    od = do.astype(F32).T * pick(step, ota_ref, otb_ref, per_half)
    deltas = [jnp.sum(od[h * HEAD_DIM : (h + 1) * HEAD_DIM, :], axis=0, keepdims=True) for h in range(heads)]

    @pl.when(step == 0)
    def _():
        dk_acc[...] = jnp.zeros_like(dk_acc)
        dv_acc[...] = jnp.zeros_like(dv_acc)

    dqt[...] = jnp.zeros_like(dqt)
    for j in range(total // tk):
        at = slice(j * tk, (j + 1) * tk)
        kj, vj = k_ref[at, :], v_ref[at, :]
        for h in range(heads):
            hs = slice(h * HEAD_DIM, (h + 1) * HEAD_DIM)
            s = mm(kj, qs[h], NT) * scale
            p = jnp.exp(s - lse[h : h + 1, :])
            dp = mm(vj, ds[h], NT)
            dsc = (p * (dp - deltas[h])).astype(BF)
            dv_acc[at, :] += mm(p.astype(BF), ds[h])
            dk_acc[at, :] += mm(dsc, qs[h])
            dqt[hs, :] += mm(kt_ref[hs, at], dsc)
    dq = dqt[...].T * scale
    cosines, sines = spin(cos_ref, sin_ref, wide)
    dq_ref[...] = (dq * cosines - half_turn(dq) * sines).astype(BF)

    @pl.when(step == pl.num_programs(0) - 1)
    def _():
        dk = dk_acc[...] * scale
        cosines, sines = spin(cosb, sinb, wide)
        dk_ref[...] = (dk * cosines - half_turn(dk) * sines).astype(BF)
        dv_ref[...] = dv_acc[...].astype(BF)


def attend_back_call(q, do_a, do_b, ots, lses, k, v, kt, cosb, sinb, tile=512, tk=512):
    total, wide = q.shape
    heads = wide // HEAD_DIM
    per_half = total // 2 // tile
    row = pl.BlockSpec((tile, wide), lambda i: (i, 0))
    lanes_a = lambda h: pl.BlockSpec((h, tile), lambda i: (0, jnp.minimum(i, per_half - 1)))
    lanes_b = lambda h: pl.BlockSpec((h, tile), lambda i: (0, jnp.maximum(i - per_half, 0)))
    full = pl.BlockSpec((total, wide), lambda i: (0, 0))
    turned = pl.BlockSpec((cosb.shape[0], tile), lambda i: (0, i))
    return call(
        partial(attend_back_kernel, HEAD_DIM**-0.5, tk, per_half), "attend_back", (total // tile,), (),
        (q, do_a, do_b, *ots, *lses, cosb, sinb, k, v, kt, cosb, sinb),
        [row, pl.BlockSpec((tile, wide), own_map(per_half)), pl.BlockSpec((tile, wide), other_map(per_half)),
         lanes_a(wide), lanes_b(wide), lanes_a(heads), lanes_b(heads), turned, turned, full, full, whole(kt), whole(cosb), whole(sinb)],
        [shape((total, wide), BF)] * 3,
        [row, full, full],
        cost(29.0 * PER_US),
        [pltpu.VMEM((wide, tile), F32), pltpu.VMEM((total, wide), F32), pltpu.VMEM((total, wide), F32)],
    )


def gather_kernel(blk, *refs):
    n = (len(refs) - 2) // 5
    rs = refs[:n]
    ws = [refs[n + 4 * i : n + 4 * i + 4] for i in range(n)]
    own_ref, oth_ref = refs[5 * n :]
    rows = own_ref.shape[0]
    span = ws[0][0].shape[0]
    for j in range(4):
        acc = None
        for r, w in zip(rs, ws):
            part = mm(r[...], w[j][...], NT)
            acc = part if acc is None else acc + part
        own_ref[:, cols(blk[j], span)] = acc[:rows]
        oth_ref[:, cols(blk[j], span)] = acc[rows:].astype(BF)


def gather(blk, rs, slots, width):
    rows = rs[0].shape[0] // 2
    flat = [w for slot in slots for w in slot]
    back = pl.BlockSpec((rows, width), lambda i, *_: (0, 0))
    return call(
        gather_kernel, "gather", (1,), (blk,), (*rs, *flat),
        [*[whole(r) for r in rs], *[whole(w) for w in flat]],
        [shape((rows, width), F32), shape((rows, width), BF)],
        [back, back],
        cost(6.5 * PER_US),
    )


def last_kernel(dh_ref, in_ref, x_ref, dx_ref, mods, out_ref, sums):
    dx, s1, s0 = norm_turn(dh_ref[...] + in_ref[...].astype(F32), x_ref[...].astype(F32), mods[0:1, :])
    out_ref[...] = (dx + dx_ref[...]).astype(BF)
    sums[...] = jnp.zeros_like(sums)
    sums[0:1, :] = s1
    sums[1:2, :] = s0


def last(dh, received, x, dx, mods):
    rows, width = dh.shape
    return call(
        last_kernel, "last", (1,), (), (dh, received, x, dx, mods),
        [whole(v) for v in (dh, received, x, dx, mods)],
        [shape((rows, width), BF), shape((8, width), F32)],
        [pl.BlockSpec((rows, width), lambda i: (0, 0)), pl.BlockSpec((8, width), lambda i: (0, 0))],
        cost(3.5 * PER_US),
    )


def after(values, *events):
    return lax.optimization_barrier((values, events))[0]


def fast_body(
    activations, timestep, positions, qkv_weight, out_weight, up_weight, down_weight, time_weight, norm_gains, cotangent
):
    n_s, n_t = lax.axis_size("shard"), lax.axis_size("tp")
    s, c, t = lax.axis_index("shard"), lax.axis_index("ctx"), lax.axis_index("tp")
    x_own = activations[0]
    cot_own = cotangent[0]
    half, width = x_own.shape
    span = width // n_s
    quarter = half // n_t
    near = jnp.where(c == 0, 1, 2)
    blk = jnp.stack([s, s ^ near, s ^ (3 - near), s ^ 3]).astype(jnp.int32)
    blo = jnp.stack([s, s ^ (3 - near), s ^ near, s ^ 3]).astype(jnp.int32)
    pairs_a = [(v * 2 + k, (v ^ (1 + k)) * 2 + k) for v in range(n_s) for k in range(2)]
    pairs_b = [(v * 2 + k, (v ^ (2 - k)) * 2 + k) for v in range(n_s) for k in range(2)]
    cycle = [(i, (i + 1) % n_t) for i in range(n_t)]
    swap = lambda v: lax.ppermute(v, "ctx", [(0, 1), (1, 0)])
    move_a = lambda v: lax.ppermute(v, ("shard", "ctx"), pairs_a)
    move_b = lambda v: lax.ppermute(v, ("shard", "ctx"), pairs_b)
    upward = lambda v: lax.ppermute(v, "tp", cycle)

    def by_z(v, d):
        return lax.ppermute(v, "tp", [(i, (i + d) % n_t) for i in range(n_t)])

    def turn_shard(v, d):
        return lax.ppermute(v, "shard", [(i, (i + d) % n_s) for i in range(n_s)])

    def half_of(v, axis):
        size = v.shape[axis] // 2
        return lax.dynamic_slice_in_dim(v, c * size, size, axis)

    def both(v, axis):
        other = swap(v)
        return jnp.where(c == 0, jnp.concatenate([v, other], axis), jnp.concatenate([other, v], axis))

    gains = norm_gains.astype(F32)
    small = jnp.concatenate([gains, jnp.broadcast_to(timestep.astype(F32)[:, None], (1, span))], axis=0)
    smalls = [small] + [turn_shard(small, d) for d in range(1, n_s)]

    wide = qkv_weight.shape[2] // 2
    qkv_half = half_of(qkv_weight, 2)
    qkv_share = jnp.concatenate([qkv_half[0], qkv_half[1], qkv_half[2]], axis=1)
    qkv_a, qkv_b = move_a(qkv_share), move_b(qkv_share)
    qkv_c = move_b(qkv_a)
    w_qkv = [qkv_share, qkv_a, qkv_b, qkv_c]
    x_oth = swap(x_own)
    pos_own = positions.astype(F32)
    pos_oth = swap(pos_own)

    up_half = half_of(up_weight, 1)
    down_half = half_of(down_weight, 0)
    pack = jnp.concatenate([up_half[:, :span], up_half[:, span:], down_half, half_of(out_weight, 0)], axis=0)
    pack = after(pack, qkv_a, qkv_b)
    z1 = upward(pack)
    m0a, m0b = move_a(pack), move_b(pack)

    steps = jnp.stack([v[2, 0] for v in smalls])
    embedding = embed_time(steps)
    parts = jnp.einsum("sk,kcd->scd", embedding, time_weight.astype(F32), precision=highest)
    gain_full = jnp.zeros((2, width), F32)
    mod_full = jnp.zeros((4, width), F32)
    for d in range(n_s):
        from_s = (s - d) % n_s
        gain_full = lax.dynamic_update_slice_in_dim(gain_full, smalls[d][:2], from_s * span, 1)
        got = parts[0] if d == 0 else turn_shard(parts[d], n_s - d)
        mod_full = lax.dynamic_update_slice_in_dim(mod_full, got, ((s + d) % n_s) * span, 1)
    factor_one = gain_full[0] * (1.0 + mod_full[0])
    factor_two = gain_full[1] * (1.0 + mod_full[2])
    zero = jnp.zeros_like(factor_one)
    mods = jnp.stack([factor_one, mod_full[1], factor_two, mod_full[3], zero, zero, zero, zero])

    half_width = HEAD_DIM // 2
    frequency = jnp.exp(-math.log(10000.0) * jnp.arange(half_width, dtype=F32) / half_width)
    angles = frequency[:, None] * jnp.concatenate([pos_own, pos_oth], axis=1)
    cosb, sinb = jnp.cos(angles), jnp.sin(angles)

    z1 = after(z1, mods)
    z2 = upward(z1)
    m1a, m1b = move_a(z1), move_b(z1)
    x_now = after(x_own, z1, m0a, m0b)
    h1, q, k, kt, v, vt = project(blk, x_now, x_oth, w_qkv, mods, cosb, sinb)
    m0c, m1c, z3 = move_b(after(m0a, q)), move_b(after(m1a, q, m1b)), upward(after(z2, q))
    o_far, ot_far, lse_far = attend(q, k, vt, half, half)
    o_got = swap(o_far)
    z2_late = after(z2, o_far, m0c, m1c)
    m2a, m2b = move_a(z2_late), move_b(z2_late)
    far = [after(o_got, z3)]
    far.append(upward(far[0]))
    o_near, ot_near, lse_near = attend(after(q, o_far), k, vt, 0, half)
    z3_late, m2a_late, near_go = after((z3, m2a, o_near), m2b, far[1])
    m3a, m3b, m2c = move_a(z3_late), move_b(z3_late), move_b(m2a_late)
    near = [near_go, upward(near_go)]
    far.append(upward(after(far[1], near_go)))
    m3a_late = after(m3a, m3b, m2c, near[1], far[2])
    m3c = move_b(m3a_late)
    near.append(upward(after(near[1], m3b)))
    far.append(upward(after(far[2], m3b)))
    near.append(upward(after(near[2], m3c)))
    cot_oth = swap(cot_own)
    w_mlp = [[pack, m0a, m0b, m0c], [z1, m1a, m1b, m1c], [z2, m2a, m2b, m2c], [z3, m3a, m3b, m3c]]
    out_other = swap(stack_parts([w_mlp[j][i] for i in range(n_s) for j in range(n_t)], wide))

    x1, h2 = join(blk, blo, x_own, near, far, w_mlp, out_other, mods)
    h2_oth = swap(h2)
    groups = (n_t,)
    dh2, g_all, du0 = mlp(blk, h2, h2_oth, cot_own, cot_oth, w_mlp, None, True)
    gs = [g_all]
    qkv_again = after(qkv_share, h2_oth)
    qz_pack = jnp.concatenate([by_z(qkv_again, d) for d in range(1, n_t)], axis=0)
    dh2_in = swap(after(dh2[half:].astype(BF), qz_pack))
    qz_pack = after(qz_pack, dh2_in)
    qza, qzb = move_a(qz_pack), move_b(qz_pack)
    dx1, da, do_own, do_send, sums_two = turn(blk, blo, dh2, dh2_in, x1, cot_own, mods, w_mlp[0], out_other, wide)
    do_got = swap(do_send)
    qza, qzb, do_got = after((qza, qzb, do_got), da)
    qzc = move_b(qza)
    w_back = [w_qkv] + [[v[i * span : (i + 1) * span] for v in (qz_pack, qza, qzb, qzc)] for i in range(n_t - 1)]
    dq, dk, dv = attend_back_call(q, do_own, do_got, (ot_near, ot_far), (lse_near, lse_far), k, v, kt, cosb, sinb)

    dqkv = jnp.concatenate([dq, dk, dv], axis=1).reshape(2, half, 3 * wide)

    def tokens_of(d):
        return lax.dynamic_slice_in_dim(dqkv, ((t + d) % n_t) * quarter, quarter, 1).reshape(2 * quarter, 3 * wide)

    got = [tokens_of(0), by_z(tokens_of(1), 1)]

    h2_late, h2o_late, du0_late, g_late = after((h2, h2_oth, du0, gs[0]), tokens_of(1))
    g_up = mm(jnp.concatenate([h2_late, h2o_late], axis=0), du0_late, TN)
    g_down = mm(g_late[:, : 2 * span], jnp.concatenate([cot_own, cot_oth], axis=0), TN)
    got.append(by_z(after(tokens_of(2), got[1], g_up, g_down), 2))
    g_later = after(g_late, got[1], g_up, g_down)
    y_own, y_send = lift(blk, [g_later], groups, w_mlp, width)
    got[2], y_own, y_send, da_late, g_up, g_down = after((got[2], y_own, y_send, da, g_up, g_down), got[2])
    got.append(by_z(after(tokens_of(3), got[2], y_own), 3))
    g_out = mm(o_near, da_late, TN) + swap(mm(o_got, da_late, TN).astype(BF)).astype(F32)

    def mlp_piece(j):
        ups = lax.dynamic_slice_in_dim(g_up, blk[j] * span, span, 0)
        downs = lax.dynamic_slice_in_dim(g_down, blk[j] * span, span, 1)
        outs = lax.dynamic_slice_in_dim(g_out, blk[j] * span, span, 1)
        return jnp.concatenate([ups[:, :span], ups[:, span:], downs, outs], axis=0)

    def reduce_first(pieces):
        return move_b(jnp.concatenate([pieces(2), pieces(3)], axis=0).astype(BF))

    def reduce_last(pieces, came):
        rows = came.shape[0] // 2
        return pieces(0) + came[:rows].astype(F32) + move_a((pieces(1) + came[rows:].astype(F32)).astype(BF)).astype(F32)

    mlp_came = reduce_first(mlp_piece)
    output = (x1 + y_own + swap(y_send).astype(F32)).astype(BF)

    dh1_own, dh1_send = gather(blk, after(got, output, mlp_came), w_back, width)
    dh1_got = swap(dh1_send)

    def token_block(v):
        return lax.dynamic_slice_in_dim(v, t * quarter, quarter, 0)

    grad_mine, sums_one = last(dh1_own, dh1_got, token_block(x_own), token_block(dx1), mods)
    slots = [grad_mine, upward(grad_mine)]
    h1_late, dqkv_late, mlp_late = after((h1, dqkv, mlp_came), grad_mine)
    g_qkv = mm(h1_late, dqkv_late.reshape(2 * half, 3 * wide), TN)
    qkv_piece = lambda j: lax.dynamic_slice_in_dim(g_qkv, blk[j] * span, span, 0)
    qkv_came = reduce_first(qkv_piece)
    rows = mlp_late.shape[0] // 2
    mlp_base = mlp_piece(0) + mlp_late[:rows].astype(F32)
    mlp_last = move_a((mlp_piece(1) + mlp_late[rows:].astype(F32)).astype(BF))
    keep = jnp.where(t == 0, 1.0, 0.0)
    tally = jnp.concatenate([sums_one[:2], sums_two[:2] * keep], axis=0)
    tally = tally + swap(tally)

    slots[1], mlp_last, tally = after((slots[1], mlp_last, tally), mlp_base, g_qkv)
    slots.append(upward(slots[1]))
    done = mlp_base + mlp_last.astype(F32)
    grad_up = both(jnp.concatenate([done[:span], done[span : 2 * span]], axis=1), 1)
    grad_down = both(done[2 * span : 4 * span], 0)
    grad_out = both(done[4 * span :], 0)
    qkv_came = after(qkv_came, slots[1])
    rows = qkv_came.shape[0] // 2
    qkv_base = qkv_piece(0) + qkv_came[:rows].astype(F32)
    qkv_last = move_a((qkv_piece(1) + qkv_came[rows:].astype(F32)).astype(BF))
    full = tally
    for d in range(1, n_t):
        full = full + by_z(tally, d)

    slots[2], qkv_last, full = after((slots[2], qkv_last, full), grad_up, grad_down, grad_out, qkv_base)
    slots.append(upward(slots[2]))
    done_qkv = qkv_base + qkv_last.astype(F32)
    grad_qkv = both(jnp.stack([done_qkv[:, i * wide : (i + 1) * wide] for i in range(3)]), 2)
    dmods = jnp.stack([full[0] * gain_full[0], full[1], full[2] * gain_full[1], full[3],
                       full[0] * (1.0 + mod_full[0]), full[2] * (1.0 + mod_full[2])])
    per_seq = []
    for d in range(n_s):
        block = lax.dynamic_slice_in_dim(dmods, ((s + d) % n_s) * span, span, 1)
        per_seq.append(block if d == 0 else turn_shard(block, d))
    seqs = jnp.stack(per_seq)
    grad_time = jnp.einsum("sk,scd->kcd", embedding, seqs[:, :4], precision=highest)
    grad_gains = jnp.sum(seqs[:, 4:], axis=0)
    slots[3] = after(slots[3], grad_qkv, grad_time, grad_gains)
    input_grad = jnp.zeros((half, width), BF)
    for j in range(n_t):
        input_grad = lax.dynamic_update_slice_in_dim(input_grad, slots[j], ((t - j) % n_t) * quarter, 0)
    return (output[None], input_grad[None], grad_qkv, grad_out, grad_up, grad_down, grad_time, grad_gains)


def solution(mesh):
    sizes = dict(mesh.shape)
    chosen = fast_body if (sizes["shard"], sizes["ctx"], sizes["tp"]) == (4, 2, 4) else body
    placed = (
        P("shard", "ctx", None),
        P("shard"),
        P("shard", "ctx"),
        P(None, "shard", "tp"),
        P("tp", "shard"),
        P("shard", "tp"),
        P("tp", "shard"),
        P(None, None, "shard"),
        P(None, "shard"),
        P("shard", "ctx", None),
    )
    return jax.shard_map(
        chosen,
        mesh=mesh,
        in_specs=placed,
        out_specs=(
            P("shard", "ctx", None),
            P("shard", "ctx", None),
            P(None, "shard", "tp"),
            P("tp", "shard"),
            P("shard", "tp"),
            P("tp", "shard"),
            P(None, None, "shard"),
            P(None, "shard"),
        ),
        check_vma=False,
    )
```

```python
from functools import partial
import math

import jax
import jax.numpy as jnp
from jax import lax
from jax.experimental import pallas as pl
from jax.experimental.pallas import tpu as pltpu
from jax.sharding import PartitionSpec as P

HEAD_DIM = 64
TEMB = 256


highest = lax.Precision.HIGHEST
norm_epsilon = 1e-05


def embed_time(timestep):
    half_width = TEMB // 2
    frequency = jnp.exp(-math.log(10000.0) * jnp.arange(half_width, dtype=jnp.float32) / half_width)
    angles = timestep.astype(jnp.float32)[:, None] * frequency[None, :]
    return jnp.concatenate([jnp.sin(angles), jnp.cos(angles)], axis=-1)


def rotary_tables(positions):
    half_width = HEAD_DIM // 2
    frequency = jnp.exp(-math.log(10000.0) * jnp.arange(half_width, dtype=jnp.float32) / half_width)
    angles = positions.astype(jnp.float32)[..., None] * frequency
    return (jnp.cos(angles), jnp.sin(angles))


def rotate(heads_in, cosines, sines):
    half_width = HEAD_DIM // 2
    first = heads_in[..., :half_width]
    second = heads_in[..., half_width:]
    cos_wide = cosines[..., None, :]
    sin_wide = sines[..., None, :]
    return jnp.concatenate(
        [first * cos_wide - second * sin_wide, second * cos_wide + first * sin_wide], axis=-1
    )


def unrotate(heads_in, cosines, sines):
    half_width = HEAD_DIM // 2
    first = heads_in[..., :half_width]
    second = heads_in[..., half_width:]
    cos_wide = cosines[..., None, :]
    sin_wide = sines[..., None, :]
    return jnp.concatenate(
        [first * cos_wide + second * sin_wide, second * cos_wide - first * sin_wide], axis=-1
    )


def scaled_norm(values, gain_vec, scaling, offset):
    centered = values - jnp.mean(values, axis=-1, keepdims=True)
    variance = jnp.mean(centered * centered, axis=-1, keepdims=True)
    inverse_std = lax.rsqrt(variance + norm_epsilon)
    normed = centered * inverse_std
    return (
        normed * gain_vec * (1.0 + scaling[:, None, :]) + offset[:, None, :],
        normed,
        inverse_std,
    )


def norm_back(grad_in, normed, inverse_std, gain_vec, scaling):
    factor = gain_vec * (1.0 + scaling[:, None, :])
    grad_normed = grad_in * factor
    grad_values = inverse_std * (
        grad_normed
        - jnp.mean(grad_normed, axis=-1, keepdims=True)
        - normed * jnp.mean(grad_normed * normed, axis=-1, keepdims=True)
    )
    grad_gain = jnp.sum(grad_in * normed * (1.0 + scaling[:, None, :]), axis=(0, 1))
    grad_scaling = jnp.sum(grad_in * normed * gain_vec, axis=1)
    grad_offset = jnp.sum(grad_in, axis=1)
    return (grad_values, grad_gain, grad_scaling, grad_offset)


def group_heads(field, per_group):
    seq_count, rows_count, _ = field.shape
    split = field.reshape(seq_count, rows_count, -1, HEAD_DIM).transpose(0, 2, 1, 3)
    return split.reshape(-1, per_group, rows_count, HEAD_DIM)


def ungroup_heads(field, seq_count):
    rows_count = field.shape[2]
    joined = field.reshape(seq_count, -1, rows_count, HEAD_DIM).transpose(0, 2, 1, 3)
    return joined.reshape(seq_count, rows_count, -1)


def attend_block(triple, scaling):
    queries, keys, values = triple
    scores = jnp.einsum("gqd,gkd->gqk", queries, keys, preferred_element_type=jnp.float32) * scaling
    top_score = jnp.max(scores, axis=-1, keepdims=True)
    raised = jnp.exp(scores - top_score)
    total = jnp.sum(raised, axis=-1, keepdims=True)
    weights = (raised / total).astype(jnp.bfloat16)
    attended = jnp.einsum("gqk,gkd->gqd", weights, values, preferred_element_type=jnp.float32)
    return (attended, (top_score + jnp.log(total))[..., 0])


def attend_back(bundle, scaling):
    queries, keys, values, grad_out, log_total = bundle
    scores = jnp.einsum("gqd,gkd->gqk", queries, keys, preferred_element_type=jnp.float32) * scaling
    weights = jnp.exp(scores - log_total[..., None])
    grad_values = jnp.einsum(
        "gqk,gqd->gkd", weights.astype(jnp.bfloat16), grad_out, preferred_element_type=jnp.float32
    )
    grad_weights = jnp.einsum("gqd,gkd->gqk", grad_out, values, preferred_element_type=jnp.float32)
    row_term = jnp.sum(weights * grad_weights, axis=-1, keepdims=True)
    grad_scores = (weights * (grad_weights - row_term)).astype(jnp.bfloat16)
    grad_queries = (
        jnp.einsum("gqk,gkd->gqd", grad_scores, keys, preferred_element_type=jnp.float32) * scaling
    )
    grad_keys = (
        jnp.einsum("gqk,gqd->gkd", grad_scores, queries, preferred_element_type=jnp.float32)
        * scaling
    )
    return (grad_queries, grad_keys, grad_values)


def gelu_slope(hidden):
    return (
        0.5 * (1.0 + lax.erf(hidden * 0.7071067811865476))
        + hidden * jnp.exp(-0.5 * hidden * hidden) * 0.3989422804014327
    )


def body(
    activations,
    timestep,
    positions,
    qkv_weight,
    out_weight,
    up_weight,
    down_weight,
    time_weight,
    norm_gains,
    cotangent,
):
    seq_count, tokens, width = activations.shape
    local_width = qkv_weight.shape[2]
    heads_local = local_width // HEAD_DIM
    per_group = min(heads_local, max(1, 512 // tokens))
    while heads_local % per_group:
        per_group -= 1
    scaling = HEAD_DIM ** (-0.5)
    full_qkv, full_out, full_up, full_down, full_time, full_gains = (
        lax.all_gather(qkv_weight, "shard", axis=1, tiled=True),
        lax.all_gather(out_weight, "shard", axis=1, tiled=True),
        lax.all_gather(up_weight, "shard", axis=0, tiled=True),
        lax.all_gather(down_weight, "shard", axis=1, tiled=True),
        lax.all_gather(time_weight, "shard", axis=2, tiled=True),
        lax.all_gather(norm_gains, "shard", axis=1, tiled=True),
    )
    gains_f = full_gains.astype(jnp.float32)
    embedding = embed_time(timestep)
    modulation = jnp.einsum(
        "sk,kcd->scd", embedding, full_time.astype(jnp.float32), precision=highest
    )
    cosines, sines = rotary_tables(positions)
    inputs_f = activations.astype(jnp.float32)
    first_out, normed_one, inverse_one = scaled_norm(
        inputs_f, gains_f[0], modulation[:, 0], modulation[:, 1]
    )
    first_low = first_out.astype(jnp.bfloat16)
    projected = jnp.einsum("std,cde->cste", first_low, full_qkv, preferred_element_type=jnp.float32)
    head_shape = (seq_count, tokens, heads_local, HEAD_DIM)
    query_rot = (
        rotate(projected[0].reshape(head_shape), cosines, sines)
        .reshape(seq_count, tokens, local_width)
        .astype(jnp.bfloat16)
    )
    key_rot = (
        rotate(projected[1].reshape(head_shape), cosines, sines)
        .reshape(seq_count, tokens, local_width)
        .astype(jnp.bfloat16)
    )
    value_low = projected[2].astype(jnp.bfloat16)
    keys_all, values_all = (
        lax.all_gather(key_rot, "ctx", axis=1, tiled=True),
        lax.all_gather(value_low, "ctx", axis=1, tiled=True),
    )
    query_groups = group_heads(query_rot, per_group)
    attended, log_total = lax.map(
        partial(attend_block, scaling=scaling),
        (query_groups, group_heads(keys_all, per_group), group_heads(values_all, per_group)),
    )
    attended_low = ungroup_heads(attended, seq_count).astype(jnp.bfloat16)
    branch_part = jnp.einsum(
        "ste,ed->std", attended_low, full_out, preferred_element_type=jnp.float32
    )
    middle = inputs_f + lax.psum(branch_part, "tp")
    second_out, normed_two, inverse_two = scaled_norm(
        middle, gains_f[1], modulation[:, 2], modulation[:, 3]
    )
    second_low = second_out.astype(jnp.bfloat16)
    hidden = jnp.einsum("std,df->stf", second_low, full_up, preferred_element_type=jnp.float32)
    activated = jax.nn.gelu(hidden, approximate=False).astype(jnp.bfloat16)
    mlp_part = jnp.einsum("stf,fd->std", activated, full_down, preferred_element_type=jnp.float32)
    output = (middle + lax.psum(mlp_part, "tp")).astype(jnp.bfloat16)
    back_qkv, back_out, back_up, back_down = (
        lax.all_gather(qkv_weight, "shard", axis=1, tiled=True),
        lax.all_gather(out_weight, "shard", axis=1, tiled=True),
        lax.all_gather(up_weight, "shard", axis=0, tiled=True),
        lax.all_gather(down_weight, "shard", axis=1, tiled=True),
    )
    keys_back, values_back = (
        lax.all_gather(key_rot, "ctx", axis=1, tiled=True),
        lax.all_gather(value_low, "ctx", axis=1, tiled=True),
    )
    grad_down = jnp.einsum("stf,std->fd", activated, cotangent, preferred_element_type=jnp.float32)
    grad_act = jnp.einsum("std,fd->stf", cotangent, back_down, preferred_element_type=jnp.float32)
    grad_hidden = (grad_act * gelu_slope(hidden)).astype(jnp.bfloat16)
    grad_up = jnp.einsum("std,stf->df", second_low, grad_hidden, preferred_element_type=jnp.float32)
    grad_second = lax.psum(
        jnp.einsum("stf,df->std", grad_hidden, back_up, preferred_element_type=jnp.float32), "tp"
    )
    grad_mid_norm, gain_two, scaling_two, offset_two = norm_back(
        grad_second, normed_two, inverse_two, gains_f[1], modulation[:, 2]
    )
    grad_middle = cotangent.astype(jnp.float32) + grad_mid_norm
    grad_branch = grad_middle.astype(jnp.bfloat16)
    grad_out = jnp.einsum(
        "ste,std->ed", attended_low, grad_branch, preferred_element_type=jnp.float32
    )
    grad_attended = jnp.einsum(
        "std,ed->ste", grad_branch, back_out, preferred_element_type=jnp.float32
    ).astype(jnp.bfloat16)
    grad_query_g, grad_key_g, grad_value_g = lax.map(
        partial(attend_back, scaling=scaling),
        (
            query_groups,
            group_heads(keys_back, per_group),
            group_heads(values_back, per_group),
            group_heads(grad_attended, per_group),
            log_total,
        ),
    )
    grad_key_all = ungroup_heads(grad_key_g, seq_count)
    grad_value_all = ungroup_heads(grad_value_g, seq_count)
    grad_key, grad_value = (
        lax.psum_scatter(grad_key_all, "ctx", scatter_dimension=1, tiled=True),
        lax.psum_scatter(grad_value_all, "ctx", scatter_dimension=1, tiled=True),
    )
    grad_query = ungroup_heads(grad_query_g, seq_count)
    query_back = unrotate(grad_query.reshape(head_shape), cosines, sines).reshape(
        seq_count, tokens, local_width
    )
    key_back = unrotate(grad_key.reshape(head_shape), cosines, sines).reshape(
        seq_count, tokens, local_width
    )
    grad_projected = jnp.stack([query_back, key_back, grad_value], axis=0).astype(jnp.bfloat16)
    grad_qkv = jnp.einsum(
        "std,cste->cde", first_low, grad_projected, preferred_element_type=jnp.float32
    )
    grad_first = lax.psum(
        jnp.einsum("cste,cde->std", grad_projected, back_qkv, preferred_element_type=jnp.float32),
        "tp",
    )
    grad_in_norm, gain_one, scaling_one, offset_one = norm_back(
        grad_first, normed_one, inverse_one, gains_f[0], modulation[:, 0]
    )
    input_grad = (grad_middle + grad_in_norm).astype(jnp.bfloat16)
    grad_modulation = jnp.stack([scaling_one, offset_one, scaling_two, offset_two], axis=1)
    grad_time = jnp.einsum("sk,scd->kcd", embedding, grad_modulation, precision=highest)
    grad_gains = jnp.stack([gain_one, gain_two], axis=0)
    shares = (
        lax.psum_scatter(grad_qkv, "shard", scatter_dimension=1, tiled=True),
        lax.psum_scatter(grad_out, "shard", scatter_dimension=1, tiled=True),
        lax.psum_scatter(grad_up, "shard", scatter_dimension=0, tiled=True),
        lax.psum_scatter(grad_down, "shard", scatter_dimension=1, tiled=True),
        lax.psum_scatter(grad_time, "shard", scatter_dimension=2, tiled=True),
        lax.psum_scatter(grad_gains, "shard", scatter_dimension=1, tiled=True),
    )
    shares = lax.psum((shares[0], shares[1], shares[2], shares[3], shares[4], shares[5]), "ctx")
    return (output, input_grad, shares[0], shares[1], shares[2], shares[3], shares[4], shares[5])


BF = jnp.bfloat16
F32 = jnp.float32
NN = (((1,), (0,)), ((), ()))
NT = (((1,), (1,)), ((), ()))
TN = (((0,), (0,)), ((), ()))
VMEM_BIG = 56 << 20
PER_US = 0.8e9


def mm(a, b, dims=NN):
    return lax.dot_general(a, b, dims, preferred_element_type=F32)


def cost(flops, nbytes=0, trans=0):
    return pl.CostEstimate(flops=int(flops), bytes_accessed=int(nbytes), transcendentals=int(trans))


def whole(array):
    zeros = (0,) * array.ndim
    return pl.BlockSpec(array.shape, lambda *_: zeros)


def call(kernel, name, grid, scalars, ins, in_specs, outs, out_specs, est, scratch=()):
    return pl.pallas_call(
        kernel,
        out_shape=outs,
        grid_spec=pltpu.PrefetchScalarGridSpec(
            num_scalar_prefetch=len(scalars),
            grid=grid,
            in_specs=in_specs,
            out_specs=out_specs,
            scratch_shapes=list(scratch),
        ),
        compiler_params=pltpu.CompilerParams(vmem_limit_bytes=VMEM_BIG),
        cost_estimate=est,
        name=name,
    )(*scalars, *ins)


def shape(dims, dtype):
    return jax.ShapeDtypeStruct(dims, dtype)


def cols(index, width):
    return pl.ds(pl.multiple_of(index * width, width), width)


def half_turn(values):
    lane = lax.broadcasted_iota(jnp.int32, values.shape, 1) % HEAD_DIM
    width = values.shape[1]
    up = pltpu.roll(values, HEAD_DIM // 2, 1)
    down = pltpu.roll(values, width - HEAD_DIM // 2, 1)
    return jnp.where(lane < HEAD_DIM // 2, down, up)


def spin(cos_ref, sin_ref, width):
    cosines, sines = cos_ref[...].T, sin_ref[...].T
    heads = width // HEAD_DIM
    return jnp.concatenate([cosines, cosines] * heads, axis=1), jnp.concatenate([-sines, sines] * heads, axis=1)


def pick(step, first_ref, second_ref, per_half):
    return jnp.where(step < per_half, first_ref[...], second_ref[...])


def own_map(per_half):
    return lambda i, *_: (jnp.minimum(i, per_half - 1), 0)


def other_map(per_half):
    return lambda i, *_: (jnp.maximum(i - per_half, 0), 0)


def project_kernel(per_half, blk, xa, xb, w0, w1, w2, w3, mods, cosb, sinb, h_ref, q_ref, k_ref, kt_ref, v_ref, vt_ref):
    x = pick(pl.program_id(0), xa, xb, per_half).astype(F32)
    x = x - jnp.mean(x, axis=1, keepdims=True)
    var = jnp.mean(x * x, axis=1, keepdims=True)
    n = x * lax.rsqrt(var + norm_epsilon)
    h_ref[...] = (n * mods[0:1, :] + mods[1:2, :]).astype(BF)
    rows = w0.shape[0]
    acc = None
    for j, w in enumerate((w0, w1, w2, w3)):
        part = mm(h_ref[:, cols(blk[j], rows)], w[...])
        acc = part if acc is None else acc + part
    wide = acc.shape[1] // 3
    cosines, sines = spin(cosb, sinb, wide)
    q = acc[:, :wide]
    k = acc[:, wide : 2 * wide]
    v = acc[:, 2 * wide :]
    q = q * cosines + half_turn(q) * sines
    k = k * cosines + half_turn(k) * sines
    q_ref[...] = q.astype(BF)
    k_ref[...] = k.astype(BF)
    kt_ref[...] = k.T.astype(BF)
    v_ref[...] = v.astype(BF)
    vt_ref[...] = v.T.astype(BF)


def project(blk, xa, xb, ws, mods, cosb, sinb, tile=256):
    half, width = xa.shape
    total = 2 * half
    wide = ws[0].shape[1] // 3
    per_half = half // tile
    row = lambda w: pl.BlockSpec((tile, w), lambda i, *_: (i, 0))
    turned = pl.BlockSpec((wide, tile), lambda i, *_: (0, i))
    return call(
        partial(project_kernel, per_half), "project", (total // tile,), (blk,),
        (xa, xb, *ws, mods, cosb, sinb),
        [pl.BlockSpec((tile, width), own_map(per_half)), pl.BlockSpec((tile, width), other_map(per_half)),
         *[whole(w) for w in ws], whole(mods), *[pl.BlockSpec((v.shape[0], tile), lambda i, *_: (0, i)) for v in (cosb, sinb)]],
        [shape((total, width), BF), shape((total, wide), BF), shape((total, wide), BF), shape((wide, total), BF),
         shape((total, wide), BF), shape((wide, total), BF)],
        [row(width), row(wide), row(wide), turned, row(wide), turned],
        cost(12.5 * PER_US),
    )


def attend_kernel(scale, q_ref, k_ref, vt_ref, o_ref, ot_ref, lse_ref):
    rows, wide = q_ref.shape
    q = q_ref[...]
    lane = lax.broadcasted_iota(jnp.int32, (rows, wide), 1) // HEAD_DIM
    def head(h, _):
        at = pl.ds(pl.multiple_of(h * HEAD_DIM, HEAD_DIM), HEAD_DIM)
        qh = jnp.where(lane == h, q, jnp.zeros_like(q))
        s = mm(k_ref[...], qh, NT) * scale
        top = jnp.max(s, axis=0, keepdims=True)
        p = jnp.exp(s - top)
        total = jnp.sum(p, axis=0, keepdims=True)
        ot_ref[at, :] = mm(vt_ref[at, :], p.astype(BF)) / total
        lse_ref[pl.ds(h, 1), :] = top + jnp.log(total)
        return 0

    lax.fori_loop(0, wide // HEAD_DIM, head, 0)
    o_ref[...] = ot_ref[...].T.astype(BF)


def attend(q, k, vt, first, rows, tile=1024):
    total, wide = q.shape
    heads = wide // HEAD_DIM
    skip = first // tile
    return call(
        partial(attend_kernel, HEAD_DIM**-0.5), "attend", (rows // tile,), (), (q, k, vt),
        [pl.BlockSpec((tile, wide), lambda i: (i + skip, 0)), whole(k), whole(vt)],
        [shape((rows, wide), BF), shape((wide, rows), F32), shape((heads, rows), F32)],
        [pl.BlockSpec((tile, wide), lambda i: (i, 0)), pl.BlockSpec((wide, tile), lambda i: (0, i)),
         pl.BlockSpec((heads, tile), lambda i: (0, i))],
        cost(10.0 * PER_US),
    )


def join_kernel(n_t, blk, blo, x_ref, *refs):
    near, far = refs[:n_t], refs[n_t : 2 * n_t]
    mine = refs[2 * n_t : 6 * n_t]
    theirs, mods, x1_ref, h_ref = refs[6 * n_t :]
    own = jnp.concatenate([o[...] for o in near], axis=1)
    oth = jnp.concatenate([o[...] for o in far], axis=1)
    span = theirs.shape[1]
    deep = own.shape[1]
    for k in range(4):
        at = cols(blk[k], span)
        w = jnp.concatenate([mine[4 * j + k][...] for j in range(n_t)], axis=0)
        x1_ref[:, at] = x_ref[:, at].astype(F32) + mm(own, w)
    for k in range(4):
        at = cols(blo[k], span)
        x1_ref[:, at] += mm(oth, theirs[k * deep : (k + 1) * deep, :])
    x = x1_ref[...]
    x = x - jnp.mean(x, axis=1, keepdims=True)
    var = jnp.mean(x * x, axis=1, keepdims=True)
    n = x * lax.rsqrt(var + norm_epsilon)
    h_ref[...] = (n * mods[2:3, :] + mods[3:4, :]).astype(BF)


def part_of(array, index, rows):
    return pl.BlockSpec((rows, array.shape[1]), lambda *_: (index, 0))


def stack_kernel(*refs):
    rows = refs[0].shape[0]
    for i, ref in enumerate(refs[:-1]):
        refs[-1][i * rows : (i + 1) * rows, :] = ref[...]


def stack_parts(arrays, rows):
    width = arrays[0].shape[1]
    return call(
        stack_kernel, "stack_parts", (1,), (), arrays,
        [part_of(v, v.shape[0] // rows - 1, rows) for v in arrays],
        shape((len(arrays) * rows, width), BF), pl.BlockSpec((len(arrays) * rows, width), lambda i: (0, 0)),
        cost(2.3 * PER_US),
    )


def join(blk, blo, x, near, far, slots, theirs, mods, tile=256):
    half, width = x.shape
    n_t = len(slots)
    wide = near[0].shape[1]
    row = lambda w: pl.BlockSpec((tile, w), lambda i, *_: (i, 0))
    flat = [w for slot in slots for w in slot]
    last_part = flat[0].shape[0] // wide - 1
    return call(
        partial(join_kernel, n_t), "join", (half // tile,), (blk, blo), (x, *near, *far, *flat, theirs, mods),
        [row(width), *[row(wide)] * (2 * n_t), *[part_of(w, last_part, wide) for w in flat], whole(theirs), whole(mods)],
        [shape((half, width), F32), shape((half, width), BF)],
        [row(width), row(width)],
        cost(8.5 * PER_US),
    )


def gelu_parts(u):
    half = 0.5 * (1.0 + lax.erf(u * 0.7071067811865476))
    slope = half + u * jnp.exp(-0.5 * u * u) * 0.3989422804014327
    return u * half, slope


def unpack_kernel(blk, *refs):
    ws, (up_ref, down_ref) = refs[:4], refs[-2:]
    span = ws[0].shape[1]
    for j, w in enumerate(ws):
        rows = pl.ds(pl.multiple_of(blk[j] * span, span), span)
        for b in range(2):
            up_ref[rows, b * span : (b + 1) * span] = w[b * span : (b + 1) * span, :]
        down_ref[:, cols(blk[j], span)] = w[2 * span : 4 * span, :]


def unpack(blk, slot, index, n_slots, before):
    span = slot[0].shape[1]
    width, hidden = 4 * span, 2 * span
    any_space = pl.BlockSpec(memory_space=pl.ANY)
    kept = () if before is None else before
    return pl.pallas_call(
        unpack_kernel,
        out_shape=[shape((n_slots * width, hidden), BF), shape((n_slots * hidden, width), BF)],
        grid_spec=pltpu.PrefetchScalarGridSpec(
            num_scalar_prefetch=1,
            grid=(1,),
            in_specs=[part_of(w, 0, width) for w in slot] + [any_space] * len(kept),
            out_specs=[pl.BlockSpec((width, hidden), lambda *_: (index, 0)), pl.BlockSpec((hidden, width), lambda *_: (index, 0))],
        ),
        input_output_aliases={5: 0, 6: 1} if kept else {},
        compiler_params=pltpu.CompilerParams(vmem_limit_bytes=VMEM_BIG),
        cost_estimate=cost(2.5 * PER_US),
        name="unpack",
    )(blk, *slot, *kept)


def mlp_kernel(per_half, n_slots, ha, hb, ca, cb, wu, wd, own_ref, oth_ref, g_ref, du_ref, h_buf, c_buf, du_buf):
    step = pl.program_id(0)
    width = ha.shape[1]
    hidden = wu.shape[1]
    h_buf[...] = pick(step, ha, hb, per_half)
    c_buf[...] = pick(step, ca, cb, per_half)

    def one(i, _):
        at = cols(i, hidden)
        u = mm(h_buf[...], wu[pl.ds(pl.multiple_of(i * width, width), width), :])
        dg = mm(c_buf[...], wd[pl.ds(pl.multiple_of(i * hidden, hidden), hidden), :], NT)
        g, slope = gelu_parts(u)
        g_ref[:, at] = g.astype(BF)
        du_buf[:, at] = (dg * slope).astype(BF)
        return 0

    lax.fori_loop(0, n_slots, one, 0)
    du_ref[...] = du_buf[:, :hidden]
    chunk = min(512, width)
    for n in range(width // chunk):
        at = slice(n * chunk, (n + 1) * chunk)
        acc = None
        for i in range(n_slots):
            part = mm(du_buf[:, i * hidden : (i + 1) * hidden], wu[i * width + n * chunk : i * width + (n + 1) * chunk, :], NT)
            acc = part if acc is None else acc + part

        @pl.when(step < per_half)
        def _():
            own_ref[:, at] = acc

        @pl.when(step >= per_half)
        def _():
            oth_ref[:, at] = acc.astype(BF)


def mlp(ha, hb, ca, cb, wu, wd, tile=512):
    half, width = ha.shape
    total = 2 * half
    per_half = half // tile
    hidden = wu.shape[1]
    n_slots = wu.shape[0] // width
    row = lambda w: pl.BlockSpec((tile, w), lambda i, *_: (i, 0))
    mine = pl.BlockSpec((tile, width), own_map(per_half))
    theirs = pl.BlockSpec((tile, width), other_map(per_half))
    return call(
        partial(mlp_kernel, per_half, n_slots), "mlp", (total // tile,), (), (ha, hb, ca, cb, wu, wd),
        [mine, theirs, mine, theirs, whole(wu), whole(wd)],
        [shape((half, width), F32), shape((half, width), BF), shape((total, n_slots * hidden), BF), shape((total, hidden), BF)],
        [mine, theirs, row(n_slots * hidden), row(hidden)],
        cost(42.0 * PER_US),
        [pltpu.VMEM((tile, width), BF), pltpu.VMEM((tile, width), BF), pltpu.VMEM((tile, n_slots * hidden), BF)],
    )


def lift_kernel(per_half, g_in, wd, own_ref, oth_ref):
    step = pl.program_id(0)
    chunk = 512
    for n in range(wd.shape[1] // chunk):
        at = slice(n * chunk, (n + 1) * chunk)
        part = mm(g_in[...], wd[:, at])

        @pl.when(step < per_half)
        def _():
            own_ref[:, at] = part

        @pl.when(step >= per_half)
        def _():
            oth_ref[:, at] = part.astype(BF)


def lift(g, wd, tile=512):
    total = g.shape[0]
    width = wd.shape[1]
    half = total // 2
    per_half = half // tile
    return call(
        partial(lift_kernel, per_half), "lift", (total // tile,), (), (g, wd),
        [pl.BlockSpec((tile, g.shape[1]), lambda i, *_: (i, 0)), whole(wd)],
        [shape((half, width), F32), shape((half, width), BF)],
        [pl.BlockSpec((tile, width), own_map(per_half)), pl.BlockSpec((tile, width), other_map(per_half))],
        cost(14.0 * PER_US),
    )


def norm_turn(dh, x, factor):
    x = x - jnp.mean(x, axis=1, keepdims=True)
    var = jnp.mean(x * x, axis=1, keepdims=True)
    r = lax.rsqrt(var + norm_epsilon)
    n = x * r
    dn = dh * factor
    dx = r * (dn - jnp.mean(dn, axis=1, keepdims=True) - n * jnp.mean(dn * n, axis=1, keepdims=True))
    return dx, jnp.sum(dh * n, axis=0, keepdims=True), jnp.sum(dh, axis=0, keepdims=True)


def turn_kernel(blk, blo, dh_ref, in_ref, x_ref, c_ref, mods, a0, a1, a2, a3, b_ref, dx_ref, da_ref, own_ref, oth_ref, sums):
    dh = dh_ref[...] + in_ref[...].astype(F32)
    dx, s1, s0 = norm_turn(dh, x_ref[...], mods[2:3, :])
    dx = dx + c_ref[...].astype(F32)
    dx_ref[...] = dx
    da_ref[...] = dx.astype(BF)
    wide = own_ref.shape[1]
    span = a0.shape[1]
    step = b_ref.shape[0] // 4
    theirs = [b_ref[k * step : k * step + wide, :] for k in range(4)]
    for order, ws, out in ((blk, [a[...] for a in (a0, a1, a2, a3)], own_ref), (blo, theirs, oth_ref)):
        acc = None
        for j, w in enumerate(ws):
            part = mm(da_ref[:, cols(order[j], span)], w, NT)
            acc = part if acc is None else acc + part
        out[...] = acc.astype(BF)

    @pl.when(pl.program_id(0) == 0)
    def _():
        sums[...] = jnp.zeros_like(sums)

    sums[0:1, :] += s1
    sums[1:2, :] += s0


def turn(blk, blo, dh, received, x1, cot, mods, wa, wb, wide, tile=256):
    half, width = x1.shape
    row = lambda w: pl.BlockSpec((tile, w), lambda i, *_: (i, 0))
    return call(
        turn_kernel, "turn", (half // tile,), (blk, blo), (dh, received, x1, cot, mods, *wa, wb),
        [row(width)] * 4 + [whole(mods), *[part_of(w, w.shape[0] // wide - 1, wide) for w in wa], whole(wb)],
        [shape((half, width), F32), shape((half, width), BF), shape((half, wide), BF), shape((half, wide), BF), shape((8, width), F32)],
        [row(width), row(width), row(wide), row(wide), pl.BlockSpec((8, width), lambda i, *_: (0, 0))],
        cost(11.3 * PER_US),
    )


def attend_back_kernel(scale, tk, per_half, q_ref, da_ref, db_ref, ota_ref, otb_ref, la_ref, lb_ref, cos_ref, sin_ref, k_ref, v_ref, kt_ref, cosb, sinb, dq_ref, dk_ref, dv_ref, dqt, dk_acc, dv_acc):
    rows, wide = q_ref.shape
    total = k_ref.shape[0]
    step = pl.program_id(0)
    q = q_ref[...]
    do = pick(step, da_ref, db_ref, per_half)
    lse = pick(step, la_ref, lb_ref, per_half)
    lane = lax.broadcasted_iota(jnp.int32, (rows, wide), 1) // HEAD_DIM
    heads = wide // HEAD_DIM
    qs = [jnp.where(lane == h, q, jnp.zeros_like(q)) for h in range(heads)]
    ds = [jnp.where(lane == h, do, jnp.zeros_like(do)) for h in range(heads)]
    od = do.astype(F32).T * pick(step, ota_ref, otb_ref, per_half)
    deltas = [jnp.sum(od[h * HEAD_DIM : (h + 1) * HEAD_DIM, :], axis=0, keepdims=True) for h in range(heads)]

    @pl.when(step == 0)
    def _():
        dk_acc[...] = jnp.zeros_like(dk_acc)
        dv_acc[...] = jnp.zeros_like(dv_acc)

    dqt[...] = jnp.zeros_like(dqt)
    for j in range(total // tk):
        at = slice(j * tk, (j + 1) * tk)
        kj, vj = k_ref[at, :], v_ref[at, :]
        for h in range(heads):
            hs = slice(h * HEAD_DIM, (h + 1) * HEAD_DIM)
            s = mm(kj, qs[h], NT) * scale
            p = jnp.exp(s - lse[h : h + 1, :])
            dp = mm(vj, ds[h], NT)
            dsc = (p * (dp - deltas[h])).astype(BF)
            dv_acc[at, :] += mm(p.astype(BF), ds[h])
            dk_acc[at, :] += mm(dsc, qs[h])
            dqt[hs, :] += mm(kt_ref[hs, at], dsc)
    dq = dqt[...].T * scale
    cosines, sines = spin(cos_ref, sin_ref, wide)
    dq_ref[...] = (dq * cosines - half_turn(dq) * sines).astype(BF)

    @pl.when(step == pl.num_programs(0) - 1)
    def _():
        dk = dk_acc[...] * scale
        cosines, sines = spin(cosb, sinb, wide)
        dk_ref[...] = (dk * cosines - half_turn(dk) * sines).astype(BF)
        dv_ref[...] = dv_acc[...].astype(BF)


def attend_back_call(q, do_a, do_b, ots, lses, k, v, kt, cosb, sinb, tile=512, tk=512):
    total, wide = q.shape
    heads = wide // HEAD_DIM
    per_half = total // 2 // tile
    row = pl.BlockSpec((tile, wide), lambda i: (i, 0))
    lanes_a = lambda h: pl.BlockSpec((h, tile), lambda i: (0, jnp.minimum(i, per_half - 1)))
    lanes_b = lambda h: pl.BlockSpec((h, tile), lambda i: (0, jnp.maximum(i - per_half, 0)))
    full = pl.BlockSpec((total, wide), lambda i: (0, 0))
    turned = pl.BlockSpec((cosb.shape[0], tile), lambda i: (0, i))
    return call(
        partial(attend_back_kernel, HEAD_DIM**-0.5, tk, per_half), "attend_back", (total // tile,), (),
        (q, do_a, do_b, *ots, *lses, cosb, sinb, k, v, kt, cosb, sinb),
        [row, pl.BlockSpec((tile, wide), own_map(per_half)), pl.BlockSpec((tile, wide), other_map(per_half)),
         lanes_a(wide), lanes_b(wide), lanes_a(heads), lanes_b(heads), turned, turned, full, full, whole(kt), whole(cosb), whole(sinb)],
        [shape((total, wide), BF)] * 3,
        [row, full, full],
        cost(29.0 * PER_US),
        [pltpu.VMEM((wide, tile), F32), pltpu.VMEM((total, wide), F32), pltpu.VMEM((total, wide), F32)],
    )


def gather_kernel(blk, *refs):
    n = (len(refs) - 2) // 5
    rs = refs[:n]
    ws = [refs[n + 4 * i : n + 4 * i + 4] for i in range(n)]
    own_ref, oth_ref = refs[5 * n :]
    rows = own_ref.shape[0]
    span = ws[0][0].shape[0]
    for j in range(4):
        acc = None
        for r, w in zip(rs, ws):
            part = mm(r[...], w[j][...], NT)
            acc = part if acc is None else acc + part
        own_ref[:, cols(blk[j], span)] = acc[:rows]
        oth_ref[:, cols(blk[j], span)] = acc[rows:].astype(BF)


def gather(blk, rs, slots, width):
    rows = rs[0].shape[0] // 2
    flat = [w for slot in slots for w in slot]
    back = pl.BlockSpec((rows, width), lambda i, *_: (0, 0))
    return call(
        gather_kernel, "gather", (1,), (blk,), (*rs, *flat),
        [*[whole(r) for r in rs], *[whole(w) for w in flat]],
        [shape((rows, width), F32), shape((rows, width), BF)],
        [back, back],
        cost(6.5 * PER_US),
    )


def last_kernel(dh_ref, in_ref, x_ref, dx_ref, mods, out_ref, sums):
    dx, s1, s0 = norm_turn(dh_ref[...] + in_ref[...].astype(F32), x_ref[...].astype(F32), mods[0:1, :])
    out_ref[...] = (dx + dx_ref[...]).astype(BF)
    sums[...] = jnp.zeros_like(sums)
    sums[0:1, :] = s1
    sums[1:2, :] = s0


def last(dh, received, x, dx, mods):
    rows, width = dh.shape
    return call(
        last_kernel, "last", (1,), (), (dh, received, x, dx, mods),
        [whole(v) for v in (dh, received, x, dx, mods)],
        [shape((rows, width), BF), shape((8, width), F32)],
        [pl.BlockSpec((rows, width), lambda i: (0, 0)), pl.BlockSpec((8, width), lambda i: (0, 0))],
        cost(3.5 * PER_US),
    )


def after(values, *events):
    return lax.optimization_barrier((values, events))[0]


def fast_body(
    activations, timestep, positions, qkv_weight, out_weight, up_weight, down_weight, time_weight, norm_gains, cotangent
):
    n_s, n_t = lax.axis_size("shard"), lax.axis_size("tp")
    s, c, t = lax.axis_index("shard"), lax.axis_index("ctx"), lax.axis_index("tp")
    x_own = activations[0]
    cot_own = cotangent[0]
    half, width = x_own.shape
    span = width // n_s
    quarter = half // n_t
    near = jnp.where(c == 0, 1, 2)
    blk = jnp.stack([s, s ^ near, s ^ (3 - near), s ^ 3]).astype(jnp.int32)
    blo = jnp.stack([s, s ^ (3 - near), s ^ near, s ^ 3]).astype(jnp.int32)
    pairs_a = [(v * 2 + k, (v ^ (1 + k)) * 2 + k) for v in range(n_s) for k in range(2)]
    pairs_b = [(v * 2 + k, (v ^ (2 - k)) * 2 + k) for v in range(n_s) for k in range(2)]
    cycle = [(i, (i + 1) % n_t) for i in range(n_t)]
    swap = lambda v: lax.ppermute(v, "ctx", [(0, 1), (1, 0)])
    move_a = lambda v: lax.ppermute(v, ("shard", "ctx"), pairs_a)
    move_b = lambda v: lax.ppermute(v, ("shard", "ctx"), pairs_b)
    upward = lambda v: lax.ppermute(v, "tp", cycle)

    def by_z(v, d):
        return lax.ppermute(v, "tp", [(i, (i + d) % n_t) for i in range(n_t)])

    def turn_shard(v, d):
        return lax.ppermute(v, "shard", [(i, (i + d) % n_s) for i in range(n_s)])

    def half_of(v, axis):
        size = v.shape[axis] // 2
        return lax.dynamic_slice_in_dim(v, c * size, size, axis)

    def both(v, axis):
        other = swap(v)
        return jnp.where(c == 0, jnp.concatenate([v, other], axis), jnp.concatenate([other, v], axis))

    x_oth = swap(x_own)

    def shard_pair(v, bit):
        return lax.ppermute(v, "shard", [(i, i ^ bit) for i in range(n_s)])

    gains = norm_gains.astype(F32)
    small = jnp.concatenate([gains, jnp.broadcast_to(timestep.astype(F32)[:, None], (1, span))], axis=0)
    small_two = jnp.concatenate([small, shard_pair(small, 1)], axis=0)
    small_four = jnp.concatenate([small_two, shard_pair(small_two, 2)], axis=0)
    smalls = [small_four[3 * i : 3 * i + 3] for i in range(n_s)]

    wide = qkv_weight.shape[2] // 2
    qkv_half = half_of(qkv_weight, 2)
    qkv_share = jnp.concatenate([qkv_half[0], qkv_half[1], qkv_half[2]], axis=1)
    qkv_a, qkv_b = move_a(qkv_share), move_b(qkv_share)
    qkv_c = move_b(qkv_a)
    w_qkv = [qkv_share, qkv_a, qkv_b, qkv_c]
    pos_own = positions.astype(F32)
    pos_oth = swap(pos_own)

    up_half = half_of(up_weight, 1)
    down_half = half_of(down_weight, 0)
    pack = jnp.concatenate([up_half[:, :span], up_half[:, span:], down_half, half_of(out_weight, 0)], axis=0)
    z1 = upward(pack)
    pack_go = after(pack, qkv_a, qkv_b)
    m0a, m0b = move_a(pack_go), move_b(pack_go)

    steps = small_four[2::3, 0]
    embedding = embed_time(steps)
    parts = jnp.einsum("sk,kcd->scd", embedding, time_weight.astype(F32), precision=highest)
    parts_x = shard_pair(jnp.concatenate([parts[1], parts[3]], axis=0), 1)
    parts_y = shard_pair(after(jnp.concatenate([parts[2], parts_x[4:]], axis=0), qkv_c), 2)
    parts_in = [parts[0], parts_x[:4], parts_y[:4], parts_y[4:]]
    gain_full = jnp.zeros((2, width), F32)
    mod_full = jnp.zeros((4, width), F32)
    for i in range(n_s):
        gain_full = lax.dynamic_update_slice_in_dim(gain_full, smalls[i][:2], (s ^ i) * span, 1)
        mod_full = lax.dynamic_update_slice_in_dim(mod_full, parts_in[i], (s ^ i) * span, 1)
    factor_one = gain_full[0] * (1.0 + mod_full[0])
    factor_two = gain_full[1] * (1.0 + mod_full[2])
    zero = jnp.zeros_like(factor_one)
    mods = jnp.stack([factor_one, mod_full[1], factor_two, mod_full[3], zero, zero, zero, zero])

    half_width = HEAD_DIM // 2
    frequency = jnp.exp(-math.log(10000.0) * jnp.arange(half_width, dtype=F32) / half_width)
    angles = frequency[:, None] * jnp.concatenate([pos_own, pos_oth], axis=1)
    cosb, sinb = jnp.cos(angles), jnp.sin(angles)

    z1 = after(z1, parts_y)
    z2 = upward(z1)
    m1a, m1b = move_a(z1), move_b(z1)
    x_now = after(x_own, z1)
    h1, q, k, kt, v, vt = project(blk, x_now, x_oth, w_qkv, mods, cosb, sinb)
    m0a_late, m1a_late, z2_late = after((m0a, m1a, z2), q, m0b)
    m0c, m1c, z3 = move_b(m0a_late), move_b(m1a_late), upward(z2_late)
    o_far, ot_far, lse_far = attend(q, k, vt, half, half)
    o_got = swap(o_far)
    z2_late = after(z2, o_far, m0c, m1b)
    m2a, m2b = move_a(z2_late), move_b(z2_late)
    far = [after(o_got, z3)]
    far.append(upward(far[0]))
    o_near, ot_near, lse_near = attend(after(q, o_far), k, vt, 0, half)
    wu, wd = unpack(blk, [pack, m0a, m0b, m0c], 0, n_t, None)
    z3_late, m2a_late, far_go, near_go = after((z3, m2a, far[1], o_near), m2b, m1c)
    m3a, m3b, m2c = move_a(z3_late), move_b(z3_late), move_b(m2a_late)
    near = [near_go, upward(near_go)]
    far.append(upward(far_go))
    m3a_late, near_go, far_go, m1c_late = after((m3a, near[1], far[2], m1c), m2c, m3b)
    m3c = move_b(m3a_late)
    near.append(upward(near_go))
    far.append(upward(far_go))
    wu, wd = unpack(blk, [z1, m1a, m1b, m1c_late], 1, n_t, (wu, wd))
    near_go, m3c, far_done = after((near[2], m3c, far[3]), wu)
    near.append(upward(near_go))
    far[3] = far_done
    wu, wd = unpack(blk, [z2, m2a, m2b, after(m2c, m3c)], 2, n_t, (wu, wd))
    wu, wd = unpack(blk, [z3, m3a, m3b, m3c], 3, n_t, (wu, wd))
    cot_oth = swap(cot_own)
    w_mlp = [[pack, m0a, m0b, m0c], [z1, m1a, m1b, m1c], [z2, m2a, m2b, m2c], [z3, m3a, m3b, m3c]]
    out_other = swap(stack_parts([w_mlp[j][i] for i in range(n_s) for j in range(n_t)], wide))

    x1, h2 = join(blk, blo, after(x_own, wu), near, far, w_mlp, out_other, mods)
    h2_oth = swap(h2)
    dh2, dh2_send, g_all, du0 = mlp(h2, h2_oth, cot_own, cot_oth, wu, wd)
    qkv_again = after(qkv_share, h2_oth)
    qz_pack = jnp.concatenate([by_z(qkv_again, d) for d in range(1, n_t)], axis=0)
    dh2_in = swap(after(dh2_send, qz_pack))
    qz_pack = after(qz_pack, dh2_in)
    qza, qzb = move_a(qz_pack), move_b(qz_pack)
    dx1, da, do_own, do_send, sums_two = turn(blk, blo, dh2, dh2_in, x1, cot_own, mods, w_mlp[0], out_other, wide)
    do_got = swap(do_send)
    qza, qzb, do_got = after((qza, qzb, do_got), da)
    qzc = move_b(qza)
    w_back = [w_qkv] + [[v[i * span : (i + 1) * span] for v in (qz_pack, qza, qzb, qzc)] for i in range(n_t - 1)]
    dq, dk, dv = attend_back_call(q, do_own, do_got, (ot_near, ot_far), (lse_near, lse_far), k, v, kt, cosb, sinb)

    dqkv = jnp.concatenate([dq, dk, dv], axis=1).reshape(2, half, 3 * wide)

    def tokens_of(d):
        return lax.dynamic_slice_in_dim(dqkv, ((t + d) % n_t) * quarter, quarter, 1).reshape(2 * quarter, 3 * wide)

    got = [tokens_of(0), by_z(tokens_of(1), 1)]

    h2_late, h2o_late, du0_late, g_late = after((h2, h2_oth, du0, g_all), tokens_of(1))
    g_up = mm(jnp.concatenate([h2_late, h2o_late], axis=0), du0_late, TN)
    g_down = mm(g_late[:, : 2 * span], jnp.concatenate([cot_own, cot_oth], axis=0), TN)
    got.append(by_z(after(tokens_of(2), got[1], g_up, g_down), 2))
    g_later = after(g_late, got[1], g_up, g_down)
    y_own, y_send = lift(g_later, wd)
    got[2], y_own, y_send, da_late, g_up, g_down = after((got[2], y_own, y_send, da, g_up, g_down), got[2])
    got.append(by_z(after(tokens_of(3), got[2], y_own), 3))
    g_out = mm(o_near, da_late, TN) + swap(mm(o_got, da_late, TN).astype(BF)).astype(F32)

    def mlp_piece(j):
        ups = lax.dynamic_slice_in_dim(g_up, blk[j] * span, span, 0)
        downs = lax.dynamic_slice_in_dim(g_down, blk[j] * span, span, 1)
        outs = lax.dynamic_slice_in_dim(g_out, blk[j] * span, span, 1)
        return jnp.concatenate([ups[:, :span], ups[:, span:], downs, outs], axis=0)

    def reduce_first(pieces):
        return move_b(jnp.concatenate([pieces(2), pieces(3)], axis=0).astype(BF))

    def reduce_last(pieces, came):
        rows = came.shape[0] // 2
        return pieces(0) + came[:rows].astype(F32) + move_a((pieces(1) + came[rows:].astype(F32)).astype(BF)).astype(F32)

    mlp_came = reduce_first(mlp_piece)
    output = (x1 + y_own + swap(y_send).astype(F32)).astype(BF)

    dh1_own, dh1_send = gather(blk, after(got, output, mlp_came), w_back, width)
    dh1_got = swap(dh1_send)

    def token_block(v):
        return lax.dynamic_slice_in_dim(v, t * quarter, quarter, 0)

    grad_mine, sums_one = last(dh1_own, dh1_got, token_block(x_own), token_block(dx1), mods)
    slots = [grad_mine, upward(grad_mine)]
    h1_late, dqkv_late, mlp_late = after((h1, dqkv, mlp_came), grad_mine)
    g_qkv = mm(h1_late, dqkv_late.reshape(2 * half, 3 * wide), TN)
    qkv_piece = lambda j: lax.dynamic_slice_in_dim(g_qkv, blk[j] * span, span, 0)
    qkv_came = reduce_first(qkv_piece)
    rows = mlp_late.shape[0] // 2
    mlp_base = mlp_piece(0) + mlp_late[:rows].astype(F32)
    mlp_last = move_a((mlp_piece(1) + mlp_late[rows:].astype(F32)).astype(BF))
    keep = jnp.where(t == 0, 1.0, 0.0)
    tally = jnp.concatenate([sums_one[:2], sums_two[:2] * keep], axis=0)
    tally = tally + swap(tally)

    slots[1], mlp_last, tally = after((slots[1], mlp_last, tally), mlp_base, g_qkv)
    slots.append(upward(slots[1]))
    done = mlp_base + mlp_last.astype(F32)
    grad_up = both(jnp.concatenate([done[:span], done[span : 2 * span]], axis=1), 1)
    grad_down = both(done[2 * span : 4 * span], 0)
    grad_out = both(done[4 * span :], 0)
    qkv_came = after(qkv_came, slots[1])
    rows = qkv_came.shape[0] // 2
    qkv_base = qkv_piece(0) + qkv_came[:rows].astype(F32)
    qkv_last = move_a((qkv_piece(1) + qkv_came[rows:].astype(F32)).astype(BF))
    full = tally
    for bit in (1, 2):
        full = full + lax.ppermute(full, "tp", [(i, i ^ bit) for i in range(n_t)])

    slots[2], qkv_last, full = after((slots[2], qkv_last, full), grad_up, grad_down, grad_out, qkv_base)
    slots.append(upward(slots[2]))
    done_qkv = qkv_base + qkv_last.astype(F32)
    grad_qkv = both(jnp.stack([done_qkv[:, i * wide : (i + 1) * wide] for i in range(3)]), 2)
    dmods = jnp.stack([full[0] * gain_full[0], full[1], full[2] * gain_full[1], full[3],
                       full[0] * (1.0 + mod_full[0]), full[2] * (1.0 + mod_full[2])])
    blocks = [lax.dynamic_slice_in_dim(dmods, (s ^ i) * span, span, 1) for i in range(n_s)]
    blocks_x = shard_pair(jnp.concatenate([blocks[1], blocks[3]], axis=0), 1)
    blocks_y = shard_pair(jnp.concatenate([blocks[2], blocks_x[6:]], axis=0), 2)
    seqs = jnp.stack([blocks[0], blocks_x[:6], blocks_y[:6], blocks_y[6:]])
    grad_time = jnp.einsum("sk,scd->kcd", embedding, seqs[:, :4], precision=highest)
    grad_gains = jnp.sum(seqs[:, 4:], axis=0)
    slots[3] = after(slots[3], grad_qkv, grad_time, grad_gains)
    input_grad = jnp.zeros((half, width), BF)
    for j in range(n_t):
        input_grad = lax.dynamic_update_slice_in_dim(input_grad, slots[j], ((t - j) % n_t) * quarter, 0)
    return (output[None], input_grad[None], grad_qkv, grad_out, grad_up, grad_down, grad_time, grad_gains)


def solution(mesh):
    sizes = dict(mesh.shape)
    chosen = fast_body if (sizes["shard"], sizes["ctx"], sizes["tp"]) == (4, 2, 4) else body
    placed = (
        P("shard", "ctx", None),
        P("shard"),
        P("shard", "ctx"),
        P(None, "shard", "tp"),
        P("tp", "shard"),
        P("shard", "tp"),
        P("tp", "shard"),
        P(None, None, "shard"),
        P(None, "shard"),
        P("shard", "ctx", None),
    )
    return jax.shard_map(
        chosen,
        mesh=mesh,
        in_specs=placed,
        out_specs=(
            P("shard", "ctx", None),
            P("shard", "ctx", None),
            P(None, "shard", "tp"),
            P("tp", "shard"),
            P("shard", "tp"),
            P("tp", "shard"),
            P(None, None, "shard"),
            P(None, "shard"),
        ),
        check_vma=False,
    )
```

```python
from functools import partial
import math

import jax
import jax.numpy as jnp
from jax import lax
from jax.experimental import pallas as pl
from jax.experimental.pallas import tpu as pltpu
from jax.sharding import PartitionSpec as P

HEAD_DIM = 64
TEMB = 256


highest = lax.Precision.HIGHEST
norm_epsilon = 1e-05


def embed_time(timestep):
    half_width = TEMB // 2
    frequency = jnp.exp(-math.log(10000.0) * jnp.arange(half_width, dtype=jnp.float32) / half_width)
    angles = timestep.astype(jnp.float32)[:, None] * frequency[None, :]
    return jnp.concatenate([jnp.sin(angles), jnp.cos(angles)], axis=-1)


def rotary_tables(positions):
    half_width = HEAD_DIM // 2
    frequency = jnp.exp(-math.log(10000.0) * jnp.arange(half_width, dtype=jnp.float32) / half_width)
    angles = positions.astype(jnp.float32)[..., None] * frequency
    return (jnp.cos(angles), jnp.sin(angles))


def rotate(heads_in, cosines, sines):
    half_width = HEAD_DIM // 2
    first = heads_in[..., :half_width]
    second = heads_in[..., half_width:]
    cos_wide = cosines[..., None, :]
    sin_wide = sines[..., None, :]
    return jnp.concatenate(
        [first * cos_wide - second * sin_wide, second * cos_wide + first * sin_wide], axis=-1
    )


def unrotate(heads_in, cosines, sines):
    half_width = HEAD_DIM // 2
    first = heads_in[..., :half_width]
    second = heads_in[..., half_width:]
    cos_wide = cosines[..., None, :]
    sin_wide = sines[..., None, :]
    return jnp.concatenate(
        [first * cos_wide + second * sin_wide, second * cos_wide - first * sin_wide], axis=-1
    )


def scaled_norm(values, gain_vec, scaling, offset):
    centered = values - jnp.mean(values, axis=-1, keepdims=True)
    variance = jnp.mean(centered * centered, axis=-1, keepdims=True)
    inverse_std = lax.rsqrt(variance + norm_epsilon)
    normed = centered * inverse_std
    return (
        normed * gain_vec * (1.0 + scaling[:, None, :]) + offset[:, None, :],
        normed,
        inverse_std,
    )


def norm_back(grad_in, normed, inverse_std, gain_vec, scaling):
    factor = gain_vec * (1.0 + scaling[:, None, :])
    grad_normed = grad_in * factor
    grad_values = inverse_std * (
        grad_normed
        - jnp.mean(grad_normed, axis=-1, keepdims=True)
        - normed * jnp.mean(grad_normed * normed, axis=-1, keepdims=True)
    )
    grad_gain = jnp.sum(grad_in * normed * (1.0 + scaling[:, None, :]), axis=(0, 1))
    grad_scaling = jnp.sum(grad_in * normed * gain_vec, axis=1)
    grad_offset = jnp.sum(grad_in, axis=1)
    return (grad_values, grad_gain, grad_scaling, grad_offset)


def group_heads(field, per_group):
    seq_count, rows_count, _ = field.shape
    split = field.reshape(seq_count, rows_count, -1, HEAD_DIM).transpose(0, 2, 1, 3)
    return split.reshape(-1, per_group, rows_count, HEAD_DIM)


def ungroup_heads(field, seq_count):
    rows_count = field.shape[2]
    joined = field.reshape(seq_count, -1, rows_count, HEAD_DIM).transpose(0, 2, 1, 3)
    return joined.reshape(seq_count, rows_count, -1)


def attend_block(triple, scaling):
    queries, keys, values = triple
    scores = jnp.einsum("gqd,gkd->gqk", queries, keys, preferred_element_type=jnp.float32) * scaling
    top_score = jnp.max(scores, axis=-1, keepdims=True)
    raised = jnp.exp(scores - top_score)
    total = jnp.sum(raised, axis=-1, keepdims=True)
    weights = (raised / total).astype(jnp.bfloat16)
    attended = jnp.einsum("gqk,gkd->gqd", weights, values, preferred_element_type=jnp.float32)
    return (attended, (top_score + jnp.log(total))[..., 0])


def attend_back(bundle, scaling):
    queries, keys, values, grad_out, log_total = bundle
    scores = jnp.einsum("gqd,gkd->gqk", queries, keys, preferred_element_type=jnp.float32) * scaling
    weights = jnp.exp(scores - log_total[..., None])
    grad_values = jnp.einsum(
        "gqk,gqd->gkd", weights.astype(jnp.bfloat16), grad_out, preferred_element_type=jnp.float32
    )
    grad_weights = jnp.einsum("gqd,gkd->gqk", grad_out, values, preferred_element_type=jnp.float32)
    row_term = jnp.sum(weights * grad_weights, axis=-1, keepdims=True)
    grad_scores = (weights * (grad_weights - row_term)).astype(jnp.bfloat16)
    grad_queries = (
        jnp.einsum("gqk,gkd->gqd", grad_scores, keys, preferred_element_type=jnp.float32) * scaling
    )
    grad_keys = (
        jnp.einsum("gqk,gqd->gkd", grad_scores, queries, preferred_element_type=jnp.float32)
        * scaling
    )
    return (grad_queries, grad_keys, grad_values)


def gelu_slope(hidden):
    return (
        0.5 * (1.0 + lax.erf(hidden * 0.7071067811865476))
        + hidden * jnp.exp(-0.5 * hidden * hidden) * 0.3989422804014327
    )


def body(
    activations,
    timestep,
    positions,
    qkv_weight,
    out_weight,
    up_weight,
    down_weight,
    time_weight,
    norm_gains,
    cotangent,
):
    seq_count, tokens, width = activations.shape
    local_width = qkv_weight.shape[2]
    heads_local = local_width // HEAD_DIM
    per_group = min(heads_local, max(1, 512 // tokens))
    while heads_local % per_group:
        per_group -= 1
    scaling = HEAD_DIM ** (-0.5)
    full_qkv, full_out, full_up, full_down, full_time, full_gains = (
        lax.all_gather(qkv_weight, "shard", axis=1, tiled=True),
        lax.all_gather(out_weight, "shard", axis=1, tiled=True),
        lax.all_gather(up_weight, "shard", axis=0, tiled=True),
        lax.all_gather(down_weight, "shard", axis=1, tiled=True),
        lax.all_gather(time_weight, "shard", axis=2, tiled=True),
        lax.all_gather(norm_gains, "shard", axis=1, tiled=True),
    )
    gains_f = full_gains.astype(jnp.float32)
    embedding = embed_time(timestep)
    modulation = jnp.einsum(
        "sk,kcd->scd", embedding, full_time.astype(jnp.float32), precision=highest
    )
    cosines, sines = rotary_tables(positions)
    inputs_f = activations.astype(jnp.float32)
    first_out, normed_one, inverse_one = scaled_norm(
        inputs_f, gains_f[0], modulation[:, 0], modulation[:, 1]
    )
    first_low = first_out.astype(jnp.bfloat16)
    projected = jnp.einsum("std,cde->cste", first_low, full_qkv, preferred_element_type=jnp.float32)
    head_shape = (seq_count, tokens, heads_local, HEAD_DIM)
    query_rot = (
        rotate(projected[0].reshape(head_shape), cosines, sines)
        .reshape(seq_count, tokens, local_width)
        .astype(jnp.bfloat16)
    )
    key_rot = (
        rotate(projected[1].reshape(head_shape), cosines, sines)
        .reshape(seq_count, tokens, local_width)
        .astype(jnp.bfloat16)
    )
    value_low = projected[2].astype(jnp.bfloat16)
    keys_all, values_all = (
        lax.all_gather(key_rot, "ctx", axis=1, tiled=True),
        lax.all_gather(value_low, "ctx", axis=1, tiled=True),
    )
    query_groups = group_heads(query_rot, per_group)
    attended, log_total = lax.map(
        partial(attend_block, scaling=scaling),
        (query_groups, group_heads(keys_all, per_group), group_heads(values_all, per_group)),
    )
    attended_low = ungroup_heads(attended, seq_count).astype(jnp.bfloat16)
    branch_part = jnp.einsum(
        "ste,ed->std", attended_low, full_out, preferred_element_type=jnp.float32
    )
    middle = inputs_f + lax.psum(branch_part, "tp")
    second_out, normed_two, inverse_two = scaled_norm(
        middle, gains_f[1], modulation[:, 2], modulation[:, 3]
    )
    second_low = second_out.astype(jnp.bfloat16)
    hidden = jnp.einsum("std,df->stf", second_low, full_up, preferred_element_type=jnp.float32)
    activated = jax.nn.gelu(hidden, approximate=False).astype(jnp.bfloat16)
    mlp_part = jnp.einsum("stf,fd->std", activated, full_down, preferred_element_type=jnp.float32)
    output = (middle + lax.psum(mlp_part, "tp")).astype(jnp.bfloat16)
    back_qkv, back_out, back_up, back_down = (
        lax.all_gather(qkv_weight, "shard", axis=1, tiled=True),
        lax.all_gather(out_weight, "shard", axis=1, tiled=True),
        lax.all_gather(up_weight, "shard", axis=0, tiled=True),
        lax.all_gather(down_weight, "shard", axis=1, tiled=True),
    )
    keys_back, values_back = (
        lax.all_gather(key_rot, "ctx", axis=1, tiled=True),
        lax.all_gather(value_low, "ctx", axis=1, tiled=True),
    )
    grad_down = jnp.einsum("stf,std->fd", activated, cotangent, preferred_element_type=jnp.float32)
    grad_act = jnp.einsum("std,fd->stf", cotangent, back_down, preferred_element_type=jnp.float32)
    grad_hidden = (grad_act * gelu_slope(hidden)).astype(jnp.bfloat16)
    grad_up = jnp.einsum("std,stf->df", second_low, grad_hidden, preferred_element_type=jnp.float32)
    grad_second = lax.psum(
        jnp.einsum("stf,df->std", grad_hidden, back_up, preferred_element_type=jnp.float32), "tp"
    )
    grad_mid_norm, gain_two, scaling_two, offset_two = norm_back(
        grad_second, normed_two, inverse_two, gains_f[1], modulation[:, 2]
    )
    grad_middle = cotangent.astype(jnp.float32) + grad_mid_norm
    grad_branch = grad_middle.astype(jnp.bfloat16)
    grad_out = jnp.einsum(
        "ste,std->ed", attended_low, grad_branch, preferred_element_type=jnp.float32
    )
    grad_attended = jnp.einsum(
        "std,ed->ste", grad_branch, back_out, preferred_element_type=jnp.float32
    ).astype(jnp.bfloat16)
    grad_query_g, grad_key_g, grad_value_g = lax.map(
        partial(attend_back, scaling=scaling),
        (
            query_groups,
            group_heads(keys_back, per_group),
            group_heads(values_back, per_group),
            group_heads(grad_attended, per_group),
            log_total,
        ),
    )
    grad_key_all = ungroup_heads(grad_key_g, seq_count)
    grad_value_all = ungroup_heads(grad_value_g, seq_count)
    grad_key, grad_value = (
        lax.psum_scatter(grad_key_all, "ctx", scatter_dimension=1, tiled=True),
        lax.psum_scatter(grad_value_all, "ctx", scatter_dimension=1, tiled=True),
    )
    grad_query = ungroup_heads(grad_query_g, seq_count)
    query_back = unrotate(grad_query.reshape(head_shape), cosines, sines).reshape(
        seq_count, tokens, local_width
    )
    key_back = unrotate(grad_key.reshape(head_shape), cosines, sines).reshape(
        seq_count, tokens, local_width
    )
    grad_projected = jnp.stack([query_back, key_back, grad_value], axis=0).astype(jnp.bfloat16)
    grad_qkv = jnp.einsum(
        "std,cste->cde", first_low, grad_projected, preferred_element_type=jnp.float32
    )
    grad_first = lax.psum(
        jnp.einsum("cste,cde->std", grad_projected, back_qkv, preferred_element_type=jnp.float32),
        "tp",
    )
    grad_in_norm, gain_one, scaling_one, offset_one = norm_back(
        grad_first, normed_one, inverse_one, gains_f[0], modulation[:, 0]
    )
    input_grad = (grad_middle + grad_in_norm).astype(jnp.bfloat16)
    grad_modulation = jnp.stack([scaling_one, offset_one, scaling_two, offset_two], axis=1)
    grad_time = jnp.einsum("sk,scd->kcd", embedding, grad_modulation, precision=highest)
    grad_gains = jnp.stack([gain_one, gain_two], axis=0)
    shares = (
        lax.psum_scatter(grad_qkv, "shard", scatter_dimension=1, tiled=True),
        lax.psum_scatter(grad_out, "shard", scatter_dimension=1, tiled=True),
        lax.psum_scatter(grad_up, "shard", scatter_dimension=0, tiled=True),
        lax.psum_scatter(grad_down, "shard", scatter_dimension=1, tiled=True),
        lax.psum_scatter(grad_time, "shard", scatter_dimension=2, tiled=True),
        lax.psum_scatter(grad_gains, "shard", scatter_dimension=1, tiled=True),
    )
    shares = lax.psum((shares[0], shares[1], shares[2], shares[3], shares[4], shares[5]), "ctx")
    return (output, input_grad, shares[0], shares[1], shares[2], shares[3], shares[4], shares[5])


BF = jnp.bfloat16
F32 = jnp.float32
NN = (((1,), (0,)), ((), ()))
NT = (((1,), (1,)), ((), ()))
TN = (((0,), (0,)), ((), ()))
VMEM_BIG = 56 << 20
PER_US = 0.8e9


def mm(a, b, dims=NN):
    return lax.dot_general(a, b, dims, preferred_element_type=F32)


def cost(flops, nbytes=0, trans=0):
    return pl.CostEstimate(flops=int(flops), bytes_accessed=int(nbytes), transcendentals=int(trans))


def whole(array):
    zeros = (0,) * array.ndim
    return pl.BlockSpec(array.shape, lambda *_: zeros)


def call(kernel, name, grid, scalars, ins, in_specs, outs, out_specs, est, scratch=()):
    return pl.pallas_call(
        kernel,
        out_shape=outs,
        grid_spec=pltpu.PrefetchScalarGridSpec(
            num_scalar_prefetch=len(scalars),
            grid=grid,
            in_specs=in_specs,
            out_specs=out_specs,
            scratch_shapes=list(scratch),
        ),
        compiler_params=pltpu.CompilerParams(vmem_limit_bytes=VMEM_BIG),
        cost_estimate=est,
        name=name,
    )(*scalars, *ins)


def shape(dims, dtype):
    return jax.ShapeDtypeStruct(dims, dtype)


def cols(index, width):
    return pl.ds(pl.multiple_of(index * width, width), width)


def half_turn(values):
    lane = lax.broadcasted_iota(jnp.int32, values.shape, 1) % HEAD_DIM
    width = values.shape[1]
    up = pltpu.roll(values, HEAD_DIM // 2, 1)
    down = pltpu.roll(values, width - HEAD_DIM // 2, 1)
    return jnp.where(lane < HEAD_DIM // 2, down, up)


def spin(cos_ref, sin_ref, width):
    cosines, sines = cos_ref[...].T, sin_ref[...].T
    heads = width // HEAD_DIM
    return jnp.concatenate([cosines, cosines] * heads, axis=1), jnp.concatenate([-sines, sines] * heads, axis=1)


def pick(step, first_ref, second_ref, per_half):
    return jnp.where(step < per_half, first_ref[...], second_ref[...])


def own_map(per_half):
    return lambda i, *_: (jnp.minimum(i, per_half - 1), 0)


def other_map(per_half):
    return lambda i, *_: (jnp.maximum(i - per_half, 0), 0)


def project_kernel(per_half, blk, xa, xb, w0, w1, w2, w3, mods, cosb, sinb, h_ref, q_ref, k_ref, kt_ref, v_ref, vt_ref):
    x = pick(pl.program_id(0), xa, xb, per_half).astype(F32)
    x = x - jnp.mean(x, axis=1, keepdims=True)
    var = jnp.mean(x * x, axis=1, keepdims=True)
    n = x * lax.rsqrt(var + norm_epsilon)
    h_ref[...] = (n * mods[0:1, :] + mods[1:2, :]).astype(BF)
    rows = w0.shape[0]
    acc = None
    for j, w in enumerate((w0, w1, w2, w3)):
        part = mm(h_ref[:, cols(blk[j], rows)], w[...])
        acc = part if acc is None else acc + part
    wide = acc.shape[1] // 3
    cosines, sines = spin(cosb, sinb, wide)
    q = acc[:, :wide]
    k = acc[:, wide : 2 * wide]
    v = acc[:, 2 * wide :]
    q = q * cosines + half_turn(q) * sines
    k = k * cosines + half_turn(k) * sines
    q_ref[...] = q.astype(BF)
    k_ref[...] = k.astype(BF)
    kt_ref[...] = k.T.astype(BF)
    v_ref[...] = v.astype(BF)
    vt_ref[...] = v.T.astype(BF)


def project(blk, xa, xb, ws, mods, cosb, sinb, tile=256):
    half, width = xa.shape
    total = 2 * half
    wide = ws[0].shape[1] // 3
    per_half = half // tile
    row = lambda w: pl.BlockSpec((tile, w), lambda i, *_: (i, 0))
    turned = pl.BlockSpec((wide, tile), lambda i, *_: (0, i))
    return call(
        partial(project_kernel, per_half), "project", (total // tile,), (blk,),
        (xa, xb, *ws, mods, cosb, sinb),
        [pl.BlockSpec((tile, width), own_map(per_half)), pl.BlockSpec((tile, width), other_map(per_half)),
         *[whole(w) for w in ws], whole(mods), *[pl.BlockSpec((v.shape[0], tile), lambda i, *_: (0, i)) for v in (cosb, sinb)]],
        [shape((total, width), BF), shape((total, wide), BF), shape((total, wide), BF), shape((wide, total), BF),
         shape((total, wide), BF), shape((wide, total), BF)],
        [row(width), row(wide), row(wide), turned, row(wide), turned],
        cost(12.5 * PER_US),
    )


def attend_kernel(scale, q_ref, k_ref, vt_ref, o_ref, ot_ref, lse_ref):
    rows, wide = q_ref.shape
    q = q_ref[...]
    lane = lax.broadcasted_iota(jnp.int32, (rows, wide), 1) // HEAD_DIM
    def head(h, _):
        at = pl.ds(pl.multiple_of(h * HEAD_DIM, HEAD_DIM), HEAD_DIM)
        qh = jnp.where(lane == h, q, jnp.zeros_like(q))
        s = mm(k_ref[...], qh, NT) * scale
        top = jnp.max(s, axis=0, keepdims=True)
        p = jnp.exp(s - top)
        total = jnp.sum(p, axis=0, keepdims=True)
        ot_ref[at, :] = mm(vt_ref[at, :], p.astype(BF)) / total
        lse_ref[pl.ds(h, 1), :] = top + jnp.log(total)
        return 0

    lax.fori_loop(0, wide // HEAD_DIM, head, 0)
    o_ref[...] = ot_ref[...].T.astype(BF)


def attend(q, k, vt, first, rows, tile=1024):
    total, wide = q.shape
    heads = wide // HEAD_DIM
    skip = first // tile
    return call(
        partial(attend_kernel, HEAD_DIM**-0.5), "attend", (rows // tile,), (), (q, k, vt),
        [pl.BlockSpec((tile, wide), lambda i: (i + skip, 0)), whole(k), whole(vt)],
        [shape((rows, wide), BF), shape((wide, rows), F32), shape((heads, rows), F32)],
        [pl.BlockSpec((tile, wide), lambda i: (i, 0)), pl.BlockSpec((wide, tile), lambda i: (0, i)),
         pl.BlockSpec((heads, tile), lambda i: (0, i))],
        cost(10.0 * PER_US),
    )


def join_kernel(n_t, blk, blo, x_ref, *refs):
    near, far = refs[:n_t], refs[n_t : 2 * n_t]
    mine = refs[2 * n_t : 6 * n_t]
    theirs, mods, x1_ref, h_ref = refs[6 * n_t :]
    own = jnp.concatenate([o[...] for o in near], axis=1)
    oth = jnp.concatenate([o[...] for o in far], axis=1)
    span = theirs.shape[1]
    deep = own.shape[1]
    for k in range(4):
        at = cols(blk[k], span)
        w = jnp.concatenate([mine[4 * j + k][...] for j in range(n_t)], axis=0)
        x1_ref[:, at] = x_ref[:, at].astype(F32) + mm(own, w)
    for k in range(4):
        at = cols(blo[k], span)
        x1_ref[:, at] += mm(oth, theirs[k * deep : (k + 1) * deep, :])
    x = x1_ref[...]
    x = x - jnp.mean(x, axis=1, keepdims=True)
    var = jnp.mean(x * x, axis=1, keepdims=True)
    n = x * lax.rsqrt(var + norm_epsilon)
    h_ref[...] = (n * mods[2:3, :] + mods[3:4, :]).astype(BF)


def part_of(array, index, rows):
    return pl.BlockSpec((rows, array.shape[1]), lambda *_: (index, 0))


def stack_kernel(*refs):
    rows = refs[0].shape[0]
    for i, ref in enumerate(refs[:-1]):
        refs[-1][i * rows : (i + 1) * rows, :] = ref[...]


def stack_parts(arrays, rows):
    width = arrays[0].shape[1]
    return call(
        stack_kernel, "stack_parts", (1,), (), arrays,
        [part_of(v, v.shape[0] // rows - 1, rows) for v in arrays],
        shape((len(arrays) * rows, width), BF), pl.BlockSpec((len(arrays) * rows, width), lambda i: (0, 0)),
        cost(2.3 * PER_US),
    )


def join(blk, blo, x, near, far, slots, theirs, mods, tile=256):
    half, width = x.shape
    n_t = len(slots)
    wide = near[0].shape[1]
    row = lambda w: pl.BlockSpec((tile, w), lambda i, *_: (i, 0))
    flat = [w for slot in slots for w in slot]
    last_part = flat[0].shape[0] // wide - 1
    return call(
        partial(join_kernel, n_t), "join", (half // tile,), (blk, blo), (x, *near, *far, *flat, theirs, mods),
        [row(width), *[row(wide)] * (2 * n_t), *[part_of(w, last_part, wide) for w in flat], whole(theirs), whole(mods)],
        [shape((half, width), F32), shape((half, width), BF)],
        [row(width), row(width)],
        cost(8.5 * PER_US),
    )


def gelu_parts(u):
    half = 0.5 * (1.0 + lax.erf(u * 0.7071067811865476))
    slope = half + u * jnp.exp(-0.5 * u * u) * 0.3989422804014327
    return u * half, slope


def unpack_kernel(blk, *refs):
    ws, (up_ref, down_ref) = refs[:4], refs[-2:]
    span = ws[0].shape[1]
    for j, w in enumerate(ws):
        rows = pl.ds(pl.multiple_of(blk[j] * span, span), span)
        for b in range(2):
            up_ref[rows, b * span : (b + 1) * span] = w[b * span : (b + 1) * span, :]
        down_ref[:, cols(blk[j], span)] = w[2 * span : 4 * span, :]


def unpack(blk, slot, index, n_slots, before):
    span = slot[0].shape[1]
    width, hidden = 4 * span, 2 * span
    any_space = pl.BlockSpec(memory_space=pl.ANY)
    kept = () if before is None else before
    return pl.pallas_call(
        unpack_kernel,
        out_shape=[shape((n_slots * width, hidden), BF), shape((n_slots * hidden, width), BF)],
        grid_spec=pltpu.PrefetchScalarGridSpec(
            num_scalar_prefetch=1,
            grid=(1,),
            in_specs=[part_of(w, 0, width) for w in slot] + [any_space] * len(kept),
            out_specs=[pl.BlockSpec((width, hidden), lambda *_: (index, 0)), pl.BlockSpec((hidden, width), lambda *_: (index, 0))],
        ),
        input_output_aliases={5: 0, 6: 1} if kept else {},
        compiler_params=pltpu.CompilerParams(vmem_limit_bytes=VMEM_BIG),
        cost_estimate=cost(2.5 * PER_US),
        name="unpack",
    )(blk, *slot, *kept)


def mlp_kernel(per_half, n_slots, ha, hb, ca, cb, wu, wd, own_ref, oth_ref, g_ref, du_ref, h_buf, c_buf, du_buf):
    step = pl.program_id(0)
    width = ha.shape[1]
    hidden = wu.shape[1]
    h_buf[...] = pick(step, ha, hb, per_half)
    c_buf[...] = pick(step, ca, cb, per_half)

    def one(i, _):
        at = cols(i, hidden)
        u = mm(h_buf[...], wu[pl.ds(pl.multiple_of(i * width, width), width), :])
        dg = mm(c_buf[...], wd[pl.ds(pl.multiple_of(i * hidden, hidden), hidden), :], NT)
        g, slope = gelu_parts(u)
        g_ref[:, at] = g.astype(BF)
        du_buf[:, at] = (dg * slope).astype(BF)
        return 0

    lax.fori_loop(0, n_slots, one, 0)
    du_ref[...] = du_buf[:, :hidden]
    chunk = min(512, width)
    for n in range(width // chunk):
        at = slice(n * chunk, (n + 1) * chunk)
        acc = None
        for i in range(n_slots):
            part = mm(du_buf[:, i * hidden : (i + 1) * hidden], wu[i * width + n * chunk : i * width + (n + 1) * chunk, :], NT)
            acc = part if acc is None else acc + part

        @pl.when(step < per_half)
        def _():
            own_ref[:, at] = acc

        @pl.when(step >= per_half)
        def _():
            oth_ref[:, at] = acc.astype(BF)


def mlp(ha, hb, ca, cb, wu, wd, tile=512):
    half, width = ha.shape
    total = 2 * half
    per_half = half // tile
    hidden = wu.shape[1]
    n_slots = wu.shape[0] // width
    row = lambda w: pl.BlockSpec((tile, w), lambda i, *_: (i, 0))
    mine = pl.BlockSpec((tile, width), own_map(per_half))
    theirs = pl.BlockSpec((tile, width), other_map(per_half))
    return call(
        partial(mlp_kernel, per_half, n_slots), "mlp", (total // tile,), (), (ha, hb, ca, cb, wu, wd),
        [mine, theirs, mine, theirs, whole(wu), whole(wd)],
        [shape((half, width), F32), shape((half, width), BF), shape((total, n_slots * hidden), BF), shape((total, hidden), BF)],
        [mine, theirs, row(n_slots * hidden), row(hidden)],
        cost(42.0 * PER_US),
        [pltpu.VMEM((tile, width), BF), pltpu.VMEM((tile, width), BF), pltpu.VMEM((tile, n_slots * hidden), BF)],
    )


def lift_kernel(per_half, g_in, wd, own_ref, oth_ref):
    step = pl.program_id(0)
    chunk = 512
    for n in range(wd.shape[1] // chunk):
        at = slice(n * chunk, (n + 1) * chunk)
        part = mm(g_in[...], wd[:, at])

        @pl.when(step < per_half)
        def _():
            own_ref[:, at] = part

        @pl.when(step >= per_half)
        def _():
            oth_ref[:, at] = part.astype(BF)


def lift(g, wd, tile=512):
    total = g.shape[0]
    width = wd.shape[1]
    half = total // 2
    per_half = half // tile
    return call(
        partial(lift_kernel, per_half), "lift", (total // tile,), (), (g, wd),
        [pl.BlockSpec((tile, g.shape[1]), lambda i, *_: (i, 0)), whole(wd)],
        [shape((half, width), F32), shape((half, width), BF)],
        [pl.BlockSpec((tile, width), own_map(per_half)), pl.BlockSpec((tile, width), other_map(per_half))],
        cost(14.0 * PER_US),
    )


def norm_turn(dh, x, factor):
    x = x - jnp.mean(x, axis=1, keepdims=True)
    var = jnp.mean(x * x, axis=1, keepdims=True)
    r = lax.rsqrt(var + norm_epsilon)
    n = x * r
    dn = dh * factor
    dx = r * (dn - jnp.mean(dn, axis=1, keepdims=True) - n * jnp.mean(dn * n, axis=1, keepdims=True))
    return dx, jnp.sum(dh * n, axis=0, keepdims=True), jnp.sum(dh, axis=0, keepdims=True)


def turn_kernel(blk, blo, dh_ref, in_ref, x_ref, c_ref, mods, a0, a1, a2, a3, b_ref, dx_ref, da_ref, own_ref, oth_ref, sums):
    dh = dh_ref[...] + in_ref[...].astype(F32)
    dx, s1, s0 = norm_turn(dh, x_ref[...], mods[2:3, :])
    dx = dx + c_ref[...].astype(F32)
    dx_ref[...] = dx
    da_ref[...] = dx.astype(BF)
    wide = own_ref.shape[1]
    span = a0.shape[1]
    step = b_ref.shape[0] // 4
    theirs = [b_ref[k * step : k * step + wide, :] for k in range(4)]
    for order, ws, out in ((blk, [a[...] for a in (a0, a1, a2, a3)], own_ref), (blo, theirs, oth_ref)):
        acc = None
        for j, w in enumerate(ws):
            part = mm(da_ref[:, cols(order[j], span)], w, NT)
            acc = part if acc is None else acc + part
        out[...] = acc.astype(BF)

    @pl.when(pl.program_id(0) == 0)
    def _():
        sums[...] = jnp.zeros_like(sums)

    sums[0:1, :] += s1
    sums[1:2, :] += s0


def turn(blk, blo, dh, received, x1, cot, mods, wa, wb, wide, tile=256):
    half, width = x1.shape
    row = lambda w: pl.BlockSpec((tile, w), lambda i, *_: (i, 0))
    return call(
        turn_kernel, "turn", (half // tile,), (blk, blo), (dh, received, x1, cot, mods, *wa, wb),
        [row(width)] * 4 + [whole(mods), *[part_of(w, w.shape[0] // wide - 1, wide) for w in wa], whole(wb)],
        [shape((half, width), F32), shape((half, width), BF), shape((half, wide), BF), shape((half, wide), BF), shape((8, width), F32)],
        [row(width), row(width), row(wide), row(wide), pl.BlockSpec((8, width), lambda i, *_: (0, 0))],
        cost(11.3 * PER_US),
    )


def attend_back_kernel(scale, tk, per_half, q_ref, da_ref, db_ref, ota_ref, otb_ref, la_ref, lb_ref, cos_ref, sin_ref, k_ref, v_ref, kt_ref, cosb, sinb, out_ref, dqt, dk_acc, dv_acc):
    rows, wide = q_ref.shape
    total = k_ref.shape[0]
    step = pl.program_id(0)
    q = q_ref[...]
    do = pick(step, da_ref, db_ref, per_half)
    lse = pick(step, la_ref, lb_ref, per_half)
    lane = lax.broadcasted_iota(jnp.int32, (rows, wide), 1) // HEAD_DIM
    heads = wide // HEAD_DIM
    qs = [jnp.where(lane == h, q, jnp.zeros_like(q)) for h in range(heads)]
    ds = [jnp.where(lane == h, do, jnp.zeros_like(do)) for h in range(heads)]
    od = do.astype(F32).T * pick(step, ota_ref, otb_ref, per_half)
    deltas = [jnp.sum(od[h * HEAD_DIM : (h + 1) * HEAD_DIM, :], axis=0, keepdims=True) for h in range(heads)]

    @pl.when(step == 0)
    def _():
        dk_acc[...] = jnp.zeros_like(dk_acc)
        dv_acc[...] = jnp.zeros_like(dv_acc)

    dqt[...] = jnp.zeros_like(dqt)
    for j in range(total // tk):
        at = slice(j * tk, (j + 1) * tk)
        kj, vj = k_ref[at, :], v_ref[at, :]
        for h in range(heads):
            hs = slice(h * HEAD_DIM, (h + 1) * HEAD_DIM)
            s = mm(kj, qs[h], NT) * scale
            p = jnp.exp(s - lse[h : h + 1, :])
            dp = mm(vj, ds[h], NT)
            dsc = (p * (dp - deltas[h])).astype(BF)
            dv_acc[at, :] += mm(p.astype(BF), ds[h])
            dk_acc[at, :] += mm(dsc, qs[h])
            dqt[hs, :] += mm(kt_ref[hs, at], dsc)
    dq = dqt[...].T * scale
    cosines, sines = spin(cos_ref, sin_ref, wide)
    out_ref[pl.ds(pl.multiple_of(step * rows, rows), rows), :wide] = (dq * cosines - half_turn(dq) * sines).astype(BF)

    @pl.when(step == pl.num_programs(0) - 1)
    def _():
        dk = dk_acc[...] * scale
        cosines, sines = spin(cosb, sinb, wide)
        out_ref[:, wide : 2 * wide] = (dk * cosines - half_turn(dk) * sines).astype(BF)
        out_ref[:, 2 * wide :] = dv_acc[...].astype(BF)


def attend_back_call(q, do_a, do_b, ots, lses, k, v, kt, cosb, sinb, tile=512, tk=512):
    total, wide = q.shape
    heads = wide // HEAD_DIM
    per_half = total // 2 // tile
    row = pl.BlockSpec((tile, wide), lambda i: (i, 0))
    lanes_a = lambda h: pl.BlockSpec((h, tile), lambda i: (0, jnp.minimum(i, per_half - 1)))
    lanes_b = lambda h: pl.BlockSpec((h, tile), lambda i: (0, jnp.maximum(i - per_half, 0)))
    full = pl.BlockSpec((total, wide), lambda i: (0, 0))
    turned = pl.BlockSpec((cosb.shape[0], tile), lambda i: (0, i))
    return call(
        partial(attend_back_kernel, HEAD_DIM**-0.5, tk, per_half), "attend_back", (total // tile,), (),
        (q, do_a, do_b, *ots, *lses, cosb, sinb, k, v, kt, cosb, sinb),
        [row, pl.BlockSpec((tile, wide), own_map(per_half)), pl.BlockSpec((tile, wide), other_map(per_half)),
         lanes_a(wide), lanes_b(wide), lanes_a(heads), lanes_b(heads), turned, turned, full, full, whole(kt), whole(cosb), whole(sinb)],
        shape((total, 3 * wide), BF),
        pl.BlockSpec((total, 3 * wide), lambda i: (0, 0)),
        cost(29.0 * PER_US),
        [pltpu.VMEM((wide, tile), F32), pltpu.VMEM((total, wide), F32), pltpu.VMEM((total, wide), F32)],
    )


def gather_kernel(n, blk, *refs):
    rs = refs[:n]
    ws = [refs[n + 4 * i : n + 4 * i + 4] for i in range(n)]
    own_ref, oth_ref = refs[5 * n :]
    rows = own_ref.shape[0]
    span = ws[0][0].shape[0]
    for j in range(4):
        acc = None
        for r, w in zip(rs, ws):
            part = mm(r[...], w[j][...], NT)
            acc = part if acc is None else acc + part
        own_ref[:, cols(blk[j], span)] = acc[:rows]
        oth_ref[:, cols(blk[j], span)] = acc[rows:].astype(BF)


def gather(blk, rs, first, others, width):
    n = len(rs)
    rows, span = rs[0].shape[0] // 2, first[0].shape[0]
    back = pl.BlockSpec((rows, width), lambda i, *_: (0, 0))
    return call(
        partial(gather_kernel, n), "gather", (1,), (blk,), (*rs, *first, *(others * (n - 1))),
        [*[whole(r) for r in rs], *[whole(w) for w in first], *[part_of(w, i, span) for i in range(n - 1) for w in others]],
        [shape((rows, width), F32), shape((rows, width), BF)],
        [back, back],
        cost(6.5 * PER_US),
    )


def last_kernel(at, dh_ref, in_ref, x_ref, dx_ref, mods, out_ref, sums):
    dx, s1, s0 = norm_turn(dh_ref[...] + in_ref[...].astype(F32), x_ref[...].astype(F32), mods[0:1, :])
    out_ref[...] = (dx + dx_ref[...]).astype(BF)
    sums[...] = jnp.zeros_like(sums)
    sums[0:1, :] = s1
    sums[1:2, :] = s0


def last(at, dh, received, x, dx, mods):
    rows, width = dh.shape
    block = pl.BlockSpec((rows, width), lambda i, at: (at[0], 0))
    return call(
        last_kernel, "last", (1,), (at,), (dh, received, x, dx, mods),
        [whole(dh), whole(received), block, block, whole(mods)],
        [shape((rows, width), BF), shape((8, width), F32)],
        [pl.BlockSpec((rows, width), lambda i, *_: (0, 0)), pl.BlockSpec((8, width), lambda i, *_: (0, 0))],
        cost(3.5 * PER_US),
    )


def after(values, *events):
    return lax.optimization_barrier((values, events))[0]


def fast_body(
    activations, timestep, positions, qkv_weight, out_weight, up_weight, down_weight, time_weight, norm_gains, cotangent
):
    n_s, n_t = lax.axis_size("shard"), lax.axis_size("tp")
    s, c, t = lax.axis_index("shard"), lax.axis_index("ctx"), lax.axis_index("tp")
    x_own = activations[0]
    cot_own = cotangent[0]
    half, width = x_own.shape
    span = width // n_s
    quarter = half // n_t
    near = jnp.where(c == 0, 1, 2)
    blk = jnp.stack([s, s ^ near, s ^ (3 - near), s ^ 3]).astype(jnp.int32)
    blo = jnp.stack([s, s ^ (3 - near), s ^ near, s ^ 3]).astype(jnp.int32)
    pairs_a = [(v * 2 + k, (v ^ (1 + k)) * 2 + k) for v in range(n_s) for k in range(2)]
    pairs_b = [(v * 2 + k, (v ^ (2 - k)) * 2 + k) for v in range(n_s) for k in range(2)]
    cycle = [(i, (i + 1) % n_t) for i in range(n_t)]
    swap = lambda v: lax.ppermute(v, "ctx", [(0, 1), (1, 0)])
    move_a = lambda v: lax.ppermute(v, ("shard", "ctx"), pairs_a)
    move_b = lambda v: lax.ppermute(v, ("shard", "ctx"), pairs_b)
    upward = lambda v: lax.ppermute(v, "tp", cycle)

    def by_z(v, d):
        return lax.ppermute(v, "tp", [(i, (i + d) % n_t) for i in range(n_t)])

    def turn_shard(v, d):
        return lax.ppermute(v, "shard", [(i, (i + d) % n_s) for i in range(n_s)])

    def half_of(v, axis):
        size = v.shape[axis] // 2
        return lax.dynamic_slice_in_dim(v, c * size, size, axis)

    def both(v, axis):
        other = swap(v)
        return jnp.where(c == 0, jnp.concatenate([v, other], axis), jnp.concatenate([other, v], axis))

    x_oth = swap(x_own)

    def shard_pair(v, bit):
        return lax.ppermute(v, "shard", [(i, i ^ bit) for i in range(n_s)])

    gains = norm_gains.astype(F32)
    small = jnp.concatenate([gains, jnp.broadcast_to(timestep.astype(F32)[:, None], (1, span))], axis=0)
    small_two = jnp.concatenate([small, shard_pair(small, 1)], axis=0)
    small_four = jnp.concatenate([small_two, shard_pair(small_two, 2)], axis=0)
    smalls = [small_four[3 * i : 3 * i + 3] for i in range(n_s)]

    wide = qkv_weight.shape[2] // 2
    qkv_half = half_of(qkv_weight, 2)
    qkv_share = jnp.concatenate([qkv_half[0], qkv_half[1], qkv_half[2]], axis=1)
    qkv_a, qkv_b = move_a(qkv_share), move_b(qkv_share)
    qkv_c = move_b(qkv_a)
    w_qkv = [qkv_share, qkv_a, qkv_b, qkv_c]
    pos_own = positions.astype(F32)
    pos_oth = swap(pos_own)

    up_half = half_of(up_weight, 1)
    down_half = half_of(down_weight, 0)
    pack = jnp.concatenate([up_half[:, :span], up_half[:, span:], down_half, half_of(out_weight, 0)], axis=0)
    z1 = upward(pack)
    pack_go = after(pack, qkv_a, qkv_b)
    m0a, m0b = move_a(pack_go), move_b(pack_go)

    steps = small_four[2::3, 0]
    embedding = embed_time(steps)
    parts = jnp.einsum("sk,kcd->scd", embedding, time_weight.astype(F32), precision=highest)
    parts_x = shard_pair(jnp.concatenate([parts[1], parts[3]], axis=0), 1)
    parts_y = shard_pair(after(jnp.concatenate([parts[2], parts_x[4:]], axis=0), qkv_c), 2)
    parts_in = [parts[0], parts_x[:4], parts_y[:4], parts_y[4:]]
    gain_full = jnp.zeros((2, width), F32)
    mod_full = jnp.zeros((4, width), F32)
    for i in range(n_s):
        gain_full = lax.dynamic_update_slice_in_dim(gain_full, smalls[i][:2], (s ^ i) * span, 1)
        mod_full = lax.dynamic_update_slice_in_dim(mod_full, parts_in[i], (s ^ i) * span, 1)
    factor_one = gain_full[0] * (1.0 + mod_full[0])
    factor_two = gain_full[1] * (1.0 + mod_full[2])
    zero = jnp.zeros_like(factor_one)
    mods = jnp.stack([factor_one, mod_full[1], factor_two, mod_full[3], zero, zero, zero, zero])

    half_width = HEAD_DIM // 2
    frequency = jnp.exp(-math.log(10000.0) * jnp.arange(half_width, dtype=F32) / half_width)
    angles = frequency[:, None] * jnp.concatenate([pos_own, pos_oth], axis=1)
    cosb, sinb = jnp.cos(angles), jnp.sin(angles)

    z1 = after(z1, parts_y)
    z2 = upward(z1)
    m1a, m1b = move_a(z1), move_b(z1)
    x_now = after(x_own, z1)
    h1, q, k, kt, v, vt = project(blk, x_now, x_oth, w_qkv, mods, cosb, sinb)
    m0a_late, m1a_late, z2_late = after((m0a, m1a, z2), q, m0b)
    m0c, m1c, z3 = move_b(m0a_late), move_b(m1a_late), upward(z2_late)
    o_far, ot_far, lse_far = attend(q, k, vt, half, half)
    o_got = swap(o_far)
    z2_late = after(z2, o_far, m0c, m1b)
    m2a, m2b = move_a(z2_late), move_b(z2_late)
    far = [after(o_got, z3)]
    far.append(upward(far[0]))
    o_near, ot_near, lse_near = attend(after(q, o_far), k, vt, 0, half)
    wu, wd = unpack(blk, [pack, m0a, m0b, m0c], 0, n_t, None)
    z3_late, m2a_late, far_go, near_go = after((z3, m2a, far[1], o_near), m2b, m1c)
    m3a, m3b, m2c = move_a(z3_late), move_b(z3_late), move_b(m2a_late)
    near = [near_go, upward(near_go)]
    far.append(upward(far_go))
    m3a_late, near_go, far_go, m1c_late = after((m3a, near[1], far[2], m1c), m2c, m3b)
    m3c = move_b(m3a_late)
    near.append(upward(near_go))
    far.append(upward(far_go))
    wu, wd = unpack(blk, [z1, m1a, m1b, m1c_late], 1, n_t, (wu, wd))
    near_go, m3c, far_done = after((near[2], m3c, far[3]), wu)
    near.append(upward(near_go))
    far[3] = far_done
    wu, wd = unpack(blk, [z2, m2a, m2b, after(m2c, m3c)], 2, n_t, (wu, wd))
    wu, wd = unpack(blk, [z3, m3a, m3b, m3c], 3, n_t, (wu, wd))
    cot_oth = swap(cot_own)
    w_mlp = [[pack, m0a, m0b, m0c], [z1, m1a, m1b, m1c], [z2, m2a, m2b, m2c], [z3, m3a, m3b, m3c]]
    out_other = swap(stack_parts([w_mlp[j][i] for i in range(n_s) for j in range(n_t)], wide))

    x1, h2 = join(blk, blo, after(x_own, wu), near, far, w_mlp, out_other, mods)
    h2_oth = swap(h2)
    dh2, dh2_send, g_all, du0 = mlp(h2, h2_oth, cot_own, cot_oth, wu, wd)
    qkv_again = after(qkv_share, h2_oth)
    qz_pack = jnp.concatenate([by_z(qkv_again, d) for d in range(1, n_t)], axis=0)
    dh2_in = swap(after(dh2_send, qz_pack))
    qz_pack = after(qz_pack, dh2_in)
    qza, qzb = move_a(qz_pack), move_b(qz_pack)
    dx1, da, do_own, do_send, sums_two = turn(blk, blo, dh2, dh2_in, x1, cot_own, mods, w_mlp[0], out_other, wide)
    do_got = swap(do_send)
    qza, qzb, do_got = after((qza, qzb, do_got), da)
    qzc = move_b(qza)
    w_back = [qz_pack, qza, qzb, qzc]
    dqkv = attend_back_call(q, do_own, do_got, (ot_near, ot_far), (lse_near, lse_far), k, v, kt, cosb, sinb)

    dqkv = dqkv.reshape(2, half, 3 * wide)

    def tokens_of(d):
        return lax.dynamic_slice_in_dim(dqkv, ((t + d) % n_t) * quarter, quarter, 1).reshape(2 * quarter, 3 * wide)

    got = [tokens_of(0), by_z(tokens_of(1), 1)]

    h2_late, h2o_late, du0_late, g_late = after((h2, h2_oth, du0, g_all), tokens_of(1))
    g_up = mm(jnp.concatenate([h2_late, h2o_late], axis=0), du0_late, TN)
    g_down = mm(g_late[:, : 2 * span], jnp.concatenate([cot_own, cot_oth], axis=0), TN)
    got.append(by_z(after(tokens_of(2), got[1], g_up, g_down), 2))
    g_later = after(g_late, got[1], g_up, g_down)
    y_own, y_send = lift(g_later, wd)
    got.append(by_z(after(tokens_of(3), got[2], y_own), 3))

    def mlp_piece(j):
        ups = lax.dynamic_slice_in_dim(g_up, blk[j] * span, span, 0)
        downs = lax.dynamic_slice_in_dim(g_down, blk[j] * span, span, 1)
        outs = lax.dynamic_slice_in_dim(g_out, blk[j] * span, span, 1)
        return jnp.concatenate([ups[:, :span], ups[:, span:], downs, outs], axis=0)

    def reduce_first(pieces):
        return move_b(jnp.concatenate([pieces(2), pieces(3)], axis=0).astype(BF))

    def reduce_last(pieces, came):
        rows = came.shape[0] // 2
        return pieces(0) + came[:rows].astype(F32) + move_a((pieces(1) + came[rows:].astype(F32)).astype(BF)).astype(F32)

    dh1_own, dh1_send = gather(blk, got, w_qkv, w_back, width)
    dh1_got = swap(dh1_send)

    at = t.astype(jnp.int32).reshape(1)
    grad_mine, sums_one = last(at, dh1_own, dh1_got, x_own, dx1, mods)
    slots = [grad_mine, upward(grad_mine)]
    h1_late, dqkv_late, da_late, g_up, g_down, y_send = after((h1, dqkv, da, g_up, g_down, y_send), grad_mine)
    g_out = mm(o_near, da_late, TN) + swap(mm(o_got, da_late, TN).astype(BF)).astype(F32)
    mlp_came = reduce_first(mlp_piece)
    g_qkv = mm(h1_late, dqkv_late.reshape(2 * half, 3 * wide), TN)
    qkv_piece = lambda j: lax.dynamic_slice_in_dim(g_qkv, blk[j] * span, span, 0)
    y_got = swap(y_send)
    qkv_came = reduce_first(qkv_piece)
    keep = jnp.where(t == 0, 1.0, 0.0)
    tally = jnp.concatenate([sums_one[:2], sums_two[:2] * keep], axis=0)
    tally = tally + swap(tally)
    slots[1], tally, mlp_came, qkv_came, y_got = after((slots[1], tally, mlp_came, qkv_came, y_got), g_qkv)
    slots.append(upward(slots[1]))
    full = tally
    for bit in (1, 2):
        full = full + lax.ppermute(full, "tp", [(i, i ^ bit) for i in range(n_t)])
    rows = mlp_came.shape[0] // 2
    mlp_base = mlp_piece(0) + mlp_came[:rows].astype(F32)
    mlp_last = move_a((mlp_piece(1) + mlp_came[rows:].astype(F32)).astype(BF))
    rows = qkv_came.shape[0] // 2
    qkv_base = qkv_piece(0) + qkv_came[:rows].astype(F32)
    qkv_last = move_a((qkv_piece(1) + qkv_came[rows:].astype(F32)).astype(BF))
    output = (x1 + y_own + y_got.astype(F32)).astype(BF)

    slots[2], qkv_last, mlp_last, full = after((slots[2], qkv_last, mlp_last, full), output)
    slots.append(upward(slots[2]))
    done = mlp_base + mlp_last.astype(F32)
    grad_up = both(jnp.concatenate([done[:span], done[span : 2 * span]], axis=1), 1)
    grad_down = both(done[2 * span : 4 * span], 0)
    grad_out = both(done[4 * span :], 0)
    done_qkv = qkv_base + qkv_last.astype(F32)
    grad_qkv = both(jnp.stack([done_qkv[:, i * wide : (i + 1) * wide] for i in range(3)]), 2)
    dmods = jnp.stack([full[0] * gain_full[0], full[1], full[2] * gain_full[1], full[3],
                       full[0] * (1.0 + mod_full[0]), full[2] * (1.0 + mod_full[2])])
    blocks = [lax.dynamic_slice_in_dim(dmods, (s ^ i) * span, span, 1) for i in range(n_s)]
    blocks_x = shard_pair(jnp.concatenate([blocks[1], blocks[3]], axis=0), 1)
    blocks_y = shard_pair(jnp.concatenate([blocks[2], blocks_x[6:]], axis=0), 2)
    seqs = jnp.stack([blocks[0], blocks_x[:6], blocks_y[:6], blocks_y[6:]])
    grad_time = jnp.einsum("sk,scd->kcd", embedding, seqs[:, :4], precision=highest)
    grad_gains = jnp.sum(seqs[:, 4:], axis=0)
    slots[3] = after(slots[3], grad_qkv, grad_up, grad_down, grad_out, grad_time, grad_gains)
    input_grad = jnp.zeros((half, width), BF)
    for j in range(n_t):
        input_grad = lax.dynamic_update_slice_in_dim(input_grad, slots[j], ((t - j) % n_t) * quarter, 0)
    return (output[None], input_grad[None], grad_qkv, grad_out, grad_up, grad_down, grad_time, grad_gains)


def solution(mesh):
    sizes = dict(mesh.shape)
    chosen = fast_body if (sizes["shard"], sizes["ctx"], sizes["tp"]) == (4, 2, 4) else body
    placed = (
        P("shard", "ctx", None),
        P("shard"),
        P("shard", "ctx"),
        P(None, "shard", "tp"),
        P("tp", "shard"),
        P("shard", "tp"),
        P("tp", "shard"),
        P(None, None, "shard"),
        P(None, "shard"),
        P("shard", "ctx", None),
    )
    return jax.shard_map(
        chosen,
        mesh=mesh,
        in_specs=placed,
        out_specs=(
            P("shard", "ctx", None),
            P("shard", "ctx", None),
            P(None, "shard", "tp"),
            P("tp", "shard"),
            P("shard", "tp"),
            P("tp", "shard"),
            P(None, None, "shard"),
            P(None, "shard"),
        ),
        check_vma=False,
    )
```

```python
from functools import partial
import math

import jax
import jax.numpy as jnp
from jax import lax
from jax.experimental import pallas as pl
from jax.experimental.pallas import tpu as pltpu
from jax.sharding import PartitionSpec as P

HEAD_DIM = 64
TEMB = 256


highest = lax.Precision.HIGHEST
norm_epsilon = 1e-05


def embed_time(timestep):
    half_width = TEMB // 2
    frequency = jnp.exp(-math.log(10000.0) * jnp.arange(half_width, dtype=jnp.float32) / half_width)
    angles = timestep.astype(jnp.float32)[:, None] * frequency[None, :]
    return jnp.concatenate([jnp.sin(angles), jnp.cos(angles)], axis=-1)


def rotary_tables(positions):
    half_width = HEAD_DIM // 2
    frequency = jnp.exp(-math.log(10000.0) * jnp.arange(half_width, dtype=jnp.float32) / half_width)
    angles = positions.astype(jnp.float32)[..., None] * frequency
    return (jnp.cos(angles), jnp.sin(angles))


def rotate(heads_in, cosines, sines):
    half_width = HEAD_DIM // 2
    first = heads_in[..., :half_width]
    second = heads_in[..., half_width:]
    cos_wide = cosines[..., None, :]
    sin_wide = sines[..., None, :]
    return jnp.concatenate(
        [first * cos_wide - second * sin_wide, second * cos_wide + first * sin_wide], axis=-1
    )


def unrotate(heads_in, cosines, sines):
    half_width = HEAD_DIM // 2
    first = heads_in[..., :half_width]
    second = heads_in[..., half_width:]
    cos_wide = cosines[..., None, :]
    sin_wide = sines[..., None, :]
    return jnp.concatenate(
        [first * cos_wide + second * sin_wide, second * cos_wide - first * sin_wide], axis=-1
    )


def scaled_norm(values, gain_vec, scaling, offset):
    centered = values - jnp.mean(values, axis=-1, keepdims=True)
    variance = jnp.mean(centered * centered, axis=-1, keepdims=True)
    inverse_std = lax.rsqrt(variance + norm_epsilon)
    normed = centered * inverse_std
    return (
        normed * gain_vec * (1.0 + scaling[:, None, :]) + offset[:, None, :],
        normed,
        inverse_std,
    )


def norm_back(grad_in, normed, inverse_std, gain_vec, scaling):
    factor = gain_vec * (1.0 + scaling[:, None, :])
    grad_normed = grad_in * factor
    grad_values = inverse_std * (
        grad_normed
        - jnp.mean(grad_normed, axis=-1, keepdims=True)
        - normed * jnp.mean(grad_normed * normed, axis=-1, keepdims=True)
    )
    grad_gain = jnp.sum(grad_in * normed * (1.0 + scaling[:, None, :]), axis=(0, 1))
    grad_scaling = jnp.sum(grad_in * normed * gain_vec, axis=1)
    grad_offset = jnp.sum(grad_in, axis=1)
    return (grad_values, grad_gain, grad_scaling, grad_offset)


def group_heads(field, per_group):
    seq_count, rows_count, _ = field.shape
    split = field.reshape(seq_count, rows_count, -1, HEAD_DIM).transpose(0, 2, 1, 3)
    return split.reshape(-1, per_group, rows_count, HEAD_DIM)


def ungroup_heads(field, seq_count):
    rows_count = field.shape[2]
    joined = field.reshape(seq_count, -1, rows_count, HEAD_DIM).transpose(0, 2, 1, 3)
    return joined.reshape(seq_count, rows_count, -1)


def attend_block(triple, scaling):
    queries, keys, values = triple
    scores = jnp.einsum("gqd,gkd->gqk", queries, keys, preferred_element_type=jnp.float32) * scaling
    top_score = jnp.max(scores, axis=-1, keepdims=True)
    raised = jnp.exp(scores - top_score)
    total = jnp.sum(raised, axis=-1, keepdims=True)
    weights = (raised / total).astype(jnp.bfloat16)
    attended = jnp.einsum("gqk,gkd->gqd", weights, values, preferred_element_type=jnp.float32)
    return (attended, (top_score + jnp.log(total))[..., 0])


def attend_back(bundle, scaling):
    queries, keys, values, grad_out, log_total = bundle
    scores = jnp.einsum("gqd,gkd->gqk", queries, keys, preferred_element_type=jnp.float32) * scaling
    weights = jnp.exp(scores - log_total[..., None])
    grad_values = jnp.einsum(
        "gqk,gqd->gkd", weights.astype(jnp.bfloat16), grad_out, preferred_element_type=jnp.float32
    )
    grad_weights = jnp.einsum("gqd,gkd->gqk", grad_out, values, preferred_element_type=jnp.float32)
    row_term = jnp.sum(weights * grad_weights, axis=-1, keepdims=True)
    grad_scores = (weights * (grad_weights - row_term)).astype(jnp.bfloat16)
    grad_queries = (
        jnp.einsum("gqk,gkd->gqd", grad_scores, keys, preferred_element_type=jnp.float32) * scaling
    )
    grad_keys = (
        jnp.einsum("gqk,gqd->gkd", grad_scores, queries, preferred_element_type=jnp.float32)
        * scaling
    )
    return (grad_queries, grad_keys, grad_values)


def gelu_slope(hidden):
    return (
        0.5 * (1.0 + lax.erf(hidden * 0.7071067811865476))
        + hidden * jnp.exp(-0.5 * hidden * hidden) * 0.3989422804014327
    )


def body(
    activations,
    timestep,
    positions,
    qkv_weight,
    out_weight,
    up_weight,
    down_weight,
    time_weight,
    norm_gains,
    cotangent,
):
    seq_count, tokens, width = activations.shape
    local_width = qkv_weight.shape[2]
    heads_local = local_width // HEAD_DIM
    per_group = min(heads_local, max(1, 512 // tokens))
    while heads_local % per_group:
        per_group -= 1
    scaling = HEAD_DIM ** (-0.5)
    full_qkv, full_out, full_up, full_down, full_time, full_gains = (
        lax.all_gather(qkv_weight, "shard", axis=1, tiled=True),
        lax.all_gather(out_weight, "shard", axis=1, tiled=True),
        lax.all_gather(up_weight, "shard", axis=0, tiled=True),
        lax.all_gather(down_weight, "shard", axis=1, tiled=True),
        lax.all_gather(time_weight, "shard", axis=2, tiled=True),
        lax.all_gather(norm_gains, "shard", axis=1, tiled=True),
    )
    gains_f = full_gains.astype(jnp.float32)
    embedding = embed_time(timestep)
    modulation = jnp.einsum(
        "sk,kcd->scd", embedding, full_time.astype(jnp.float32), precision=highest
    )
    cosines, sines = rotary_tables(positions)
    inputs_f = activations.astype(jnp.float32)
    first_out, normed_one, inverse_one = scaled_norm(
        inputs_f, gains_f[0], modulation[:, 0], modulation[:, 1]
    )
    first_low = first_out.astype(jnp.bfloat16)
    projected = jnp.einsum("std,cde->cste", first_low, full_qkv, preferred_element_type=jnp.float32)
    head_shape = (seq_count, tokens, heads_local, HEAD_DIM)
    query_rot = (
        rotate(projected[0].reshape(head_shape), cosines, sines)
        .reshape(seq_count, tokens, local_width)
        .astype(jnp.bfloat16)
    )
    key_rot = (
        rotate(projected[1].reshape(head_shape), cosines, sines)
        .reshape(seq_count, tokens, local_width)
        .astype(jnp.bfloat16)
    )
    value_low = projected[2].astype(jnp.bfloat16)
    keys_all, values_all = (
        lax.all_gather(key_rot, "ctx", axis=1, tiled=True),
        lax.all_gather(value_low, "ctx", axis=1, tiled=True),
    )
    query_groups = group_heads(query_rot, per_group)
    attended, log_total = lax.map(
        partial(attend_block, scaling=scaling),
        (query_groups, group_heads(keys_all, per_group), group_heads(values_all, per_group)),
    )
    attended_low = ungroup_heads(attended, seq_count).astype(jnp.bfloat16)
    branch_part = jnp.einsum(
        "ste,ed->std", attended_low, full_out, preferred_element_type=jnp.float32
    )
    middle = inputs_f + lax.psum(branch_part, "tp")
    second_out, normed_two, inverse_two = scaled_norm(
        middle, gains_f[1], modulation[:, 2], modulation[:, 3]
    )
    second_low = second_out.astype(jnp.bfloat16)
    hidden = jnp.einsum("std,df->stf", second_low, full_up, preferred_element_type=jnp.float32)
    activated = jax.nn.gelu(hidden, approximate=False).astype(jnp.bfloat16)
    mlp_part = jnp.einsum("stf,fd->std", activated, full_down, preferred_element_type=jnp.float32)
    output = (middle + lax.psum(mlp_part, "tp")).astype(jnp.bfloat16)
    back_qkv, back_out, back_up, back_down = (
        lax.all_gather(qkv_weight, "shard", axis=1, tiled=True),
        lax.all_gather(out_weight, "shard", axis=1, tiled=True),
        lax.all_gather(up_weight, "shard", axis=0, tiled=True),
        lax.all_gather(down_weight, "shard", axis=1, tiled=True),
    )
    keys_back, values_back = (
        lax.all_gather(key_rot, "ctx", axis=1, tiled=True),
        lax.all_gather(value_low, "ctx", axis=1, tiled=True),
    )
    grad_down = jnp.einsum("stf,std->fd", activated, cotangent, preferred_element_type=jnp.float32)
    grad_act = jnp.einsum("std,fd->stf", cotangent, back_down, preferred_element_type=jnp.float32)
    grad_hidden = (grad_act * gelu_slope(hidden)).astype(jnp.bfloat16)
    grad_up = jnp.einsum("std,stf->df", second_low, grad_hidden, preferred_element_type=jnp.float32)
    grad_second = lax.psum(
        jnp.einsum("stf,df->std", grad_hidden, back_up, preferred_element_type=jnp.float32), "tp"
    )
    grad_mid_norm, gain_two, scaling_two, offset_two = norm_back(
        grad_second, normed_two, inverse_two, gains_f[1], modulation[:, 2]
    )
    grad_middle = cotangent.astype(jnp.float32) + grad_mid_norm
    grad_branch = grad_middle.astype(jnp.bfloat16)
    grad_out = jnp.einsum(
        "ste,std->ed", attended_low, grad_branch, preferred_element_type=jnp.float32
    )
    grad_attended = jnp.einsum(
        "std,ed->ste", grad_branch, back_out, preferred_element_type=jnp.float32
    ).astype(jnp.bfloat16)
    grad_query_g, grad_key_g, grad_value_g = lax.map(
        partial(attend_back, scaling=scaling),
        (
            query_groups,
            group_heads(keys_back, per_group),
            group_heads(values_back, per_group),
            group_heads(grad_attended, per_group),
            log_total,
        ),
    )
    grad_key_all = ungroup_heads(grad_key_g, seq_count)
    grad_value_all = ungroup_heads(grad_value_g, seq_count)
    grad_key, grad_value = (
        lax.psum_scatter(grad_key_all, "ctx", scatter_dimension=1, tiled=True),
        lax.psum_scatter(grad_value_all, "ctx", scatter_dimension=1, tiled=True),
    )
    grad_query = ungroup_heads(grad_query_g, seq_count)
    query_back = unrotate(grad_query.reshape(head_shape), cosines, sines).reshape(
        seq_count, tokens, local_width
    )
    key_back = unrotate(grad_key.reshape(head_shape), cosines, sines).reshape(
        seq_count, tokens, local_width
    )
    grad_projected = jnp.stack([query_back, key_back, grad_value], axis=0).astype(jnp.bfloat16)
    grad_qkv = jnp.einsum(
        "std,cste->cde", first_low, grad_projected, preferred_element_type=jnp.float32
    )
    grad_first = lax.psum(
        jnp.einsum("cste,cde->std", grad_projected, back_qkv, preferred_element_type=jnp.float32),
        "tp",
    )
    grad_in_norm, gain_one, scaling_one, offset_one = norm_back(
        grad_first, normed_one, inverse_one, gains_f[0], modulation[:, 0]
    )
    input_grad = (grad_middle + grad_in_norm).astype(jnp.bfloat16)
    grad_modulation = jnp.stack([scaling_one, offset_one, scaling_two, offset_two], axis=1)
    grad_time = jnp.einsum("sk,scd->kcd", embedding, grad_modulation, precision=highest)
    grad_gains = jnp.stack([gain_one, gain_two], axis=0)
    shares = (
        lax.psum_scatter(grad_qkv, "shard", scatter_dimension=1, tiled=True),
        lax.psum_scatter(grad_out, "shard", scatter_dimension=1, tiled=True),
        lax.psum_scatter(grad_up, "shard", scatter_dimension=0, tiled=True),
        lax.psum_scatter(grad_down, "shard", scatter_dimension=1, tiled=True),
        lax.psum_scatter(grad_time, "shard", scatter_dimension=2, tiled=True),
        lax.psum_scatter(grad_gains, "shard", scatter_dimension=1, tiled=True),
    )
    shares = lax.psum((shares[0], shares[1], shares[2], shares[3], shares[4], shares[5]), "ctx")
    return (output, input_grad, shares[0], shares[1], shares[2], shares[3], shares[4], shares[5])


BF = jnp.bfloat16
F32 = jnp.float32
NN = (((1,), (0,)), ((), ()))
NT = (((1,), (1,)), ((), ()))
TN = (((0,), (0,)), ((), ()))
VMEM_BIG = 56 << 20
PER_US = 0.8e9


def mm(a, b, dims=NN):
    return lax.dot_general(a, b, dims, preferred_element_type=F32)


def cost(flops, nbytes=0, trans=0):
    return pl.CostEstimate(flops=int(flops), bytes_accessed=int(nbytes), transcendentals=int(trans))


def whole(array):
    zeros = (0,) * array.ndim
    return pl.BlockSpec(array.shape, lambda *_: zeros)


def call(kernel, name, grid, scalars, ins, in_specs, outs, out_specs, est, scratch=()):
    return pl.pallas_call(
        kernel,
        out_shape=outs,
        grid_spec=pltpu.PrefetchScalarGridSpec(
            num_scalar_prefetch=len(scalars),
            grid=grid,
            in_specs=in_specs,
            out_specs=out_specs,
            scratch_shapes=list(scratch),
        ),
        compiler_params=pltpu.CompilerParams(vmem_limit_bytes=VMEM_BIG),
        cost_estimate=est,
        name=name,
    )(*scalars, *ins)


def shape(dims, dtype):
    return jax.ShapeDtypeStruct(dims, dtype)


def cols(index, width):
    return pl.ds(pl.multiple_of(index * width, width), width)


def half_turn(values):
    lane = lax.broadcasted_iota(jnp.int32, values.shape, 1) % HEAD_DIM
    width = values.shape[1]
    up = pltpu.roll(values, HEAD_DIM // 2, 1)
    down = pltpu.roll(values, width - HEAD_DIM // 2, 1)
    return jnp.where(lane < HEAD_DIM // 2, down, up)


def spin(cos_ref, sin_ref, width):
    cosines, sines = cos_ref[...].T, sin_ref[...].T
    heads = width // HEAD_DIM
    return jnp.concatenate([cosines, cosines] * heads, axis=1), jnp.concatenate([-sines, sines] * heads, axis=1)


def pick(step, first_ref, second_ref, per_half):
    return jnp.where(step < per_half, first_ref[...], second_ref[...])


def own_map(per_half):
    return lambda i, *_: (jnp.minimum(i, per_half - 1), 0)


def other_map(per_half):
    return lambda i, *_: (jnp.maximum(i - per_half, 0), 0)


def project_kernel(per_half, blk, xa, xb, w0, w1, w2, w3, mods, cosb, sinb, h_ref, q_ref, k_ref, kt_ref, v_ref, vt_ref):
    x = pick(pl.program_id(0), xa, xb, per_half).astype(F32)
    x = x - jnp.mean(x, axis=1, keepdims=True)
    var = jnp.mean(x * x, axis=1, keepdims=True)
    n = x * lax.rsqrt(var + norm_epsilon)
    h_ref[...] = (n * mods[0:1, :] + mods[1:2, :]).astype(BF)
    rows = w0.shape[0]
    acc = None
    for j, w in enumerate((w0, w1, w2, w3)):
        part = mm(h_ref[:, cols(blk[j], rows)], w[...])
        acc = part if acc is None else acc + part
    wide = acc.shape[1] // 3
    cosines, sines = spin(cosb, sinb, wide)
    q = acc[:, :wide]
    k = acc[:, wide : 2 * wide]
    v = acc[:, 2 * wide :]
    q = q * cosines + half_turn(q) * sines
    k = k * cosines + half_turn(k) * sines
    q_ref[...] = q.astype(BF)
    k_ref[...] = k.astype(BF)
    kt_ref[...] = k.T.astype(BF)
    v_ref[...] = v.astype(BF)
    vt_ref[...] = v.T.astype(BF)


def project(blk, xa, xb, ws, mods, cosb, sinb, tile=256):
    half, width = xa.shape
    total = 2 * half
    wide = ws[0].shape[1] // 3
    per_half = half // tile
    row = lambda w: pl.BlockSpec((tile, w), lambda i, *_: (i, 0))
    turned = pl.BlockSpec((wide, tile), lambda i, *_: (0, i))
    return call(
        partial(project_kernel, per_half), "project", (total // tile,), (blk,),
        (xa, xb, *ws, mods, cosb, sinb),
        [pl.BlockSpec((tile, width), own_map(per_half)), pl.BlockSpec((tile, width), other_map(per_half)),
         *[whole(w) for w in ws], whole(mods), *[pl.BlockSpec((v.shape[0], tile), lambda i, *_: (0, i)) for v in (cosb, sinb)]],
        [shape((total, width), BF), shape((total, wide), BF), shape((total, wide), BF), shape((wide, total), BF),
         shape((total, wide), BF), shape((wide, total), BF)],
        [row(width), row(wide), row(wide), turned, row(wide), turned],
        cost(12.5 * PER_US),
    )


def attend_kernel(scale, q_ref, k_ref, vt_ref, o_ref, ot_ref, lse_ref):
    rows, wide = q_ref.shape
    q = q_ref[...]
    lane = lax.broadcasted_iota(jnp.int32, (rows, wide), 1) // HEAD_DIM
    def head(h, _):
        at = pl.ds(pl.multiple_of(h * HEAD_DIM, HEAD_DIM), HEAD_DIM)
        qh = jnp.where(lane == h, q, jnp.zeros_like(q))
        s = mm(k_ref[...], qh, NT) * scale
        top = jnp.max(s, axis=0, keepdims=True)
        p = jnp.exp(s - top)
        total = jnp.sum(p, axis=0, keepdims=True)
        ot_ref[at, :] = mm(vt_ref[at, :], p.astype(BF)) / total
        lse_ref[pl.ds(h, 1), :] = top + jnp.log(total)
        return 0

    lax.fori_loop(0, wide // HEAD_DIM, head, 0)
    o_ref[...] = ot_ref[...].T.astype(BF)


def attend(q, k, vt, first, rows, tile=1024):
    total, wide = q.shape
    heads = wide // HEAD_DIM
    skip = first // tile
    return call(
        partial(attend_kernel, HEAD_DIM**-0.5), "attend", (rows // tile,), (), (q, k, vt),
        [pl.BlockSpec((tile, wide), lambda i: (i + skip, 0)), whole(k), whole(vt)],
        [shape((rows, wide), BF), shape((wide, rows), F32), shape((heads, rows), F32)],
        [pl.BlockSpec((tile, wide), lambda i: (i, 0)), pl.BlockSpec((wide, tile), lambda i: (0, i)),
         pl.BlockSpec((heads, tile), lambda i: (0, i))],
        cost(10.0 * PER_US),
    )


def join_kernel(n_t, blk, blo, x_ref, *refs):
    near, far = refs[:n_t], refs[n_t : 2 * n_t]
    mine = refs[2 * n_t : 6 * n_t]
    theirs, mods, x1_ref, h_ref = refs[6 * n_t :]
    own = jnp.concatenate([o[...] for o in near], axis=1)
    oth = jnp.concatenate([o[...] for o in far], axis=1)
    span = theirs.shape[1]
    deep = own.shape[1]
    for k in range(4):
        at = cols(blk[k], span)
        w = jnp.concatenate([mine[4 * j + k][...] for j in range(n_t)], axis=0)
        x1_ref[:, at] = x_ref[:, at].astype(F32) + mm(own, w)
    for k in range(4):
        at = cols(blo[k], span)
        x1_ref[:, at] += mm(oth, theirs[k * deep : (k + 1) * deep, :])
    x = x1_ref[...]
    x = x - jnp.mean(x, axis=1, keepdims=True)
    var = jnp.mean(x * x, axis=1, keepdims=True)
    n = x * lax.rsqrt(var + norm_epsilon)
    h_ref[...] = (n * mods[2:3, :] + mods[3:4, :]).astype(BF)


def part_of(array, index, rows):
    return pl.BlockSpec((rows, array.shape[1]), lambda *_: (index, 0))


def stack_kernel(*refs):
    rows = refs[0].shape[0]
    for i, ref in enumerate(refs[:-1]):
        refs[-1][i * rows : (i + 1) * rows, :] = ref[...]


def stack_parts(arrays, rows):
    width = arrays[0].shape[1]
    return call(
        stack_kernel, "stack_parts", (1,), (), arrays,
        [part_of(v, v.shape[0] // rows - 1, rows) for v in arrays],
        shape((len(arrays) * rows, width), BF), pl.BlockSpec((len(arrays) * rows, width), lambda i: (0, 0)),
        cost(2.3 * PER_US),
    )


def join(blk, blo, x, near, far, slots, theirs, mods, tile=256):
    half, width = x.shape
    n_t = len(slots)
    wide = near[0].shape[1]
    row = lambda w: pl.BlockSpec((tile, w), lambda i, *_: (i, 0))
    flat = [w for slot in slots for w in slot]
    last_part = flat[0].shape[0] // wide - 1
    return call(
        partial(join_kernel, n_t), "join", (half // tile,), (blk, blo), (x, *near, *far, *flat, theirs, mods),
        [row(width), *[row(wide)] * (2 * n_t), *[part_of(w, last_part, wide) for w in flat], whole(theirs), whole(mods)],
        [shape((half, width), F32), shape((half, width), BF)],
        [row(width), row(width)],
        cost(8.5 * PER_US),
    )


def gelu_parts(u):
    half = 0.5 * (1.0 + lax.erf(u * 0.7071067811865476))
    slope = half + u * jnp.exp(-0.5 * u * u) * 0.3989422804014327
    return u * half, slope


def unpack_kernel(blk, *refs):
    ws, (up_ref, down_ref) = refs[:4], refs[-2:]
    span = ws[0].shape[1]
    for j, w in enumerate(ws):
        rows = pl.ds(pl.multiple_of(blk[j] * span, span), span)
        for b in range(2):
            up_ref[rows, b * span : (b + 1) * span] = w[b * span : (b + 1) * span, :]
        down_ref[:, cols(blk[j], span)] = w[2 * span : 4 * span, :]


def unpack(blk, slot, index, n_slots, before):
    span = slot[0].shape[1]
    width, hidden = 4 * span, 2 * span
    any_space = pl.BlockSpec(memory_space=pl.ANY)
    kept = () if before is None else before
    return pl.pallas_call(
        unpack_kernel,
        out_shape=[shape((n_slots * width, hidden), BF), shape((n_slots * hidden, width), BF)],
        grid_spec=pltpu.PrefetchScalarGridSpec(
            num_scalar_prefetch=1,
            grid=(1,),
            in_specs=[part_of(w, 0, width) for w in slot] + [any_space] * len(kept),
            out_specs=[pl.BlockSpec((width, hidden), lambda *_: (index, 0)), pl.BlockSpec((hidden, width), lambda *_: (index, 0))],
        ),
        input_output_aliases={5: 0, 6: 1} if kept else {},
        compiler_params=pltpu.CompilerParams(vmem_limit_bytes=VMEM_BIG),
        cost_estimate=cost(2.5 * PER_US),
        name="unpack",
    )(blk, *slot, *kept)


def mlp_kernel(per_half, n_slots, ha, hb, ca, cb, wu, wd, own_ref, oth_ref, g_ref, du_ref, h_buf, c_buf, du_buf):
    step = pl.program_id(0)
    width = ha.shape[1]
    hidden = wu.shape[1]
    h_buf[...] = pick(step, ha, hb, per_half)
    c_buf[...] = pick(step, ca, cb, per_half)

    def one(i, _):
        at = cols(i, hidden)
        u = mm(h_buf[...], wu[pl.ds(pl.multiple_of(i * width, width), width), :])
        dg = mm(c_buf[...], wd[pl.ds(pl.multiple_of(i * hidden, hidden), hidden), :], NT)
        g, slope = gelu_parts(u)
        g_ref[:, at] = g.astype(BF)
        du_buf[:, at] = (dg * slope).astype(BF)
        return 0

    lax.fori_loop(0, n_slots, one, 0)
    du_ref[...] = du_buf[:, :hidden]
    chunk = min(512, width)
    for n in range(width // chunk):
        at = slice(n * chunk, (n + 1) * chunk)
        acc = None
        for i in range(n_slots):
            part = mm(du_buf[:, i * hidden : (i + 1) * hidden], wu[i * width + n * chunk : i * width + (n + 1) * chunk, :], NT)
            acc = part if acc is None else acc + part

        @pl.when(step < per_half)
        def _():
            own_ref[:, at] = acc

        @pl.when(step >= per_half)
        def _():
            oth_ref[:, at] = acc.astype(BF)


def mlp(ha, hb, ca, cb, wu, wd, tile=512):
    half, width = ha.shape
    total = 2 * half
    per_half = half // tile
    hidden = wu.shape[1]
    n_slots = wu.shape[0] // width
    row = lambda w: pl.BlockSpec((tile, w), lambda i, *_: (i, 0))
    mine = pl.BlockSpec((tile, width), own_map(per_half))
    theirs = pl.BlockSpec((tile, width), other_map(per_half))
    return call(
        partial(mlp_kernel, per_half, n_slots), "mlp", (total // tile,), (), (ha, hb, ca, cb, wu, wd),
        [mine, theirs, mine, theirs, whole(wu), whole(wd)],
        [shape((half, width), F32), shape((half, width), BF), shape((total, n_slots * hidden), BF), shape((total, hidden), BF)],
        [mine, theirs, row(n_slots * hidden), row(hidden)],
        cost(42.0 * PER_US),
        [pltpu.VMEM((tile, width), BF), pltpu.VMEM((tile, width), BF), pltpu.VMEM((tile, n_slots * hidden), BF)],
    )


def lift_kernel(per_half, g_in, wd, own_ref, oth_ref):
    step = pl.program_id(0)
    chunk = 512
    for n in range(wd.shape[1] // chunk):
        at = slice(n * chunk, (n + 1) * chunk)
        part = mm(g_in[...], wd[:, at])

        @pl.when(step < per_half)
        def _():
            own_ref[:, at] = part

        @pl.when(step >= per_half)
        def _():
            oth_ref[:, at] = part.astype(BF)


def lift(g, wd, tile=512):
    total = g.shape[0]
    width = wd.shape[1]
    half = total // 2
    per_half = half // tile
    return call(
        partial(lift_kernel, per_half), "lift", (total // tile,), (), (g, wd),
        [pl.BlockSpec((tile, g.shape[1]), lambda i, *_: (i, 0)), whole(wd)],
        [shape((half, width), F32), shape((half, width), BF)],
        [pl.BlockSpec((tile, width), own_map(per_half)), pl.BlockSpec((tile, width), other_map(per_half))],
        cost(14.0 * PER_US),
    )


def norm_turn(dh, x, factor):
    x = x - jnp.mean(x, axis=1, keepdims=True)
    var = jnp.mean(x * x, axis=1, keepdims=True)
    r = lax.rsqrt(var + norm_epsilon)
    n = x * r
    dn = dh * factor
    dx = r * (dn - jnp.mean(dn, axis=1, keepdims=True) - n * jnp.mean(dn * n, axis=1, keepdims=True))
    return dx, jnp.sum(dh * n, axis=0, keepdims=True), jnp.sum(dh, axis=0, keepdims=True)


def turn_kernel(blk, blo, dh_ref, in_ref, x_ref, c_ref, mods, a0, a1, a2, a3, b_ref, dx_ref, da_ref, own_ref, oth_ref, sums):
    dh = dh_ref[...] + in_ref[...].astype(F32)
    dx, s1, s0 = norm_turn(dh, x_ref[...], mods[2:3, :])
    dx = dx + c_ref[...].astype(F32)
    dx_ref[...] = dx
    da_ref[...] = dx.astype(BF)
    wide = own_ref.shape[1]
    span = a0.shape[1]
    step = b_ref.shape[0] // 4
    theirs = [b_ref[k * step : k * step + wide, :] for k in range(4)]
    for order, ws, out in ((blk, [a[...] for a in (a0, a1, a2, a3)], own_ref), (blo, theirs, oth_ref)):
        acc = None
        for j, w in enumerate(ws):
            part = mm(da_ref[:, cols(order[j], span)], w, NT)
            acc = part if acc is None else acc + part
        out[...] = acc.astype(BF)

    @pl.when(pl.program_id(0) == 0)
    def _():
        sums[...] = jnp.zeros_like(sums)

    sums[0:1, :] += s1
    sums[1:2, :] += s0


def turn(blk, blo, dh, received, x1, cot, mods, wa, wb, wide, tile=256):
    half, width = x1.shape
    row = lambda w: pl.BlockSpec((tile, w), lambda i, *_: (i, 0))
    return call(
        turn_kernel, "turn", (half // tile,), (blk, blo), (dh, received, x1, cot, mods, *wa, wb),
        [row(width)] * 4 + [whole(mods), *[part_of(w, w.shape[0] // wide - 1, wide) for w in wa], whole(wb)],
        [shape((half, width), F32), shape((half, width), BF), shape((half, wide), BF), shape((half, wide), BF), shape((8, width), F32)],
        [row(width), row(width), row(wide), row(wide), pl.BlockSpec((8, width), lambda i, *_: (0, 0))],
        cost(11.3 * PER_US),
    )


def attend_back_kernel(scale, tk, per_half, q_ref, da_ref, db_ref, ota_ref, otb_ref, la_ref, lb_ref, cos_ref, sin_ref, k_ref, v_ref, kt_ref, cosb, sinb, out_ref, dqt, dk_acc, dv_acc):
    rows, wide = q_ref.shape
    total = k_ref.shape[0]
    step = pl.program_id(0)
    q = q_ref[...]
    do = pick(step, da_ref, db_ref, per_half)
    lse = pick(step, la_ref, lb_ref, per_half)
    lane = lax.broadcasted_iota(jnp.int32, (rows, wide), 1) // HEAD_DIM
    heads = wide // HEAD_DIM
    qs = [jnp.where(lane == h, q, jnp.zeros_like(q)) for h in range(heads)]
    ds = [jnp.where(lane == h, do, jnp.zeros_like(do)) for h in range(heads)]
    od = do.astype(F32).T * pick(step, ota_ref, otb_ref, per_half)
    deltas = [jnp.sum(od[h * HEAD_DIM : (h + 1) * HEAD_DIM, :], axis=0, keepdims=True) for h in range(heads)]

    @pl.when(step == 0)
    def _():
        dk_acc[...] = jnp.zeros_like(dk_acc)
        dv_acc[...] = jnp.zeros_like(dv_acc)

    dqt[...] = jnp.zeros_like(dqt)
    for j in range(total // tk):
        at = slice(j * tk, (j + 1) * tk)
        kj, vj = k_ref[at, :], v_ref[at, :]
        for h in range(heads):
            hs = slice(h * HEAD_DIM, (h + 1) * HEAD_DIM)
            s = mm(kj, qs[h], NT) * scale
            p = jnp.exp(s - lse[h : h + 1, :])
            dp = mm(vj, ds[h], NT)
            dsc = (p * (dp - deltas[h])).astype(BF)
            dv_acc[at, :] += mm(p.astype(BF), ds[h])
            dk_acc[at, :] += mm(dsc, qs[h])
            dqt[hs, :] += mm(kt_ref[hs, at], dsc)
    dq = dqt[...].T * scale
    cosines, sines = spin(cos_ref, sin_ref, wide)
    out_ref[pl.ds(pl.multiple_of(step * rows, rows), rows), :wide] = (dq * cosines - half_turn(dq) * sines).astype(BF)

    @pl.when(step == pl.num_programs(0) - 1)
    def _():
        dk = dk_acc[...] * scale
        cosines, sines = spin(cosb, sinb, wide)
        out_ref[:, wide : 2 * wide] = (dk * cosines - half_turn(dk) * sines).astype(BF)
        out_ref[:, 2 * wide :] = dv_acc[...].astype(BF)


def attend_back_call(q, do_a, do_b, ots, lses, k, v, kt, cosb, sinb, tile=512, tk=512):
    total, wide = q.shape
    heads = wide // HEAD_DIM
    per_half = total // 2 // tile
    row = pl.BlockSpec((tile, wide), lambda i: (i, 0))
    lanes_a = lambda h: pl.BlockSpec((h, tile), lambda i: (0, jnp.minimum(i, per_half - 1)))
    lanes_b = lambda h: pl.BlockSpec((h, tile), lambda i: (0, jnp.maximum(i - per_half, 0)))
    full = pl.BlockSpec((total, wide), lambda i: (0, 0))
    turned = pl.BlockSpec((cosb.shape[0], tile), lambda i: (0, i))
    return call(
        partial(attend_back_kernel, HEAD_DIM**-0.5, tk, per_half), "attend_back", (total // tile,), (),
        (q, do_a, do_b, *ots, *lses, cosb, sinb, k, v, kt, cosb, sinb),
        [row, pl.BlockSpec((tile, wide), own_map(per_half)), pl.BlockSpec((tile, wide), other_map(per_half)),
         lanes_a(wide), lanes_b(wide), lanes_a(heads), lanes_b(heads), turned, turned, full, full, whole(kt), whole(cosb), whole(sinb)],
        shape((total, 3 * wide), BF),
        pl.BlockSpec((total, 3 * wide), lambda i: (0, 0)),
        cost(29.0 * PER_US),
        [pltpu.VMEM((wide, tile), F32), pltpu.VMEM((total, wide), F32), pltpu.VMEM((total, wide), F32)],
    )


def gather_kernel(n, blk, *refs):
    rs = refs[:n]
    ws = [refs[n + 4 * i : n + 4 * i + 4] for i in range(n)]
    own_ref, oth_ref = refs[5 * n :]
    rows = own_ref.shape[0]
    span = ws[0][0].shape[0]
    for j in range(4):
        acc = None
        for r, w in zip(rs, ws):
            part = mm(r[...], w[j][...], NT)
            acc = part if acc is None else acc + part
        own_ref[:, cols(blk[j], span)] = acc[:rows]
        oth_ref[:, cols(blk[j], span)] = acc[rows:].astype(BF)


def gather(blk, rs, first, others, width):
    n = len(rs)
    rows, span = rs[0].shape[0] // 2, first[0].shape[0]
    back = pl.BlockSpec((rows, width), lambda i, *_: (0, 0))
    return call(
        partial(gather_kernel, n), "gather", (1,), (blk,), (*rs, *first, *(others * (n - 1))),
        [*[whole(r) for r in rs], *[whole(w) for w in first], *[part_of(w, i, span) for i in range(n - 1) for w in others]],
        [shape((rows, width), F32), shape((rows, width), BF)],
        [back, back],
        cost(6.5 * PER_US),
    )


def last_kernel(at, dh_ref, in_ref, x_ref, dx_ref, mods, out_ref, sums):
    dx, s1, s0 = norm_turn(dh_ref[...] + in_ref[...].astype(F32), x_ref[...].astype(F32), mods[0:1, :])
    out_ref[...] = (dx + dx_ref[...]).astype(BF)
    sums[...] = jnp.zeros_like(sums)
    sums[0:1, :] = s1
    sums[1:2, :] = s0


def last(at, dh, received, x, dx, mods):
    rows, width = dh.shape
    block = pl.BlockSpec((rows, width), lambda i, at: (at[0], 0))
    return call(
        last_kernel, "last", (1,), (at,), (dh, received, x, dx, mods),
        [whole(dh), whole(received), block, block, whole(mods)],
        [shape((rows, width), BF), shape((8, width), F32)],
        [pl.BlockSpec((rows, width), lambda i, *_: (0, 0)), pl.BlockSpec((8, width), lambda i, *_: (0, 0))],
        cost(3.5 * PER_US),
    )


def after(values, *events):
    return lax.optimization_barrier((values, events))[0]


def fast_body(
    activations, timestep, positions, qkv_weight, out_weight, up_weight, down_weight, time_weight, norm_gains, cotangent
):
    n_s, n_t = lax.axis_size("shard"), lax.axis_size("tp")
    s, c, t = lax.axis_index("shard"), lax.axis_index("ctx"), lax.axis_index("tp")
    x_own = activations[0]
    cot_own = cotangent[0]
    half, width = x_own.shape
    span = width // n_s
    quarter = half // n_t
    near = jnp.where(c == 0, 1, 2)
    blk = jnp.stack([s, s ^ near, s ^ (3 - near), s ^ 3]).astype(jnp.int32)
    blo = jnp.stack([s, s ^ (3 - near), s ^ near, s ^ 3]).astype(jnp.int32)
    pairs_a = [(v * 2 + k, (v ^ (1 + k)) * 2 + k) for v in range(n_s) for k in range(2)]
    pairs_b = [(v * 2 + k, (v ^ (2 - k)) * 2 + k) for v in range(n_s) for k in range(2)]
    cycle = [(i, (i + 1) % n_t) for i in range(n_t)]
    swap = lambda v: lax.ppermute(v, "ctx", [(0, 1), (1, 0)])
    move_a = lambda v: lax.ppermute(v, ("shard", "ctx"), pairs_a)
    move_b = lambda v: lax.ppermute(v, ("shard", "ctx"), pairs_b)
    upward = lambda v: lax.ppermute(v, "tp", cycle)

    def by_z(v, d):
        return lax.ppermute(v, "tp", [(i, (i + d) % n_t) for i in range(n_t)])

    def turn_shard(v, d):
        return lax.ppermute(v, "shard", [(i, (i + d) % n_s) for i in range(n_s)])

    def half_of(v, axis):
        size = v.shape[axis] // 2
        return lax.dynamic_slice_in_dim(v, c * size, size, axis)

    def both(v, axis):
        other = swap(v)
        return jnp.where(c == 0, jnp.concatenate([v, other], axis), jnp.concatenate([other, v], axis))

    x_oth = swap(x_own)

    def shard_pair(v, bit):
        return lax.ppermute(v, "shard", [(i, i ^ bit) for i in range(n_s)])

    gains = norm_gains.astype(F32)
    small = jnp.concatenate([gains, jnp.broadcast_to(timestep.astype(F32)[:, None], (1, span))], axis=0)
    small_two = jnp.concatenate([small, shard_pair(small, 1)], axis=0)
    small_four = jnp.concatenate([small_two, shard_pair(small_two, 2)], axis=0)
    smalls = [small_four[3 * i : 3 * i + 3] for i in range(n_s)]

    wide = qkv_weight.shape[2] // 2
    qkv_half = half_of(qkv_weight, 2)
    qkv_share = jnp.concatenate([qkv_half[0], qkv_half[1], qkv_half[2]], axis=1)
    qkv_a, qkv_b = move_a(qkv_share), move_b(qkv_share)
    qkv_c = move_b(qkv_a)
    w_qkv = [qkv_share, qkv_a, qkv_b, qkv_c]
    pos_own = positions.astype(F32)
    pos_oth = swap(pos_own)

    up_half = half_of(up_weight, 1)
    down_half = half_of(down_weight, 0)
    pack = jnp.concatenate([up_half[:, :span], up_half[:, span:], down_half, half_of(out_weight, 0)], axis=0)
    z1 = upward(pack)
    pack_go = after(pack, qkv_a, qkv_b)
    m0a, m0b = move_a(pack_go), move_b(pack_go)

    steps = small_four[2::3, 0]
    embedding = embed_time(steps)
    parts = jnp.einsum("sk,kcd->scd", embedding, time_weight.astype(F32), precision=highest)
    parts_x = shard_pair(jnp.concatenate([parts[1], parts[3]], axis=0), 1)
    parts_y = shard_pair(after(jnp.concatenate([parts[2], parts_x[4:]], axis=0), qkv_c), 2)
    parts_in = [parts[0], parts_x[:4], parts_y[:4], parts_y[4:]]
    gain_full = jnp.zeros((2, width), F32)
    mod_full = jnp.zeros((4, width), F32)
    for i in range(n_s):
        gain_full = lax.dynamic_update_slice_in_dim(gain_full, smalls[i][:2], (s ^ i) * span, 1)
        mod_full = lax.dynamic_update_slice_in_dim(mod_full, parts_in[i], (s ^ i) * span, 1)
    factor_one = gain_full[0] * (1.0 + mod_full[0])
    factor_two = gain_full[1] * (1.0 + mod_full[2])
    zero = jnp.zeros_like(factor_one)
    mods = jnp.stack([factor_one, mod_full[1], factor_two, mod_full[3], zero, zero, zero, zero])

    half_width = HEAD_DIM // 2
    frequency = jnp.exp(-math.log(10000.0) * jnp.arange(half_width, dtype=F32) / half_width)
    angles = frequency[:, None] * jnp.concatenate([pos_own, pos_oth], axis=1)
    cosb, sinb = jnp.cos(angles), jnp.sin(angles)

    z1 = after(z1, parts_y)
    z2 = upward(z1)
    m1a, m1b = move_a(z1), move_b(z1)
    x_now = after(x_own, z1)
    h1, q, k, kt, v, vt = project(blk, x_now, x_oth, w_qkv, mods, cosb, sinb)
    m0a_late, m1a_late, z2_late = after((m0a, m1a, z2), q, m0b)
    m0c, m1c, z3 = move_b(m0a_late), move_b(m1a_late), upward(z2_late)
    o_far, ot_far, lse_far = attend(q, k, vt, half, half)
    o_got = swap(o_far)
    z2_late = after(z2, o_far, m0c, m1b)
    m2a, m2b = move_a(z2_late), move_b(z2_late)
    far = [after(o_got, z3)]
    far.append(upward(far[0]))
    o_near, ot_near, lse_near = attend(after(q, o_far), k, vt, 0, half)
    wu, wd = unpack(blk, [pack, m0a, m0b, m0c], 0, n_t, None)
    z3_late, m2a_late, far_go, near_go = after((z3, m2a, far[1], o_near), m2b, m1c)
    m3a, m3b, m2c = move_a(z3_late), move_b(z3_late), move_b(m2a_late)
    near = [near_go, upward(near_go)]
    far.append(upward(far_go))
    m3a_late, near_go, far_go, m1c_late = after((m3a, near[1], far[2], m1c), m2c, m3b)
    m3c = move_b(m3a_late)
    near.append(upward(near_go))
    far.append(upward(far_go))
    wu, wd = unpack(blk, [z1, m1a, m1b, m1c_late], 1, n_t, (wu, wd))
    near_go, m3c, far_done = after((near[2], m3c, far[3]), wu)
    near.append(upward(near_go))
    far[3] = far_done
    wu, wd = unpack(blk, [z2, m2a, m2b, after(m2c, m3c)], 2, n_t, (wu, wd))
    wu, wd = unpack(blk, [z3, m3a, m3b, m3c], 3, n_t, (wu, wd))
    cot_oth = swap(cot_own)
    w_mlp = [[pack, m0a, m0b, m0c], [z1, m1a, m1b, m1c], [z2, m2a, m2b, m2c], [z3, m3a, m3b, m3c]]
    out_other = swap(stack_parts([w_mlp[j][i] for i in range(n_s) for j in range(n_t)], wide))

    x1, h2 = join(blk, blo, after(x_own, wu), near, far, w_mlp, out_other, mods)
    h2_oth = swap(h2)
    dh2, dh2_send, g_all, du0 = mlp(h2, h2_oth, cot_own, cot_oth, wu, wd)
    qkv_again = after(qkv_share, h2_oth)
    qz_pack = jnp.concatenate([by_z(qkv_again, d) for d in range(1, n_t)], axis=0)
    dh2_in = swap(after(dh2_send, qz_pack))
    qz_pack = after(qz_pack, dh2_in)
    qza, qzb = move_a(qz_pack), move_b(qz_pack)
    dx1, da, do_own, do_send, sums_two = turn(blk, blo, dh2, dh2_in, x1, cot_own, mods, w_mlp[0], out_other, wide)
    do_got = swap(do_send)
    qza, qzb, do_got = after((qza, qzb, do_got), da)
    qzc = move_b(qza)
    w_back = [qz_pack, qza, qzb, qzc]
    dqkv = attend_back_call(q, do_own, do_got, (ot_near, ot_far), (lse_near, lse_far), k, v, kt, cosb, sinb)

    dqkv = dqkv.reshape(2, half, 3 * wide)

    def tokens_of(d):
        return lax.dynamic_slice_in_dim(dqkv, ((t + d) % n_t) * quarter, quarter, 1).reshape(2 * quarter, 3 * wide)

    got = [tokens_of(0), by_z(tokens_of(1), 1)]

    h2_late, h2o_late, du0_late, g_late = after((h2, h2_oth, du0, g_all), tokens_of(1))
    g_up = mm(jnp.concatenate([h2_late, h2o_late], axis=0), du0_late, TN)
    g_down = mm(g_late[:, : 2 * span], jnp.concatenate([cot_own, cot_oth], axis=0), TN)
    got.append(by_z(after(tokens_of(2), got[1], g_up, g_down), 2))
    g_later = after(g_late, got[1], g_up, g_down)
    y_own, y_send = lift(g_later, wd)
    got.append(by_z(after(tokens_of(3), got[2], y_own), 3))

    def mlp_piece(j):
        ups = lax.dynamic_slice_in_dim(g_up, blk[j] * span, span, 0)
        downs = lax.dynamic_slice_in_dim(g_down, blk[j] * span, span, 1)
        outs = lax.dynamic_slice_in_dim(g_out, blk[j] * span, span, 1)
        return jnp.concatenate([ups[:, :span], ups[:, span:], downs, outs], axis=0)

    def reduce_first(pieces):
        return move_b(jnp.concatenate([pieces(2), pieces(3)], axis=0).astype(BF))

    def reduce_last(pieces, came):
        rows = came.shape[0] // 2
        return pieces(0) + came[:rows].astype(F32) + move_a((pieces(1) + came[rows:].astype(F32)).astype(BF)).astype(F32)

    dh1_own, dh1_send = gather(blk, got, w_qkv, w_back, width)
    dh1_got = swap(dh1_send)

    at = t.astype(jnp.int32).reshape(1)
    grad_mine, sums_one = last(at, dh1_own, dh1_got, x_own, dx1, mods)
    slots = [grad_mine, upward(grad_mine)]
    h1_late, dqkv_late, da_late, g_up, g_down, y_send = after((h1, dqkv, da, g_up, g_down, y_send), grad_mine)
    g_out = mm(o_near, da_late, TN) + swap(mm(o_got, da_late, TN).astype(BF)).astype(F32)
    mlp_came = reduce_first(mlp_piece)
    g_qkv = mm(h1_late, dqkv_late.reshape(2 * half, 3 * wide), TN)
    qkv_piece = lambda j: lax.dynamic_slice_in_dim(g_qkv, blk[j] * span, span, 0)
    y_got = swap(y_send)
    qkv_came = reduce_first(qkv_piece)
    keep = jnp.where(t == 0, 1.0, 0.0)
    tally = jnp.concatenate([sums_one[:2], sums_two[:2] * keep], axis=0)
    tally = tally + swap(tally)
    slots[1], tally, mlp_came, y_got = after((slots[1], tally, mlp_came, y_got), g_qkv)
    qkv_came = after(qkv_came, mlp_came, slots[1])
    slots.append(upward(slots[1]))
    full = tally
    for bit in (1, 2):
        full = full + lax.ppermute(full, "tp", [(i, i ^ bit) for i in range(n_t)])
    rows = mlp_came.shape[0] // 2
    mlp_base = mlp_piece(0) + mlp_came[:rows].astype(F32)
    mlp_last = move_a((mlp_piece(1) + mlp_came[rows:].astype(F32)).astype(BF))
    rows = qkv_came.shape[0] // 2
    qkv_base = qkv_piece(0) + qkv_came[:rows].astype(F32)
    qkv_last = move_a((qkv_piece(1) + qkv_came[rows:].astype(F32)).astype(BF))
    output = (x1 + y_own + y_got.astype(F32)).astype(BF)

    slots[2], mlp_last, full = after((slots[2], mlp_last, full), output)
    slots.append(upward(slots[2]))
    done = mlp_base + mlp_last.astype(F32)
    grad_up = both(jnp.concatenate([done[:span], done[span : 2 * span]], axis=1), 1)
    grad_down = both(done[2 * span : 4 * span], 0)
    grad_out = both(done[4 * span :], 0)
    done_qkv = qkv_base + qkv_last.astype(F32)
    grad_qkv = both(jnp.stack([done_qkv[:, i * wide : (i + 1) * wide] for i in range(3)]), 2)
    dmods = jnp.stack([full[0] * gain_full[0], full[1], full[2] * gain_full[1], full[3],
                       full[0] * (1.0 + mod_full[0]), full[2] * (1.0 + mod_full[2])])
    blocks = [lax.dynamic_slice_in_dim(dmods, (s ^ i) * span, span, 1) for i in range(n_s)]
    blocks_x = shard_pair(jnp.concatenate([blocks[1], blocks[3]], axis=0), 1)
    blocks_y = shard_pair(jnp.concatenate([blocks[2], blocks_x[6:]], axis=0), 2)
    seqs = jnp.stack([blocks[0], blocks_x[:6], blocks_y[:6], blocks_y[6:]])
    grad_time = jnp.einsum("sk,scd->kcd", embedding, seqs[:, :4], precision=highest)
    grad_gains = jnp.sum(seqs[:, 4:], axis=0)
    slots[3] = after(slots[3], grad_qkv, grad_up, grad_down, grad_out, grad_time, grad_gains)
    input_grad = jnp.zeros((half, width), BF)
    for j in range(n_t):
        input_grad = lax.dynamic_update_slice_in_dim(input_grad, slots[j], ((t - j) % n_t) * quarter, 0)
    return (output[None], input_grad[None], grad_qkv, grad_out, grad_up, grad_down, grad_time, grad_gains)


def solution(mesh):
    sizes = dict(mesh.shape)
    chosen = fast_body if (sizes["shard"], sizes["ctx"], sizes["tp"]) == (4, 2, 4) else body
    placed = (
        P("shard", "ctx", None),
        P("shard"),
        P("shard", "ctx"),
        P(None, "shard", "tp"),
        P("tp", "shard"),
        P("shard", "tp"),
        P("tp", "shard"),
        P(None, None, "shard"),
        P(None, "shard"),
        P("shard", "ctx", None),
    )
    return jax.shard_map(
        chosen,
        mesh=mesh,
        in_specs=placed,
        out_specs=(
            P("shard", "ctx", None),
            P("shard", "ctx", None),
            P(None, "shard", "tp"),
            P("tp", "shard"),
            P("shard", "tp"),
            P("tp", "shard"),
            P(None, None, "shard"),
            P(None, "shard"),
        ),
        check_vma=False,
    )
```

```python
from functools import partial
import math

import jax
import jax.numpy as jnp
from jax import lax
from jax.experimental import pallas as pl
from jax.experimental.pallas import tpu as pltpu
from jax.sharding import PartitionSpec as P

HEAD_DIM = 64
TEMB = 256


highest = lax.Precision.HIGHEST
norm_epsilon = 1e-05


def embed_time(timestep):
    half_width = TEMB // 2
    frequency = jnp.exp(-math.log(10000.0) * jnp.arange(half_width, dtype=jnp.float32) / half_width)
    angles = timestep.astype(jnp.float32)[:, None] * frequency[None, :]
    return jnp.concatenate([jnp.sin(angles), jnp.cos(angles)], axis=-1)


def rotary_tables(positions):
    half_width = HEAD_DIM // 2
    frequency = jnp.exp(-math.log(10000.0) * jnp.arange(half_width, dtype=jnp.float32) / half_width)
    angles = positions.astype(jnp.float32)[..., None] * frequency
    return (jnp.cos(angles), jnp.sin(angles))


def rotate(heads_in, cosines, sines):
    half_width = HEAD_DIM // 2
    first = heads_in[..., :half_width]
    second = heads_in[..., half_width:]
    cos_wide = cosines[..., None, :]
    sin_wide = sines[..., None, :]
    return jnp.concatenate(
        [first * cos_wide - second * sin_wide, second * cos_wide + first * sin_wide], axis=-1
    )


def unrotate(heads_in, cosines, sines):
    half_width = HEAD_DIM // 2
    first = heads_in[..., :half_width]
    second = heads_in[..., half_width:]
    cos_wide = cosines[..., None, :]
    sin_wide = sines[..., None, :]
    return jnp.concatenate(
        [first * cos_wide + second * sin_wide, second * cos_wide - first * sin_wide], axis=-1
    )


def scaled_norm(values, gain_vec, scaling, offset):
    centered = values - jnp.mean(values, axis=-1, keepdims=True)
    variance = jnp.mean(centered * centered, axis=-1, keepdims=True)
    inverse_std = lax.rsqrt(variance + norm_epsilon)
    normed = centered * inverse_std
    return (
        normed * gain_vec * (1.0 + scaling[:, None, :]) + offset[:, None, :],
        normed,
        inverse_std,
    )


def norm_back(grad_in, normed, inverse_std, gain_vec, scaling):
    factor = gain_vec * (1.0 + scaling[:, None, :])
    grad_normed = grad_in * factor
    grad_values = inverse_std * (
        grad_normed
        - jnp.mean(grad_normed, axis=-1, keepdims=True)
        - normed * jnp.mean(grad_normed * normed, axis=-1, keepdims=True)
    )
    grad_gain = jnp.sum(grad_in * normed * (1.0 + scaling[:, None, :]), axis=(0, 1))
    grad_scaling = jnp.sum(grad_in * normed * gain_vec, axis=1)
    grad_offset = jnp.sum(grad_in, axis=1)
    return (grad_values, grad_gain, grad_scaling, grad_offset)


def group_heads(field, per_group):
    seq_count, rows_count, _ = field.shape
    split = field.reshape(seq_count, rows_count, -1, HEAD_DIM).transpose(0, 2, 1, 3)
    return split.reshape(-1, per_group, rows_count, HEAD_DIM)


def ungroup_heads(field, seq_count):
    rows_count = field.shape[2]
    joined = field.reshape(seq_count, -1, rows_count, HEAD_DIM).transpose(0, 2, 1, 3)
    return joined.reshape(seq_count, rows_count, -1)


def attend_block(triple, scaling):
    queries, keys, values = triple
    scores = jnp.einsum("gqd,gkd->gqk", queries, keys, preferred_element_type=jnp.float32) * scaling
    top_score = jnp.max(scores, axis=-1, keepdims=True)
    raised = jnp.exp(scores - top_score)
    total = jnp.sum(raised, axis=-1, keepdims=True)
    weights = (raised / total).astype(jnp.bfloat16)
    attended = jnp.einsum("gqk,gkd->gqd", weights, values, preferred_element_type=jnp.float32)
    return (attended, (top_score + jnp.log(total))[..., 0])


def attend_back(bundle, scaling):
    queries, keys, values, grad_out, log_total = bundle
    scores = jnp.einsum("gqd,gkd->gqk", queries, keys, preferred_element_type=jnp.float32) * scaling
    weights = jnp.exp(scores - log_total[..., None])
    grad_values = jnp.einsum(
        "gqk,gqd->gkd", weights.astype(jnp.bfloat16), grad_out, preferred_element_type=jnp.float32
    )
    grad_weights = jnp.einsum("gqd,gkd->gqk", grad_out, values, preferred_element_type=jnp.float32)
    row_term = jnp.sum(weights * grad_weights, axis=-1, keepdims=True)
    grad_scores = (weights * (grad_weights - row_term)).astype(jnp.bfloat16)
    grad_queries = (
        jnp.einsum("gqk,gkd->gqd", grad_scores, keys, preferred_element_type=jnp.float32) * scaling
    )
    grad_keys = (
        jnp.einsum("gqk,gqd->gkd", grad_scores, queries, preferred_element_type=jnp.float32)
        * scaling
    )
    return (grad_queries, grad_keys, grad_values)


def gelu_slope(hidden):
    return (
        0.5 * (1.0 + lax.erf(hidden * 0.7071067811865476))
        + hidden * jnp.exp(-0.5 * hidden * hidden) * 0.3989422804014327
    )


def body(
    activations,
    timestep,
    positions,
    qkv_weight,
    out_weight,
    up_weight,
    down_weight,
    time_weight,
    norm_gains,
    cotangent,
):
    seq_count, tokens, width = activations.shape
    local_width = qkv_weight.shape[2]
    heads_local = local_width // HEAD_DIM
    per_group = min(heads_local, max(1, 512 // tokens))
    while heads_local % per_group:
        per_group -= 1
    scaling = HEAD_DIM ** (-0.5)
    full_qkv, full_out, full_up, full_down, full_time, full_gains = (
        lax.all_gather(qkv_weight, "shard", axis=1, tiled=True),
        lax.all_gather(out_weight, "shard", axis=1, tiled=True),
        lax.all_gather(up_weight, "shard", axis=0, tiled=True),
        lax.all_gather(down_weight, "shard", axis=1, tiled=True),
        lax.all_gather(time_weight, "shard", axis=2, tiled=True),
        lax.all_gather(norm_gains, "shard", axis=1, tiled=True),
    )
    gains_f = full_gains.astype(jnp.float32)
    embedding = embed_time(timestep)
    modulation = jnp.einsum(
        "sk,kcd->scd", embedding, full_time.astype(jnp.float32), precision=highest
    )
    cosines, sines = rotary_tables(positions)
    inputs_f = activations.astype(jnp.float32)
    first_out, normed_one, inverse_one = scaled_norm(
        inputs_f, gains_f[0], modulation[:, 0], modulation[:, 1]
    )
    first_low = first_out.astype(jnp.bfloat16)
    projected = jnp.einsum("std,cde->cste", first_low, full_qkv, preferred_element_type=jnp.float32)
    head_shape = (seq_count, tokens, heads_local, HEAD_DIM)
    query_rot = (
        rotate(projected[0].reshape(head_shape), cosines, sines)
        .reshape(seq_count, tokens, local_width)
        .astype(jnp.bfloat16)
    )
    key_rot = (
        rotate(projected[1].reshape(head_shape), cosines, sines)
        .reshape(seq_count, tokens, local_width)
        .astype(jnp.bfloat16)
    )
    value_low = projected[2].astype(jnp.bfloat16)
    keys_all, values_all = (
        lax.all_gather(key_rot, "ctx", axis=1, tiled=True),
        lax.all_gather(value_low, "ctx", axis=1, tiled=True),
    )
    query_groups = group_heads(query_rot, per_group)
    attended, log_total = lax.map(
        partial(attend_block, scaling=scaling),
        (query_groups, group_heads(keys_all, per_group), group_heads(values_all, per_group)),
    )
    attended_low = ungroup_heads(attended, seq_count).astype(jnp.bfloat16)
    branch_part = jnp.einsum(
        "ste,ed->std", attended_low, full_out, preferred_element_type=jnp.float32
    )
    middle = inputs_f + lax.psum(branch_part, "tp")
    second_out, normed_two, inverse_two = scaled_norm(
        middle, gains_f[1], modulation[:, 2], modulation[:, 3]
    )
    second_low = second_out.astype(jnp.bfloat16)
    hidden = jnp.einsum("std,df->stf", second_low, full_up, preferred_element_type=jnp.float32)
    activated = jax.nn.gelu(hidden, approximate=False).astype(jnp.bfloat16)
    mlp_part = jnp.einsum("stf,fd->std", activated, full_down, preferred_element_type=jnp.float32)
    output = (middle + lax.psum(mlp_part, "tp")).astype(jnp.bfloat16)
    back_qkv, back_out, back_up, back_down = (
        lax.all_gather(qkv_weight, "shard", axis=1, tiled=True),
        lax.all_gather(out_weight, "shard", axis=1, tiled=True),
        lax.all_gather(up_weight, "shard", axis=0, tiled=True),
        lax.all_gather(down_weight, "shard", axis=1, tiled=True),
    )
    keys_back, values_back = (
        lax.all_gather(key_rot, "ctx", axis=1, tiled=True),
        lax.all_gather(value_low, "ctx", axis=1, tiled=True),
    )
    grad_down = jnp.einsum("stf,std->fd", activated, cotangent, preferred_element_type=jnp.float32)
    grad_act = jnp.einsum("std,fd->stf", cotangent, back_down, preferred_element_type=jnp.float32)
    grad_hidden = (grad_act * gelu_slope(hidden)).astype(jnp.bfloat16)
    grad_up = jnp.einsum("std,stf->df", second_low, grad_hidden, preferred_element_type=jnp.float32)
    grad_second = lax.psum(
        jnp.einsum("stf,df->std", grad_hidden, back_up, preferred_element_type=jnp.float32), "tp"
    )
    grad_mid_norm, gain_two, scaling_two, offset_two = norm_back(
        grad_second, normed_two, inverse_two, gains_f[1], modulation[:, 2]
    )
    grad_middle = cotangent.astype(jnp.float32) + grad_mid_norm
    grad_branch = grad_middle.astype(jnp.bfloat16)
    grad_out = jnp.einsum(
        "ste,std->ed", attended_low, grad_branch, preferred_element_type=jnp.float32
    )
    grad_attended = jnp.einsum(
        "std,ed->ste", grad_branch, back_out, preferred_element_type=jnp.float32
    ).astype(jnp.bfloat16)
    grad_query_g, grad_key_g, grad_value_g = lax.map(
        partial(attend_back, scaling=scaling),
        (
            query_groups,
            group_heads(keys_back, per_group),
            group_heads(values_back, per_group),
            group_heads(grad_attended, per_group),
            log_total,
        ),
    )
    grad_key_all = ungroup_heads(grad_key_g, seq_count)
    grad_value_all = ungroup_heads(grad_value_g, seq_count)
    grad_key, grad_value = (
        lax.psum_scatter(grad_key_all, "ctx", scatter_dimension=1, tiled=True),
        lax.psum_scatter(grad_value_all, "ctx", scatter_dimension=1, tiled=True),
    )
    grad_query = ungroup_heads(grad_query_g, seq_count)
    query_back = unrotate(grad_query.reshape(head_shape), cosines, sines).reshape(
        seq_count, tokens, local_width
    )
    key_back = unrotate(grad_key.reshape(head_shape), cosines, sines).reshape(
        seq_count, tokens, local_width
    )
    grad_projected = jnp.stack([query_back, key_back, grad_value], axis=0).astype(jnp.bfloat16)
    grad_qkv = jnp.einsum(
        "std,cste->cde", first_low, grad_projected, preferred_element_type=jnp.float32
    )
    grad_first = lax.psum(
        jnp.einsum("cste,cde->std", grad_projected, back_qkv, preferred_element_type=jnp.float32),
        "tp",
    )
    grad_in_norm, gain_one, scaling_one, offset_one = norm_back(
        grad_first, normed_one, inverse_one, gains_f[0], modulation[:, 0]
    )
    input_grad = (grad_middle + grad_in_norm).astype(jnp.bfloat16)
    grad_modulation = jnp.stack([scaling_one, offset_one, scaling_two, offset_two], axis=1)
    grad_time = jnp.einsum("sk,scd->kcd", embedding, grad_modulation, precision=highest)
    grad_gains = jnp.stack([gain_one, gain_two], axis=0)
    shares = (
        lax.psum_scatter(grad_qkv, "shard", scatter_dimension=1, tiled=True),
        lax.psum_scatter(grad_out, "shard", scatter_dimension=1, tiled=True),
        lax.psum_scatter(grad_up, "shard", scatter_dimension=0, tiled=True),
        lax.psum_scatter(grad_down, "shard", scatter_dimension=1, tiled=True),
        lax.psum_scatter(grad_time, "shard", scatter_dimension=2, tiled=True),
        lax.psum_scatter(grad_gains, "shard", scatter_dimension=1, tiled=True),
    )
    shares = lax.psum((shares[0], shares[1], shares[2], shares[3], shares[4], shares[5]), "ctx")
    return (output, input_grad, shares[0], shares[1], shares[2], shares[3], shares[4], shares[5])


BF = jnp.bfloat16
F32 = jnp.float32
NN = (((1,), (0,)), ((), ()))
NT = (((1,), (1,)), ((), ()))
TN = (((0,), (0,)), ((), ()))
VMEM_BIG = 56 << 20
PER_US = 0.8e9


def mm(a, b, dims=NN):
    return lax.dot_general(a, b, dims, preferred_element_type=F32)


def cost(flops, nbytes=0, trans=0):
    return pl.CostEstimate(flops=int(flops), bytes_accessed=int(nbytes), transcendentals=int(trans))


def whole(array):
    zeros = (0,) * array.ndim
    return pl.BlockSpec(array.shape, lambda *_: zeros)


def call(kernel, name, grid, scalars, ins, in_specs, outs, out_specs, est, scratch=()):
    return pl.pallas_call(
        kernel,
        out_shape=outs,
        grid_spec=pltpu.PrefetchScalarGridSpec(
            num_scalar_prefetch=len(scalars),
            grid=grid,
            in_specs=in_specs,
            out_specs=out_specs,
            scratch_shapes=list(scratch),
        ),
        compiler_params=pltpu.CompilerParams(vmem_limit_bytes=VMEM_BIG),
        cost_estimate=est,
        name=name,
    )(*scalars, *ins)


def shape(dims, dtype):
    return jax.ShapeDtypeStruct(dims, dtype)


def cols(index, width):
    return pl.ds(pl.multiple_of(index * width, width), width)


def half_turn(values):
    lane = lax.broadcasted_iota(jnp.int32, values.shape, 1) % HEAD_DIM
    width = values.shape[1]
    up = pltpu.roll(values, HEAD_DIM // 2, 1)
    down = pltpu.roll(values, width - HEAD_DIM // 2, 1)
    return jnp.where(lane < HEAD_DIM // 2, down, up)


def spin(cos_ref, sin_ref, width):
    cosines, sines = cos_ref[...].T, sin_ref[...].T
    heads = width // HEAD_DIM
    return jnp.concatenate([cosines, cosines] * heads, axis=1), jnp.concatenate([-sines, sines] * heads, axis=1)


def pick(step, first_ref, second_ref, per_half):
    return jnp.where(step < per_half, first_ref[...], second_ref[...])


def own_map(per_half):
    return lambda i, *_: (jnp.minimum(i, per_half - 1), 0)


def other_map(per_half):
    return lambda i, *_: (jnp.maximum(i - per_half, 0), 0)


def project_kernel(per_half, blk, xa, xb, w0, w1, w2, w3, mods, cosb, sinb, h_ref, q_ref, k_ref, kt_ref, v_ref, vt_ref):
    x = pick(pl.program_id(0), xa, xb, per_half).astype(F32)
    x = x - jnp.mean(x, axis=1, keepdims=True)
    var = jnp.mean(x * x, axis=1, keepdims=True)
    n = x * lax.rsqrt(var + norm_epsilon)
    h_ref[...] = (n * mods[0:1, :] + mods[1:2, :]).astype(BF)
    rows = w0.shape[0]
    acc = None
    for j, w in enumerate((w0, w1, w2, w3)):
        part = mm(h_ref[:, cols(blk[j], rows)], w[...])
        acc = part if acc is None else acc + part
    wide = acc.shape[1] // 3
    cosines, sines = spin(cosb, sinb, wide)
    q = acc[:, :wide]
    k = acc[:, wide : 2 * wide]
    v = acc[:, 2 * wide :]
    q = q * cosines + half_turn(q) * sines
    k = k * cosines + half_turn(k) * sines
    q_ref[...] = q.astype(BF)
    k_ref[...] = k.astype(BF)
    kt_ref[...] = k.T.astype(BF)
    v_ref[...] = v.astype(BF)
    vt_ref[...] = v.T.astype(BF)


def project(blk, xa, xb, ws, mods, cosb, sinb, tile=256):
    half, width = xa.shape
    total = 2 * half
    wide = ws[0].shape[1] // 3
    per_half = half // tile
    row = lambda w: pl.BlockSpec((tile, w), lambda i, *_: (i, 0))
    turned = pl.BlockSpec((wide, tile), lambda i, *_: (0, i))
    return call(
        partial(project_kernel, per_half), "project", (total // tile,), (blk,),
        (xa, xb, *ws, mods, cosb, sinb),
        [pl.BlockSpec((tile, width), own_map(per_half)), pl.BlockSpec((tile, width), other_map(per_half)),
         *[whole(w) for w in ws], whole(mods), *[pl.BlockSpec((v.shape[0], tile), lambda i, *_: (0, i)) for v in (cosb, sinb)]],
        [shape((total, width), BF), shape((total, wide), BF), shape((total, wide), BF), shape((wide, total), BF),
         shape((total, wide), BF), shape((wide, total), BF)],
        [row(width), row(wide), row(wide), turned, row(wide), turned],
        cost(12.5 * PER_US),
    )


def attend_kernel(scale, q_ref, k_ref, vt_ref, o_ref, ot_ref, lse_ref):
    rows, wide = q_ref.shape
    q = q_ref[...]
    lane = lax.broadcasted_iota(jnp.int32, (rows, wide), 1) // HEAD_DIM
    def head(h, _):
        at = pl.ds(pl.multiple_of(h * HEAD_DIM, HEAD_DIM), HEAD_DIM)
        qh = jnp.where(lane == h, q, jnp.zeros_like(q))
        s = mm(k_ref[...], qh, NT) * scale
        top = jnp.max(s, axis=0, keepdims=True)
        p = jnp.exp(s - top)
        total = jnp.sum(p, axis=0, keepdims=True)
        ot_ref[at, :] = mm(vt_ref[at, :], p.astype(BF)) / total
        lse_ref[pl.ds(h, 1), :] = top + jnp.log(total)
        return 0

    lax.fori_loop(0, wide // HEAD_DIM, head, 0)
    o_ref[...] = ot_ref[...].T.astype(BF)


def attend(q, k, vt, first, rows, tile=1024):
    total, wide = q.shape
    heads = wide // HEAD_DIM
    skip = first // tile
    return call(
        partial(attend_kernel, HEAD_DIM**-0.5), "attend", (rows // tile,), (), (q, k, vt),
        [pl.BlockSpec((tile, wide), lambda i: (i + skip, 0)), whole(k), whole(vt)],
        [shape((rows, wide), BF), shape((wide, rows), F32), shape((heads, rows), F32)],
        [pl.BlockSpec((tile, wide), lambda i: (i, 0)), pl.BlockSpec((wide, tile), lambda i: (0, i)),
         pl.BlockSpec((heads, tile), lambda i: (0, i))],
        cost(10.0 * PER_US),
    )


def join_kernel(n_t, blk, blo, x_ref, *refs):
    near, far = refs[:n_t], refs[n_t : 2 * n_t]
    mine = refs[2 * n_t : 6 * n_t]
    theirs, mods, x1_ref, h_ref = refs[6 * n_t :]
    own = jnp.concatenate([o[...] for o in near], axis=1)
    oth = jnp.concatenate([o[...] for o in far], axis=1)
    span = theirs.shape[1]
    deep = own.shape[1]
    for k in range(4):
        at = cols(blk[k], span)
        w = jnp.concatenate([mine[4 * j + k][...] for j in range(n_t)], axis=0)
        x1_ref[:, at] = x_ref[:, at].astype(F32) + mm(own, w)
    for k in range(4):
        at = cols(blo[k], span)
        x1_ref[:, at] += mm(oth, theirs[k * deep : (k + 1) * deep, :])
    x = x1_ref[...]
    x = x - jnp.mean(x, axis=1, keepdims=True)
    var = jnp.mean(x * x, axis=1, keepdims=True)
    n = x * lax.rsqrt(var + norm_epsilon)
    h_ref[...] = (n * mods[2:3, :] + mods[3:4, :]).astype(BF)


def part_of(array, index, rows):
    return pl.BlockSpec((rows, array.shape[1]), lambda *_: (index, 0))


def stack_kernel(*refs):
    rows = refs[0].shape[0]
    for i, ref in enumerate(refs[:-1]):
        refs[-1][i * rows : (i + 1) * rows, :] = ref[...]


def stack_parts(arrays, rows):
    width = arrays[0].shape[1]
    return call(
        stack_kernel, "stack_parts", (1,), (), arrays,
        [part_of(v, v.shape[0] // rows - 1, rows) for v in arrays],
        shape((len(arrays) * rows, width), BF), pl.BlockSpec((len(arrays) * rows, width), lambda i: (0, 0)),
        cost(2.3 * PER_US),
    )


def join(blk, blo, x, near, far, slots, theirs, mods, tile=256):
    half, width = x.shape
    n_t = len(slots)
    wide = near[0].shape[1]
    row = lambda w: pl.BlockSpec((tile, w), lambda i, *_: (i, 0))
    flat = [w for slot in slots for w in slot]
    last_part = flat[0].shape[0] // wide - 1
    return call(
        partial(join_kernel, n_t), "join", (half // tile,), (blk, blo), (x, *near, *far, *flat, theirs, mods),
        [row(width), *[row(wide)] * (2 * n_t), *[part_of(w, last_part, wide) for w in flat], whole(theirs), whole(mods)],
        [shape((half, width), F32), shape((half, width), BF)],
        [row(width), row(width)],
        cost(8.5 * PER_US),
    )


def gelu_parts(u):
    half = 0.5 * (1.0 + lax.erf(u * 0.7071067811865476))
    slope = half + u * jnp.exp(-0.5 * u * u) * 0.3989422804014327
    return u * half, slope


def unpack_kernel(blk, *refs):
    ws, (up_ref, down_ref) = refs[:4], refs[-2:]
    span = ws[0].shape[1]
    for j, w in enumerate(ws):
        rows = pl.ds(pl.multiple_of(blk[j] * span, span), span)
        for b in range(2):
            up_ref[rows, b * span : (b + 1) * span] = w[b * span : (b + 1) * span, :]
        down_ref[:, cols(blk[j], span)] = w[2 * span : 4 * span, :]


def unpack(blk, slot, index, n_slots, before):
    span = slot[0].shape[1]
    width, hidden = 4 * span, 2 * span
    any_space = pl.BlockSpec(memory_space=pl.ANY)
    kept = () if before is None else before
    return pl.pallas_call(
        unpack_kernel,
        out_shape=[shape((n_slots * width, hidden), BF), shape((n_slots * hidden, width), BF)],
        grid_spec=pltpu.PrefetchScalarGridSpec(
            num_scalar_prefetch=1,
            grid=(1,),
            in_specs=[part_of(w, 0, width) for w in slot] + [any_space] * len(kept),
            out_specs=[pl.BlockSpec((width, hidden), lambda *_: (index, 0)), pl.BlockSpec((hidden, width), lambda *_: (index, 0))],
        ),
        input_output_aliases={5: 0, 6: 1} if kept else {},
        compiler_params=pltpu.CompilerParams(vmem_limit_bytes=VMEM_BIG),
        cost_estimate=cost(2.5 * PER_US),
        name="unpack",
    )(blk, *slot, *kept)


def mlp_kernel(per_half, n_slots, ha, hb, ca, cb, wu, wd, own_ref, oth_ref, g_ref, du_ref, h_buf, c_buf, du_buf):
    step = pl.program_id(0)
    width = ha.shape[1]
    hidden = wu.shape[1]
    h_buf[...] = pick(step, ha, hb, per_half)
    c_buf[...] = pick(step, ca, cb, per_half)

    def one(i, _):
        at = cols(i, hidden)
        u = mm(h_buf[...], wu[pl.ds(pl.multiple_of(i * width, width), width), :])
        dg = mm(c_buf[...], wd[pl.ds(pl.multiple_of(i * hidden, hidden), hidden), :], NT)
        g, slope = gelu_parts(u)
        g_ref[:, at] = g.astype(BF)
        du_buf[:, at] = (dg * slope).astype(BF)
        return 0

    lax.fori_loop(0, n_slots, one, 0)
    du_ref[...] = du_buf[:, :hidden]
    chunk = min(512, width)
    for n in range(width // chunk):
        at = slice(n * chunk, (n + 1) * chunk)
        acc = None
        for i in range(n_slots):
            part = mm(du_buf[:, i * hidden : (i + 1) * hidden], wu[i * width + n * chunk : i * width + (n + 1) * chunk, :], NT)
            acc = part if acc is None else acc + part

        @pl.when(step < per_half)
        def _():
            own_ref[:, at] = acc

        @pl.when(step >= per_half)
        def _():
            oth_ref[:, at] = acc.astype(BF)


def mlp(ha, hb, ca, cb, wu, wd, tile=512):
    half, width = ha.shape
    total = 2 * half
    per_half = half // tile
    hidden = wu.shape[1]
    n_slots = wu.shape[0] // width
    row = lambda w: pl.BlockSpec((tile, w), lambda i, *_: (i, 0))
    mine = pl.BlockSpec((tile, width), own_map(per_half))
    theirs = pl.BlockSpec((tile, width), other_map(per_half))
    return call(
        partial(mlp_kernel, per_half, n_slots), "mlp", (total // tile,), (), (ha, hb, ca, cb, wu, wd),
        [mine, theirs, mine, theirs, whole(wu), whole(wd)],
        [shape((half, width), F32), shape((half, width), BF), shape((total, n_slots * hidden), BF), shape((total, hidden), BF)],
        [mine, theirs, row(n_slots * hidden), row(hidden)],
        cost(42.0 * PER_US),
        [pltpu.VMEM((tile, width), BF), pltpu.VMEM((tile, width), BF), pltpu.VMEM((tile, n_slots * hidden), BF)],
    )


def lift_kernel(per_half, g_in, wd, own_ref, oth_ref):
    step = pl.program_id(0)
    chunk = 512
    for n in range(wd.shape[1] // chunk):
        at = slice(n * chunk, (n + 1) * chunk)
        part = mm(g_in[...], wd[:, at])

        @pl.when(step < per_half)
        def _():
            own_ref[:, at] = part

        @pl.when(step >= per_half)
        def _():
            oth_ref[:, at] = part.astype(BF)


def lift(g, wd, tile=512):
    total = g.shape[0]
    width = wd.shape[1]
    half = total // 2
    per_half = half // tile
    return call(
        partial(lift_kernel, per_half), "lift", (total // tile,), (), (g, wd),
        [pl.BlockSpec((tile, g.shape[1]), lambda i, *_: (i, 0)), whole(wd)],
        [shape((half, width), F32), shape((half, width), BF)],
        [pl.BlockSpec((tile, width), own_map(per_half)), pl.BlockSpec((tile, width), other_map(per_half))],
        cost(14.0 * PER_US),
    )


def norm_turn(dh, x, factor):
    x = x - jnp.mean(x, axis=1, keepdims=True)
    var = jnp.mean(x * x, axis=1, keepdims=True)
    r = lax.rsqrt(var + norm_epsilon)
    n = x * r
    dn = dh * factor
    dx = r * (dn - jnp.mean(dn, axis=1, keepdims=True) - n * jnp.mean(dn * n, axis=1, keepdims=True))
    return dx, jnp.sum(dh * n, axis=0, keepdims=True), jnp.sum(dh, axis=0, keepdims=True)


def turn_kernel(blk, blo, dh_ref, in_ref, x_ref, c_ref, mods, a0, a1, a2, a3, b_ref, dx_ref, da_ref, own_ref, oth_ref, sums):
    dh = dh_ref[...] + in_ref[...].astype(F32)
    dx, s1, s0 = norm_turn(dh, x_ref[...], mods[2:3, :])
    dx = dx + c_ref[...].astype(F32)
    dx_ref[...] = dx
    da_ref[...] = dx.astype(BF)
    wide = own_ref.shape[1]
    span = a0.shape[1]
    step = b_ref.shape[0] // 4
    theirs = [b_ref[k * step : k * step + wide, :] for k in range(4)]
    for order, ws, out in ((blk, [a[...] for a in (a0, a1, a2, a3)], own_ref), (blo, theirs, oth_ref)):
        acc = None
        for j, w in enumerate(ws):
            part = mm(da_ref[:, cols(order[j], span)], w, NT)
            acc = part if acc is None else acc + part
        out[...] = acc.astype(BF)

    @pl.when(pl.program_id(0) == 0)
    def _():
        sums[...] = jnp.zeros_like(sums)

    sums[0:1, :] += s1
    sums[1:2, :] += s0


def turn(blk, blo, dh, received, x1, cot, mods, wa, wb, wide, tile=256):
    half, width = x1.shape
    row = lambda w: pl.BlockSpec((tile, w), lambda i, *_: (i, 0))
    return call(
        turn_kernel, "turn", (half // tile,), (blk, blo), (dh, received, x1, cot, mods, *wa, wb),
        [row(width)] * 4 + [whole(mods), *[part_of(w, w.shape[0] // wide - 1, wide) for w in wa], whole(wb)],
        [shape((half, width), F32), shape((half, width), BF), shape((half, wide), BF), shape((half, wide), BF), shape((8, width), F32)],
        [row(width), row(width), row(wide), row(wide), pl.BlockSpec((8, width), lambda i, *_: (0, 0))],
        cost(11.3 * PER_US),
    )


def attend_back_kernel(scale, tk, per_half, q_ref, da_ref, db_ref, ota_ref, otb_ref, la_ref, lb_ref, cos_ref, sin_ref, k_ref, v_ref, kt_ref, cosb, sinb, out_ref, dqt, dk_acc, dv_acc):
    rows, wide = q_ref.shape
    total = k_ref.shape[0]
    step = pl.program_id(0)
    q = q_ref[...]
    do = pick(step, da_ref, db_ref, per_half)
    lse = pick(step, la_ref, lb_ref, per_half)
    lane = lax.broadcasted_iota(jnp.int32, (rows, wide), 1) // HEAD_DIM
    heads = wide // HEAD_DIM
    qs = [jnp.where(lane == h, q, jnp.zeros_like(q)) for h in range(heads)]
    ds = [jnp.where(lane == h, do, jnp.zeros_like(do)) for h in range(heads)]
    od = do.astype(F32).T * pick(step, ota_ref, otb_ref, per_half)
    deltas = [jnp.sum(od[h * HEAD_DIM : (h + 1) * HEAD_DIM, :], axis=0, keepdims=True) for h in range(heads)]

    @pl.when(step == 0)
    def _():
        dk_acc[...] = jnp.zeros_like(dk_acc)
        dv_acc[...] = jnp.zeros_like(dv_acc)

    dqt[...] = jnp.zeros_like(dqt)
    for j in range(total // tk):
        at = slice(j * tk, (j + 1) * tk)
        kj, vj = k_ref[at, :], v_ref[at, :]
        for h in range(heads):
            hs = slice(h * HEAD_DIM, (h + 1) * HEAD_DIM)
            s = mm(kj, qs[h], NT) * scale
            p = jnp.exp(s - lse[h : h + 1, :])
            dp = mm(vj, ds[h], NT)
            dsc = (p * (dp - deltas[h])).astype(BF)
            dv_acc[at, :] += mm(p.astype(BF), ds[h])
            dk_acc[at, :] += mm(dsc, qs[h])
            dqt[hs, :] += mm(kt_ref[hs, at], dsc)
    dq = dqt[...].T * scale
    cosines, sines = spin(cos_ref, sin_ref, wide)
    out_ref[pl.ds(pl.multiple_of(step * rows, rows), rows), :wide] = (dq * cosines - half_turn(dq) * sines).astype(BF)

    @pl.when(step == pl.num_programs(0) - 1)
    def _():
        dk = dk_acc[...] * scale
        cosines, sines = spin(cosb, sinb, wide)
        out_ref[:, wide : 2 * wide] = (dk * cosines - half_turn(dk) * sines).astype(BF)
        out_ref[:, 2 * wide :] = dv_acc[...].astype(BF)


def attend_back_call(q, do_a, do_b, ots, lses, k, v, kt, cosb, sinb, tile=512, tk=512):
    total, wide = q.shape
    heads = wide // HEAD_DIM
    per_half = total // 2 // tile
    row = pl.BlockSpec((tile, wide), lambda i: (i, 0))
    lanes_a = lambda h: pl.BlockSpec((h, tile), lambda i: (0, jnp.minimum(i, per_half - 1)))
    lanes_b = lambda h: pl.BlockSpec((h, tile), lambda i: (0, jnp.maximum(i - per_half, 0)))
    full = pl.BlockSpec((total, wide), lambda i: (0, 0))
    turned = pl.BlockSpec((cosb.shape[0], tile), lambda i: (0, i))
    return call(
        partial(attend_back_kernel, HEAD_DIM**-0.5, tk, per_half), "attend_back", (total // tile,), (),
        (q, do_a, do_b, *ots, *lses, cosb, sinb, k, v, kt, cosb, sinb),
        [row, pl.BlockSpec((tile, wide), own_map(per_half)), pl.BlockSpec((tile, wide), other_map(per_half)),
         lanes_a(wide), lanes_b(wide), lanes_a(heads), lanes_b(heads), turned, turned, full, full, whole(kt), whole(cosb), whole(sinb)],
        shape((total, 3 * wide), BF),
        pl.BlockSpec((total, 3 * wide), lambda i: (0, 0)),
        cost(29.0 * PER_US),
        [pltpu.VMEM((wide, tile), F32), pltpu.VMEM((total, wide), F32), pltpu.VMEM((total, wide), F32)],
    )


def gather_kernel(n, blk, *refs):
    rs = refs[:n]
    ws = [refs[n + 4 * i : n + 4 * i + 4] for i in range(n)]
    own_ref, oth_ref = refs[5 * n :]
    rows = own_ref.shape[0]
    span = ws[0][0].shape[0]
    for j in range(4):
        acc = None
        for r, w in zip(rs, ws):
            part = mm(r[...], w[j][...], NT)
            acc = part if acc is None else acc + part
        own_ref[:, cols(blk[j], span)] = acc[:rows]
        oth_ref[:, cols(blk[j], span)] = acc[rows:].astype(BF)


def gather(blk, rs, first, others, width):
    n = len(rs)
    rows, span = rs[0].shape[0] // 2, first[0].shape[0]
    back = pl.BlockSpec((rows, width), lambda i, *_: (0, 0))
    return call(
        partial(gather_kernel, n), "gather", (1,), (blk,), (*rs, *first, *(others * (n - 1))),
        [*[whole(r) for r in rs], *[whole(w) for w in first], *[part_of(w, i, span) for i in range(n - 1) for w in others]],
        [shape((rows, width), F32), shape((rows, width), BF)],
        [back, back],
        cost(6.5 * PER_US),
    )


def last_kernel(at, dh_ref, in_ref, x_ref, dx_ref, mods, out_ref, sums):
    dx, s1, s0 = norm_turn(dh_ref[...] + in_ref[...].astype(F32), x_ref[...].astype(F32), mods[0:1, :])
    out_ref[...] = (dx + dx_ref[...]).astype(BF)
    sums[...] = jnp.zeros_like(sums)
    sums[0:1, :] = s1
    sums[1:2, :] = s0


def last(at, dh, received, x, dx, mods):
    rows, width = dh.shape
    block = pl.BlockSpec((rows, width), lambda i, at: (at[0], 0))
    return call(
        last_kernel, "last", (1,), (at,), (dh, received, x, dx, mods),
        [whole(dh), whole(received), block, block, whole(mods)],
        [shape((rows, width), BF), shape((8, width), F32)],
        [pl.BlockSpec((rows, width), lambda i, *_: (0, 0)), pl.BlockSpec((8, width), lambda i, *_: (0, 0))],
        cost(3.5 * PER_US),
    )


def after(values, *events):
    return lax.optimization_barrier((values, events))[0]


def fast_body(
    activations, timestep, positions, qkv_weight, out_weight, up_weight, down_weight, time_weight, norm_gains, cotangent
):
    n_s, n_t = lax.axis_size("shard"), lax.axis_size("tp")
    s, c, t = lax.axis_index("shard"), lax.axis_index("ctx"), lax.axis_index("tp")
    x_own = activations[0]
    cot_own = cotangent[0]
    half, width = x_own.shape
    span = width // n_s
    quarter = half // n_t
    near = jnp.where(c == 0, 1, 2)
    blk = jnp.stack([s, s ^ near, s ^ (3 - near), s ^ 3]).astype(jnp.int32)
    blo = jnp.stack([s, s ^ (3 - near), s ^ near, s ^ 3]).astype(jnp.int32)
    pairs_a = [(v * 2 + k, (v ^ (1 + k)) * 2 + k) for v in range(n_s) for k in range(2)]
    pairs_b = [(v * 2 + k, (v ^ (2 - k)) * 2 + k) for v in range(n_s) for k in range(2)]
    cycle = [(i, (i + 1) % n_t) for i in range(n_t)]
    swap = lambda v: lax.ppermute(v, "ctx", [(0, 1), (1, 0)])
    move_a = lambda v: lax.ppermute(v, ("shard", "ctx"), pairs_a)
    move_b = lambda v: lax.ppermute(v, ("shard", "ctx"), pairs_b)
    upward = lambda v: lax.ppermute(v, "tp", cycle)

    def by_z(v, d):
        return lax.ppermute(v, "tp", [(i, (i + d) % n_t) for i in range(n_t)])

    def turn_shard(v, d):
        return lax.ppermute(v, "shard", [(i, (i + d) % n_s) for i in range(n_s)])

    def half_of(v, axis):
        size = v.shape[axis] // 2
        return lax.dynamic_slice_in_dim(v, c * size, size, axis)

    def both(v, axis):
        other = swap(v)
        return jnp.where(c == 0, jnp.concatenate([v, other], axis), jnp.concatenate([other, v], axis))

    x_oth = swap(x_own)

    def shard_pair(v, bit):
        return lax.ppermute(v, "shard", [(i, i ^ bit) for i in range(n_s)])

    gains = norm_gains.astype(F32)
    small = jnp.concatenate([gains, jnp.broadcast_to(timestep.astype(F32)[:, None], (1, span))], axis=0)
    small_two = jnp.concatenate([small, shard_pair(small, 1)], axis=0)
    small_four = jnp.concatenate([small_two, shard_pair(small_two, 2)], axis=0)
    smalls = [small_four[3 * i : 3 * i + 3] for i in range(n_s)]

    wide = qkv_weight.shape[2] // 2
    qkv_half = half_of(qkv_weight, 2)
    qkv_share = jnp.concatenate([qkv_half[0], qkv_half[1], qkv_half[2]], axis=1)
    qkv_a, qkv_b = move_a(qkv_share), move_b(qkv_share)
    qkv_c = move_b(qkv_a)
    w_qkv = [qkv_share, qkv_a, qkv_b, qkv_c]
    pos_own = positions.astype(F32)
    pos_oth = swap(pos_own)

    up_half = half_of(up_weight, 1)
    down_half = half_of(down_weight, 0)
    pack = jnp.concatenate([up_half[:, :span], up_half[:, span:], down_half, half_of(out_weight, 0)], axis=0)
    z1 = upward(pack)
    pack_go = after(pack, qkv_a, qkv_b)
    m0a, m0b = move_a(pack_go), move_b(pack_go)

    steps = small_four[2::3, 0]
    embedding = embed_time(steps)
    parts = jnp.einsum("sk,kcd->scd", embedding, time_weight.astype(F32), precision=highest)
    parts_x = shard_pair(jnp.concatenate([parts[1], parts[3]], axis=0), 1)
    parts_y = shard_pair(after(jnp.concatenate([parts[2], parts_x[4:]], axis=0), qkv_c), 2)
    parts_in = [parts[0], parts_x[:4], parts_y[:4], parts_y[4:]]
    gain_full = jnp.zeros((2, width), F32)
    mod_full = jnp.zeros((4, width), F32)
    for i in range(n_s):
        gain_full = lax.dynamic_update_slice_in_dim(gain_full, smalls[i][:2], (s ^ i) * span, 1)
        mod_full = lax.dynamic_update_slice_in_dim(mod_full, parts_in[i], (s ^ i) * span, 1)
    factor_one = gain_full[0] * (1.0 + mod_full[0])
    factor_two = gain_full[1] * (1.0 + mod_full[2])
    zero = jnp.zeros_like(factor_one)
    mods = jnp.stack([factor_one, mod_full[1], factor_two, mod_full[3], zero, zero, zero, zero])

    half_width = HEAD_DIM // 2
    frequency = jnp.exp(-math.log(10000.0) * jnp.arange(half_width, dtype=F32) / half_width)
    angles = frequency[:, None] * jnp.concatenate([pos_own, pos_oth], axis=1)
    cosb, sinb = jnp.cos(angles), jnp.sin(angles)

    z1 = after(z1, parts_y)
    z2 = upward(z1)
    m1a, m1b = move_a(z1), move_b(z1)
    x_now = after(x_own, z1)
    h1, q, k, kt, v, vt = project(blk, x_now, x_oth, w_qkv, mods, cosb, sinb)
    m0a_late, m1a_late, z2_late = after((m0a, m1a, z2), q, m0b)
    m0c, m1c, z3 = move_b(m0a_late), move_b(m1a_late), upward(z2_late)
    o_far, ot_far, lse_far = attend(q, k, vt, half, half)
    o_got = swap(o_far)
    z2_late = after(z2, o_far, m0c, m1b)
    m2a, m2b = move_a(z2_late), move_b(z2_late)
    far = [after(o_got, z3)]
    far.append(upward(far[0]))
    o_near, ot_near, lse_near = attend(after(q, o_far), k, vt, 0, half)
    wu, wd = unpack(blk, [pack, m0a, m0b, m0c], 0, n_t, None)
    z3_late, m2a_late, far_go, near_go = after((z3, m2a, far[1], o_near), m2b, m1c)
    m3a, m3b, m2c = move_a(z3_late), move_b(z3_late), move_b(m2a_late)
    near = [near_go, upward(near_go)]
    far.append(upward(far_go))
    m3a_late, near_go, far_go, m1c_late = after((m3a, near[1], far[2], m1c), m2c, m3b)
    m3c = move_b(m3a_late)
    near.append(upward(near_go))
    far.append(upward(far_go))
    wu, wd = unpack(blk, [z1, m1a, m1b, m1c_late], 1, n_t, (wu, wd))
    near_go, m3c, far_done = after((near[2], m3c, far[3]), wu)
    near.append(upward(near_go))
    far[3] = far_done
    wu, wd = unpack(blk, [z2, m2a, m2b, after(m2c, m3c)], 2, n_t, (wu, wd))
    wu, wd = unpack(blk, [z3, m3a, m3b, m3c], 3, n_t, (wu, wd))
    cot_oth = swap(cot_own)
    w_mlp = [[pack, m0a, m0b, m0c], [z1, m1a, m1b, m1c], [z2, m2a, m2b, m2c], [z3, m3a, m3b, m3c]]
    out_other = swap(stack_parts([w_mlp[j][i] for i in range(n_s) for j in range(n_t)], wide))

    x1, h2 = join(blk, blo, after(x_own, wu), near, far, w_mlp, out_other, mods)
    h2_oth = swap(h2)
    dh2, dh2_send, g_all, du0 = mlp(h2, h2_oth, cot_own, cot_oth, wu, wd)
    qkv_again = after(qkv_share, h2_oth)
    qz_pack = jnp.concatenate([by_z(qkv_again, d) for d in range(1, n_t)], axis=0)
    dh2_in = swap(after(dh2_send, qz_pack))
    qz_pack = after(qz_pack, dh2_in)
    qza, qzb = move_a(qz_pack), move_b(qz_pack)
    dx1, da, do_own, do_send, sums_two = turn(blk, blo, dh2, dh2_in, x1, cot_own, mods, w_mlp[0], out_other, wide)
    do_got = swap(do_send)
    qza, qzb, do_got = after((qza, qzb, do_got), da)
    qzc = move_b(qza)
    w_back = [qz_pack, qza, qzb, qzc]
    dqkv = attend_back_call(q, do_own, do_got, (ot_near, ot_far), (lse_near, lse_far), k, v, kt, cosb, sinb)

    dqkv = dqkv.reshape(2, half, 3 * wide)

    def tokens_of(d):
        return lax.dynamic_slice_in_dim(dqkv, ((t + d) % n_t) * quarter, quarter, 1).reshape(2 * quarter, 3 * wide)

    got = [tokens_of(0), by_z(tokens_of(1), 1)]

    h2_late, h2o_late, du0_late, g_late = after((h2, h2_oth, du0, g_all), tokens_of(1))
    g_up = mm(jnp.concatenate([h2_late, h2o_late], axis=0), du0_late, TN)
    g_down = mm(g_late[:, : 2 * span], jnp.concatenate([cot_own, cot_oth], axis=0), TN)
    got.append(by_z(after(tokens_of(2), got[1], g_up, g_down), 2))
    g_later = after(g_late, got[1], g_up, g_down)
    y_own, y_send = lift(g_later, wd)
    got.append(by_z(after(tokens_of(3), got[2], y_own), 3))

    def mlp_piece(j):
        ups = lax.dynamic_slice_in_dim(g_up, blk[j] * span, span, 0)
        downs = lax.dynamic_slice_in_dim(g_down, blk[j] * span, span, 1)
        outs = lax.dynamic_slice_in_dim(g_out, blk[j] * span, span, 1)
        return jnp.concatenate([ups[:, :span], ups[:, span:], downs, outs], axis=0)

    def reduce_first(pieces):
        return move_b(jnp.concatenate([pieces(2), pieces(3)], axis=0).astype(BF))

    def reduce_last(pieces, came):
        rows = came.shape[0] // 2
        return pieces(0) + came[:rows].astype(F32) + move_a((pieces(1) + came[rows:].astype(F32)).astype(BF)).astype(F32)

    dh1_own, dh1_send = gather(blk, got, w_qkv, w_back, width)
    dh1_got = swap(dh1_send)

    at = t.astype(jnp.int32).reshape(1)
    grad_mine, sums_one = last(at, dh1_own, dh1_got, x_own, dx1, mods)
    slots = [grad_mine, upward(grad_mine)]
    h1_late, dqkv_late, da_late, g_up, g_down, y_send = after((h1, dqkv, da, g_up, g_down, y_send), grad_mine)
    g_out = mm(o_near, da_late, TN) + swap(mm(o_got, da_late, TN).astype(BF)).astype(F32)
    mlp_came = reduce_first(mlp_piece)
    g_qkv = mm(h1_late, dqkv_late.reshape(2 * half, 3 * wide), TN)
    qkv_piece = lambda j: lax.dynamic_slice_in_dim(g_qkv, blk[j] * span, span, 0)
    y_got = swap(y_send)
    qkv_came = reduce_first(qkv_piece)
    keep = jnp.where(t == 0, 1.0, 0.0)
    tally = jnp.concatenate([sums_one[:2], sums_two[:2] * keep], axis=0)
    tally = tally + swap(tally)
    slots[1], tally, mlp_came, y_got = after((slots[1], tally, mlp_came, y_got), g_qkv)
    qkv_came = after(qkv_came, mlp_came, slots[1])
    slots.append(upward(slots[1]))
    full = tally
    for bit in (1, 2):
        full = full + lax.ppermute(full, "tp", [(i, i ^ bit) for i in range(n_t)])
    rows = mlp_came.shape[0] // 2
    mlp_base = mlp_piece(0) + mlp_came[:rows].astype(F32)
    mlp_last = move_a((mlp_piece(1) + mlp_came[rows:].astype(F32)).astype(BF))
    rows = qkv_came.shape[0] // 2
    qkv_base = qkv_piece(0) + qkv_came[:rows].astype(F32)
    qkv_last = move_a((qkv_piece(1) + qkv_came[rows:].astype(F32)).astype(BF))
    output = (x1 + y_own + y_got.astype(F32)).astype(BF)

    slots[2], mlp_last, full = after((slots[2], mlp_last, full))
    slots.append(upward(slots[2]))
    done = mlp_base + mlp_last.astype(F32)
    grad_up = both(jnp.concatenate([done[:span], done[span : 2 * span]], axis=1), 1)
    grad_down = both(done[2 * span : 4 * span], 0)
    grad_out = both(done[4 * span :], 0)
    done_qkv = qkv_base + qkv_last.astype(F32)
    grad_qkv = both(jnp.stack([done_qkv[:, i * wide : (i + 1) * wide] for i in range(3)]), 2)
    dmods = jnp.stack([full[0] * gain_full[0], full[1], full[2] * gain_full[1], full[3],
                       full[0] * (1.0 + mod_full[0]), full[2] * (1.0 + mod_full[2])])
    blocks = [lax.dynamic_slice_in_dim(dmods, (s ^ i) * span, span, 1) for i in range(n_s)]
    blocks_x = shard_pair(jnp.concatenate([blocks[1], blocks[3]], axis=0), 1)
    blocks_y = shard_pair(jnp.concatenate([blocks[2], blocks_x[6:]], axis=0), 2)
    seqs = jnp.stack([blocks[0], blocks_x[:6], blocks_y[:6], blocks_y[6:]])
    grad_time = jnp.einsum("sk,scd->kcd", embedding, seqs[:, :4], precision=highest)
    grad_gains = jnp.sum(seqs[:, 4:], axis=0)
    slots[3] = after(slots[3], grad_qkv, grad_up, grad_down, grad_out, grad_time, grad_gains)
    input_grad = jnp.zeros((half, width), BF)
    for j in range(n_t):
        input_grad = lax.dynamic_update_slice_in_dim(input_grad, slots[j], ((t - j) % n_t) * quarter, 0)
    return (output[None], input_grad[None], grad_qkv, grad_out, grad_up, grad_down, grad_time, grad_gains)


def solution(mesh):
    sizes = dict(mesh.shape)
    chosen = fast_body if (sizes["shard"], sizes["ctx"], sizes["tp"]) == (4, 2, 4) else body
    placed = (
        P("shard", "ctx", None),
        P("shard"),
        P("shard", "ctx"),
        P(None, "shard", "tp"),
        P("tp", "shard"),
        P("shard", "tp"),
        P("tp", "shard"),
        P(None, None, "shard"),
        P(None, "shard"),
        P("shard", "ctx", None),
    )
    return jax.shard_map(
        chosen,
        mesh=mesh,
        in_specs=placed,
        out_specs=(
            P("shard", "ctx", None),
            P("shard", "ctx", None),
            P(None, "shard", "tp"),
            P("tp", "shard"),
            P("shard", "tp"),
            P("tp", "shard"),
            P(None, None, "shard"),
            P(None, "shard"),
        ),
        check_vma=False,
    )
```
